256 devices in a mesh: ctx: 32 (over y, z), ret: 2 (over core), tp: 4 (over x).
Axes of the slice: x: 4, y: 4, z: 8, core: 2. Of those that a mesh axis runs over, the one named last changes fastest.
Arguments:
- queries: bfloat16 [32768, 2048], P('ctx', 'tp'), may hold values from -256 to 256
- d_attn: bfloat16 [32768, 2048], P('ctx', 'tp'), may hold values from -6 to 6
- pool: bfloat16 [2, 32768, 896], P('ret', 'ctx'), may hold values from -6 to 6
- w_key: bfloat16 [896, 2048], P(None, 'tp'), may hold values from -0.1875 to 0.1875
- w_value: bfloat16 [896, 2048], P(None, 'tp'), may hold values from -0.1875 to 0.1875
- owners: int32 [512, 2], replicated, may hold values from 0 to 31, as said below
- picks: int32 [512, 2], replicated, may hold values from 0 to 1023
- live_counts: int32 [2, 32], replicated, may hold values from 1 to 8
Outputs:
- attn_out: bfloat16 [32768, 2048], P('ctx', 'tp')
- d_queries: bfloat16 [32768, 2048], P('ctx', 'tp')
- d_w_key: bfloat16 [896, 2048], P(None, 'tp')
- d_w_value: bfloat16 [896, 2048], P(None, 'tp')
The draws below stay inside these ranges and needn't reach their ends.
Inputs may be any that keep to these rules, and one draw needn't show every extreme that they name: `owners`: in each column, at most 1 of the 16 spans of one ctx slab name the same owner, and in every slab some owner is named exactly 1 times.
All inputs are finite; a program needn't handle non-finite values.
Results may differ from the reference program's by a relative error of at most 0.0095.
The reference program's roundings to bfloat16 on the way count: a program that leaves them out, or rounds other values in their place, can miss the bound.
Values may be sent and summed in bfloat16 or wider, within the bound.
No kernel may reach another device: no remote copies, remote signals or barrier semaphores. Data moves between devices by JAX's collectives and lax.ppermute only.
A program may use at most 128 MiB of HBM per device.

```python
import math
import jax
import jax.numpy as jnp
from jax import lax

DE = 896
HEADS = 16
HEAD_DIM = 128
SPAN = 64
NBR_LEN = 128
NBRS = 2
CH_DEV = 16
BLK_DEV = 8
HD = 2048
SPANS = 512
TOKENS = 32768
BLOCKS = 256
N_CTX = 32


def draw_queries(key, part):
    base_key = jax.random.fold_in(key, 0)
    raw_values = jnp.clip(jax.random.normal(base_key, (TOKENS, HD), jnp.float32), -4.0, 4.0) * 2.0
    return raw_values.astype(jnp.bfloat16)


def draw_owners(key, part):
    capacity = (CH_DEV + N_CTX - 1) // N_CTX
    places = N_CTX * capacity
    pop_key = jax.random.fold_in(key, 11)
    noise_key = jax.random.fold_in(key, 12)
    order_key = jax.random.fold_in(key, 13)
    favour = jax.random.randint(pop_key, (NBRS, N_CTX), 0, 4)
    favour = jnp.repeat(favour, capacity, axis=1)
    noise = jax.random.randint(noise_key, (N_CTX, NBRS, places), 0, 4096)
    scored = (noise + favour[None, :, :] * 2048) * places + jnp.arange(places, dtype=jnp.int32)[None, None, :]
    unused_vals, picked = lax.top_k(scored, CH_DEV)
    owner_pick = picked // capacity
    shuffle = jax.random.randint(order_key, (N_CTX, NBRS, CH_DEV), 0, 4096) * CH_DEV + jnp.arange(CH_DEV, dtype=jnp.int32)[None, None, :]
    order = jnp.argsort(shuffle, axis=2)
    owner_pick = jnp.take_along_axis(owner_pick, order, axis=2)
    return jnp.transpose(owner_pick, (0, 2, 1)).reshape(SPANS, NBRS).astype(jnp.int32)


def set_ends(array, key, smallest, largest):
    dims = array.shape
    place = [jax.random.randint(jax.random.fold_in(key, axis), (), 0, dims[axis]) for axis in range(len(dims))]
    array = array.at[tuple(place)].set(smallest)
    longest = dims.index(max(dims))
    place[longest] = (place[longest] + 1) % dims[longest]
    return array.at[tuple(place)].set(largest)


def level_of(rng, extent, cuts, low, largest):
    level, own = 1.0, jax.random.fold_in(rng, 6)
    for position, shards_of in cuts:
        heights = jnp.exp(jax.random.uniform(jax.random.fold_in(own, position), (shards_of,), jnp.float32, low / len(cuts), largest / len(cuts)))
        level = level * jnp.repeat(heights, extent[position] // shards_of).reshape([-1 if axis == position else 1 for axis in range(len(extent))])
    return level


def gaussian(rng, extent, deviation, limit, pieces=(), kind=jnp.bfloat16):
    gain = level_of(rng, extent, pieces, -0.22, 0.18) if pieces else 1.0
    entries = jax.random.normal(rng, extent, jnp.float32) * deviation * gain
    return jnp.minimum(jnp.maximum(entries, -limit), limit).astype(kind)


def setup_inputs(seed: int = 0) -> dict:
    key_of = jax.random.split(jax.random.key(seed), 9)
    queries = draw_queries(jax.random.fold_in(key_of[8], 71), 0)
    d_attn = gaussian(key_of[1], (TOKENS, HD), 1.0, 6.0, ((0, 32), (1, 4)))
    pool = gaussian(key_of[2], (NBRS, BLOCKS * NBR_LEN, DE), 1.0, 6.0, ((0, 2), (1, 32)))
    w_key = gaussian(key_of[3], (DE, HD), DE ** -0.5, 0.1875, ((1, 4),))
    w_value = gaussian(key_of[4], (DE, HD), DE ** -0.5, 0.1875, ((1, 4),))
    owners = draw_owners(jax.random.fold_in(key_of[8], 71), 0)
    picks = set_ends(jax.random.randint(key_of[6], (SPANS, NBRS), 0, 1024), jax.random.fold_in(key_of[6], 1), 0, 1023).astype(jnp.int32)
    live_counts = set_ends(jax.random.randint(key_of[7], (NBRS, N_CTX), 1, BLK_DEV + 1), jax.random.fold_in(key_of[7], 1), 1, BLK_DEV).astype(jnp.int32)
    return {"queries": queries, "d_attn": d_attn, "pool": pool, "w_key": w_key, "w_value": w_value, "owners": owners, "picks": picks, "live_counts": live_counts}


def reference(queries, d_attn, pool, w_key, w_value, owners, picks, live_counts):
    score_scale = 1.0 / math.sqrt(HEAD_DIM)
    column_ids = jnp.arange(NBRS, dtype=jnp.int32)[None, :]
    live_of = live_counts[column_ids, owners]
    block_ids = (owners * BLK_DEV + picks % live_of).astype(jnp.int32)
    group_count = SPANS // CH_DEV
    query_groups = queries.reshape(group_count, CH_DEV, SPAN, HEADS, HEAD_DIM)
    grad_groups = d_attn.reshape(group_count, CH_DEV, SPAN, HEADS, HEAD_DIM)
    block_groups = block_ids.reshape(group_count, CH_DEV, NBRS)
    pool_blocks = pool.reshape(NBRS, BLOCKS, NBR_LEN, DE)

    def span_step(carry, item):
        grad_keys, grad_values = carry
        query_tiles, grad_tiles, block_tiles = item
        nbr_rows = pool_blocks[column_ids, block_tiles]
        flat_rows = nbr_rows.reshape(CH_DEV * NBRS * NBR_LEN, DE)
        key_tiles = jnp.dot(flat_rows, w_key, preferred_element_type=jnp.float32).astype(jnp.bfloat16)
        value_tiles = jnp.dot(flat_rows, w_value, preferred_element_type=jnp.float32).astype(jnp.bfloat16)
        key_f = key_tiles.reshape(CH_DEV, NBRS * NBR_LEN, HEADS, HEAD_DIM).astype(jnp.float32)
        value_f = value_tiles.reshape(CH_DEV, NBRS * NBR_LEN, HEADS, HEAD_DIM).astype(jnp.float32)
        query_f = query_tiles.astype(jnp.float32)
        grad_f = grad_tiles.astype(jnp.float32)
        scores = jnp.einsum('cmhd,clhd->chml', query_f, key_f) * score_scale
        attn_prob = jax.nn.softmax(scores, axis=-1)
        prob_bf = attn_prob.astype(jnp.bfloat16)
        attn_full = jnp.einsum('chml,clhd->cmhd', prob_bf.astype(jnp.float32), value_f)
        attn_tile = attn_full.astype(jnp.bfloat16)
        out_dot = jnp.einsum('cmhd,cmhd->chm', grad_f, attn_tile.astype(jnp.float32))
        grad_prob = jnp.einsum('cmhd,clhd->chml', grad_f, value_f)
        dscore = (attn_prob * (grad_prob - out_dot[..., None]) * score_scale).astype(jnp.bfloat16)
        query_grad = jnp.einsum('chml,clhd->cmhd', dscore.astype(jnp.float32), key_f).astype(jnp.bfloat16)
        key_grad = jnp.einsum('chml,cmhd->clhd', dscore.astype(jnp.float32), query_f).astype(jnp.bfloat16).reshape(-1, HD)
        value_grad = jnp.einsum('chml,cmhd->clhd', prob_bf.astype(jnp.float32), grad_f).astype(jnp.bfloat16).reshape(-1, HD)
        grad_keys = grad_keys + jnp.dot(flat_rows.T, key_grad, preferred_element_type=jnp.float32)
        grad_values = grad_values + jnp.dot(flat_rows.T, value_grad, preferred_element_type=jnp.float32)
        return ((grad_keys, grad_values), (attn_tile, query_grad))
    zero_grad = jnp.zeros((DE, HD), jnp.float32)
    (grad_keys, grad_values), (attn_all, query_all) = lax.scan(span_step, (zero_grad, zero_grad), (query_groups, grad_groups, block_groups))
    mean_share = 1.0 / SPANS
    return (attn_all.reshape(TOKENS, HD), query_all.reshape(TOKENS, HD), (grad_keys * mean_share).astype(jnp.bfloat16), (grad_values * mean_share).astype(jnp.bfloat16))
```

```python
import math

import jax
import jax.numpy as jnp
from jax import lax
from jax.experimental import pallas as pl
from jax.experimental.pallas import tpu as pltpu
from jax.sharding import Mesh
from jax.sharding import PartitionSpec as P

HEAD_DIM = 128
SPAN = 64
NBR_LEN = 128
CH_DEV = 16
Y_CHIPS = 4

BF16 = jnp.bfloat16
F32 = jnp.float32
ANY = pl.BlockSpec(memory_space=pl.ANY)
SMEM = pl.BlockSpec(memory_space=pltpu.SMEM)


def pack_kernel(slots, place, pool, out, held, in_sem, out_sem):
    part = held.shape[1]
    start = pl.multiple_of(place[0] * part, part)
    load = pltpu.make_async_copy(pool.at[:, pl.ds(start, part), :], held, in_sem)
    load.start()
    load.wait()
    copies = [
        pltpu.make_async_copy(held.at[slots[d]], out.at[d], out_sem.at[d])
        for d in range(out.shape[0])
    ]
    for copy in copies:
        copy.start()
    for copy in copies:
        copy.wait()


def pack(send_slot, tp_place, pool_blocks, part):
    blocks, _, width = pool_blocks.shape
    count = send_slot.shape[0]
    return pl.pallas_call(
        pack_kernel,
        out_shape=jax.ShapeDtypeStruct((count, part, width), BF16),
        in_specs=[SMEM, SMEM, ANY],
        out_specs=ANY,
        scratch_shapes=[
            pltpu.VMEM((blocks, part, width), BF16),
            pltpu.SemaphoreType.DMA,
            pltpu.SemaphoreType.DMA((count,)),
        ],
        name="pack",
    )(send_slot, tp_place, pool_blocks)


def pick_kernel(wanted, incoming, keep, give, held, in_sem, out_sem):
    count = held.shape[0]
    half = count // 2
    loads = [
        pltpu.make_async_copy(incoming.at[wanted[k]], held.at[k], in_sem.at[k])
        for k in range(count)
    ]
    stores = [
        pltpu.make_async_copy(
            held.at[k],
            keep.at[k] if k < half else give.at[k - half],
            out_sem.at[k],
        )
        for k in range(count)
    ]
    for load in loads:
        load.start()
    for k in range(count):
        loads[k].wait()
        stores[k].start()
    for store in stores:
        store.wait()


def pick(wanted, incoming):
    count = wanted.shape[0]
    half = (count // 2,) + incoming.shape[1:]
    return pl.pallas_call(
        pick_kernel,
        out_shape=(jax.ShapeDtypeStruct(half, BF16), jax.ShapeDtypeStruct(half, BF16)),
        in_specs=[SMEM, ANY],
        out_specs=(ANY, ANY),
        scratch_shapes=[
            pltpu.VMEM((count,) + incoming.shape[1:], BF16),
            pltpu.SemaphoreType.DMA((count,)),
            pltpu.SemaphoreType.DMA((count,)),
        ],
        name="pick",
    )(wanted, incoming)


def dot(a, b, dims=((1,), (0,))):
    return lax.dot_general(a, b, (dims, ((), ())), preferred_element_type=F32)


def attend_kernel(
    place,
    gathered,
    queries,
    d_attn,
    w_key,
    w_value,
    attn_out,
    d_queries,
    weight_part,
    rows,
    q_held,
    g_held,
    k_grad,
    v_grad,
    row_sem,
    q_sem,
):
    parts, cols, spans, part, width = gathered.shape
    heads = w_key.shape[1] // HEAD_DIM
    nbr_rows = cols * parts * part
    tokens = spans * SPAN
    scale = 1.0 / math.sqrt(HEAD_DIM)
    me = place[0]
    first = pl.multiple_of(me * tokens, tokens)
    loads = [
        pltpu.make_async_copy(
            gathered.at[p, c],
            rows.at[:, pl.ds((c * parts + p) * part, part), :],
            row_sem.at[c * parts + p],
        )
        for p in range(parts)
        for c in range(cols)
    ] + [
        pltpu.make_async_copy(queries.at[pl.ds(first, tokens), :], q_held, q_sem.at[0]),
        pltpu.make_async_copy(d_attn.at[pl.ds(first, tokens), :], g_held, q_sem.at[1]),
    ]
    for load in loads:
        load.start()
    for load in loads:
        load.wait()

    def span_step(j, carry):
        span_rows = rows[j]
        at = pl.multiple_of(j * SPAN, SPAN)
        to = pl.multiple_of(j * nbr_rows, nbr_rows)
        keys = dot(span_rows, w_key[...]).astype(BF16)
        values = dot(span_rows, w_value[...]).astype(BF16)
        for h in range(heads):
            cut = slice(h * HEAD_DIM, (h + 1) * HEAD_DIM)
            q = q_held[pl.ds(at, SPAN), cut]
            g = g_held[pl.ds(at, SPAN), cut]
            k = keys[:, cut]
            v = values[:, cut]
            scores = dot(q, k, ((1,), (1,))) * scale
            top = jnp.max(scores, axis=1, keepdims=True)
            raised = jnp.exp(scores - top)
            total = jnp.sum(raised, axis=1, keepdims=True)
            prob = raised / total
            prob_b = prob.astype(BF16)
            out = dot(prob_b, v).astype(BF16)
            out_dot = jnp.sum(g.astype(F32) * out.astype(F32), axis=1, keepdims=True)
            grad_prob = dot(g, v, ((1,), (1,)))
            dscore = (prob * (grad_prob - out_dot) * scale).astype(BF16)
            attn_out[pl.ds(at, SPAN), cut] = out
            d_queries[pl.ds(at, SPAN), cut] = dot(dscore, k).astype(BF16)
            k_grad[pl.ds(to, nbr_rows), cut] = dot(dscore, q, ((0,), (0,))).astype(BF16)
            v_grad[pl.ds(to, nbr_rows), cut] = dot(prob_b, g, ((0,), (0,))).astype(BF16)
        return carry

    lax.fori_loop(0, spans, span_step, 0)
    mean_share = 1.0 / (CH_DEV * 32)
    flat = rows[...].reshape(spans * nbr_rows, width)
    for h in range(heads):
        cut = slice(h * HEAD_DIM, (h + 1) * HEAD_DIM)
        weight_part[me, h] = dot(flat, k_grad[:, cut], ((0,), (0,))) * mean_share
        weight_part[1 - me, h] = dot(flat, v_grad[:, cut], ((0,), (0,))) * mean_share


def attend(ret_place, gathered, queries, d_attn, w_key, w_value):
    parts, cols, spans, part, width = gathered.shape
    head_cols = w_key.shape[1]
    tokens = spans * SPAN
    nbr_rows = cols * parts * part
    whole = pl.BlockSpec(memory_space=pltpu.VMEM)
    flops = 2 * spans * nbr_rows * head_cols * (4 * width + 6 * SPAN)
    return pl.pallas_call(
        attend_kernel,
        out_shape=(
            jax.ShapeDtypeStruct((tokens, head_cols), BF16),
            jax.ShapeDtypeStruct((tokens, head_cols), BF16),
            jax.ShapeDtypeStruct((2, head_cols // HEAD_DIM, width, HEAD_DIM), F32),
        ),
        in_specs=[SMEM, ANY, ANY, ANY, whole, whole],
        out_specs=(whole, whole, whole),
        scratch_shapes=[
            pltpu.VMEM((spans, nbr_rows, width), BF16),
            pltpu.VMEM((tokens, head_cols), BF16),
            pltpu.VMEM((tokens, head_cols), BF16),
            pltpu.VMEM((spans * nbr_rows, head_cols), BF16),
            pltpu.VMEM((spans * nbr_rows, head_cols), BF16),
            pltpu.SemaphoreType.DMA((cols * parts,)),
            pltpu.SemaphoreType.DMA((2,)),
        ],
        compiler_params=pltpu.CompilerParams(vmem_limit_bytes=60 * 1024 * 1024),
        cost_estimate=pl.CostEstimate(
            flops=flops, bytes_accessed=12 << 20, transcendentals=spans * SPAN * nbr_rows * 4
        ),
        name="attend",
    )(ret_place, gathered, queries, d_attn, w_key, w_value)


def swap(x):
    return lax.ppermute(x, "ret", [(0, 1), (1, 0)])


def added(x):
    return jnp.sum(x.astype(F32), axis=0).astype(BF16)


def spread(x, axis):
    copies = jnp.broadcast_to(x[None], (lax.axis_size(axis),) + x.shape)
    return lax.all_to_all(copies, axis, split_axis=0, concat_axis=0, tiled=True)


def body(queries, d_attn, pool, w_key, w_value, owners, picks, live_counts):
    y_count = lax.axis_size("y")
    z_count = lax.axis_size("z")
    tp_count = lax.axis_size("tp")
    ctx_count = y_count * z_count
    ctx_place = lax.axis_index("y") * z_count + lax.axis_index("z")
    ret_place = lax.axis_index("ret")
    tp_place = lax.axis_index("tp")
    head_cols = w_key.shape[1]
    heads = head_cols // HEAD_DIM
    width = pool.shape[2]
    part = NBR_LEN // tp_count
    half = CH_DEV // 2
    owner_col = lax.dynamic_index_in_dim(owners, ret_place, 1, keepdims=False)
    pick_col = lax.dynamic_index_in_dim(picks, ret_place, 1, keepdims=False)
    live = live_counts[ret_place, ctx_place]
    owner_grid = owner_col.reshape(ctx_count, CH_DEV)
    pick_grid = pick_col.reshape(ctx_count, CH_DEV)
    asked = jnp.sum(jnp.where(owner_grid == ctx_place, pick_grid, 0), axis=1)
    send_slot = asked % live
    mine = lax.dynamic_slice(owner_col, (ctx_place * CH_DEV + ret_place * half,), (half,))
    others = lax.dynamic_slice(owner_col, (ctx_place * CH_DEV + (1 - ret_place) * half,), (half,))
    wanted = jnp.concatenate([mine, others])

    pool_blocks = pool[0].reshape(-1, NBR_LEN, width)
    outgoing = pack(send_slot, tp_place.reshape(1), pool_blocks, part)
    incoming = lax.all_to_all(outgoing, ("y", "z"), split_axis=0, concat_axis=0, tiled=True)
    keep, give = pick(wanted, incoming)
    got = swap(give)
    gathered = lax.all_gather(jnp.stack([keep, got]), "tp")
    attn_half, dq_half, weight_part = attend(
        ret_place.reshape(1), gathered, queries, d_attn, w_key, w_value
    )
    pair = (weight_part[0] + swap(weight_part[1])).astype(BF16)
    by_y = added(lax.all_to_all(pair, "y", split_axis=0, concat_axis=0, tiled=False))
    by_y = by_y.reshape(z_count, width // z_count, HEAD_DIM)
    by_z = added(lax.all_to_all(by_y, "z", split_axis=0, concat_axis=0, tiled=False))
    z_full = spread(by_z, "z").reshape(width, HEAD_DIM)
    mine_full = spread(z_full, "y").reshape(heads, width, HEAD_DIM)
    other_full = swap(mine_full)
    low = ret_place == 0
    d_w_key = jnp.where(low, mine_full, other_full)
    d_w_value = jnp.where(low, other_full, mine_full)
    d_w_key = jnp.transpose(d_w_key, (1, 0, 2)).reshape(width, head_cols)
    d_w_value = jnp.transpose(d_w_value, (1, 0, 2)).reshape(width, head_cols)

    def joined(x):
        y = swap(x)
        return jnp.concatenate([jnp.where(low, x, y), jnp.where(low, y, x)], axis=0)

    return (joined(attn_half), joined(dq_half), d_w_key, d_w_value)


def solution(mesh):
    shape = (Y_CHIPS, mesh.shape["ctx"] // Y_CHIPS, mesh.shape["ret"], mesh.shape["tp"])
    fine = Mesh(mesh.devices.reshape(shape), ("y", "z", "ret", "tp"))
    ctx = ("y", "z")
    return jax.shard_map(
        body,
        mesh=fine,
        in_specs=(
            P(ctx, "tp"),
            P(ctx, "tp"),
            P("ret", ctx, None),
            P(None, "tp"),
            P(None, "tp"),
            P(),
            P(),
            P(),
        ),
        out_specs=(P(ctx, "tp"), P(ctx, "tp"), P(None, "tp"), P(None, "tp")),
        check_vma=False,
    )
```

```python
import functools
import math

import jax
import jax.numpy as jnp
from jax import lax
from jax.experimental import pallas as pl
from jax.experimental.pallas import tpu as pltpu
from jax.sharding import Mesh
from jax.sharding import PartitionSpec as P

HEAD_DIM = 128
SPAN = 64
NBR_LEN = 128
CH_DEV = 16
Y_CHIPS = 4


BF16 = jnp.bfloat16
F32 = jnp.float32
ANY = pl.BlockSpec(memory_space=pl.ANY)
SMEM = pl.BlockSpec(memory_space=pltpu.SMEM)


def pack_kernel(slots, place, pool, out, held, in_sem, out_sem):
    part = held.shape[1]
    start = pl.multiple_of(place[0] * part, part)
    load = pltpu.make_async_copy(pool.at[:, pl.ds(start, part), :], held, in_sem)
    load.start()
    load.wait()
    copies = [
        pltpu.make_async_copy(held.at[slots[d]], out.at[d], out_sem.at[d])
        for d in range(out.shape[0])
    ]
    for copy in copies:
        copy.start()
    for copy in copies:
        copy.wait()


def pack(send_slot, tp_place, pool_blocks, part):
    blocks, _, width = pool_blocks.shape
    count = send_slot.shape[0]
    return pl.pallas_call(
        pack_kernel,
        out_shape=jax.ShapeDtypeStruct((count, part, width), BF16),
        in_specs=[SMEM, SMEM, ANY],
        out_specs=ANY,
        scratch_shapes=[
            pltpu.VMEM((blocks, part, width), BF16),
            pltpu.SemaphoreType.DMA,
            pltpu.SemaphoreType.DMA((count,)),
        ],
        compiler_params=pltpu.CompilerParams(vmem_limit_bytes=60 << 20),
        name="pack",
    )(send_slot, tp_place, pool_blocks)


def pick_kernel(wanted, incoming, *rest):
    outs, (held, in_sem, out_sem) = rest[:-3], rest[-3:]
    count = held.shape[0]
    each = count // len(outs)
    loads = [
        pltpu.make_async_copy(incoming.at[wanted[k]], held.at[k], in_sem.at[k])
        for k in range(count)
    ]
    stores = [
        pltpu.make_async_copy(held.at[k], outs[k // each].at[k % each], out_sem.at[k])
        for k in range(count)
    ]
    for load in loads:
        load.start()
    for k in range(count):
        loads[k].wait()
        stores[k].start()
    for store in stores:
        store.wait()


def pick(wanted, incoming, groups):
    count = wanted.shape[0]
    piece = jax.ShapeDtypeStruct((count // groups,) + incoming.shape[1:], BF16)
    return pl.pallas_call(
        pick_kernel,
        out_shape=(piece,) * groups,
        in_specs=[SMEM, ANY],
        out_specs=(ANY,) * groups,
        scratch_shapes=[
            pltpu.VMEM((count,) + incoming.shape[1:], BF16),
            pltpu.SemaphoreType.DMA((count,)),
            pltpu.SemaphoreType.DMA((count,)),
        ],
        compiler_params=pltpu.CompilerParams(vmem_limit_bytes=4 << 20),
        name="pick",
    )(wanted, incoming)


def dot(a, b, dims=((1,), (0,))):
    return lax.dot_general(a, b, (dims, ((), ())), preferred_element_type=F32)


ROWS = ((1,), (1,))
DOWN = ((0,), (0,))


def two_heads(x):
    col = lax.broadcasted_iota(jnp.int32, x.shape, 1)
    zero = jnp.zeros_like(x)
    return jnp.concatenate(
        [jnp.where(col < HEAD_DIM, x, zero), jnp.where(col < HEAD_DIM, zero, x)], axis=0
    )


def own_heads(x):
    return jnp.concatenate([x[:SPAN, :HEAD_DIM], x[SPAN:, HEAD_DIM:]], axis=1)


def attend_kernel(group, pieces, has_sum, *refs):
    place = refs[0]
    shards = refs[1 : 1 + pieces]
    queries, d_attn, w_key, w_value = refs[1 + pieces : 5 + pieces]
    refs = refs[5 + pieces :]
    if has_sum:
        mine_in, other_in = refs[:2]
        refs = refs[2:]
    attn_out, d_queries, mine, other = refs[:4]
    rows, q_held, g_held, grads, row_sem, q_sem = refs[4:]
    spans, part, width = shards[0].shape
    head_cols = w_key.shape[1]
    heads = head_cols // HEAD_DIM
    nbr_rows = pieces * part
    tokens = spans * SPAN
    scale = 1.0 / math.sqrt(HEAD_DIM)
    raise_by = scale / math.log(2.0)
    me = place[0]
    first = pl.multiple_of(me * (tokens * 2) + group * tokens, tokens)
    token_loads = [
        pltpu.make_async_copy(queries.at[pl.ds(first, tokens), :], q_held, q_sem.at[0]),
        pltpu.make_async_copy(d_attn.at[pl.ds(first, tokens), :], g_held, q_sem.at[1]),
    ]
    row_loads = [
        [
            pltpu.make_async_copy(
                shards[p].at[j], rows.at[j, pl.ds(p * part, part), :], row_sem.at[j, p]
            )
            for p in range(pieces)
        ]
        for j in range(spans)
    ]
    for load in row_loads[0] + token_loads:
        load.start()
    for loads in row_loads[1:]:
        for load in loads:
            load.start()
    for load in token_loads:
        load.wait()
    for j in range(spans):
        for load in row_loads[j]:
            load.wait()
        span_rows = rows[j]
        at = slice(j * SPAN, (j + 1) * SPAN)
        to = slice(j * nbr_rows, (j + 1) * nbr_rows)
        for h in range(0, heads, 2):
            cut = slice(h * HEAD_DIM, (h + 2) * HEAD_DIM)
            past = slice(head_cols + h * HEAD_DIM, head_cols + (h + 2) * HEAD_DIM)
            k = dot(span_rows, w_key[:, cut]).astype(BF16)
            v = dot(span_rows, w_value[:, cut]).astype(BF16)
            q = two_heads(q_held[at, cut])
            g = two_heads(g_held[at, cut])
            scores = dot(k, q, ROWS)
            top = jnp.max(scores, axis=0, keepdims=True)
            raised = jnp.exp2((scores - top) * raise_by)
            total = jnp.sum(raised, axis=0, keepdims=True)
            prob = raised * (1.0 / total)
            prob_b = prob.astype(BF16)
            grad_prob = dot(v, g, ROWS)
            out_dot = jnp.sum(prob * grad_prob, axis=0, keepdims=True)
            dscore = (prob * ((grad_prob - out_dot) * scale)).astype(BF16)
            attn_out[at, cut] = own_heads(dot(prob_b, v, DOWN)).astype(BF16)
            d_queries[at, cut] = own_heads(dot(dscore, k, DOWN)).astype(BF16)
            grads[to, cut] = dot(dscore, q).astype(BF16)
            grads[to, past] = dot(prob_b, g).astype(BF16)
    mean_share = 1.0 / (CH_DEV * 32)
    flat = rows[...].reshape(spans * nbr_rows, width)
    sums = dot(flat, grads[...], DOWN) * mean_share
    for h in range(heads):
        key_part = sums[:, h * HEAD_DIM : (h + 1) * HEAD_DIM]
        value_part = sums[:, head_cols + h * HEAD_DIM : head_cols + (h + 1) * HEAD_DIM]
        low = me == 0
        kept = jnp.where(low, key_part, value_part)
        sent = jnp.where(low, value_part, key_part)
        if has_sum:
            kept = kept + mine_in[h]
            sent = sent + other_in[h]
        mine[h] = kept
        other[h] = sent.astype(other.dtype)


def attend(group, ret_place, shards, queries, d_attn, w_key, w_value, sums=(), last=True):
    spans, part, width = shards[0].shape
    pieces = len(shards)
    head_cols = w_key.shape[1]
    heads = head_cols // HEAD_DIM
    tokens = spans * SPAN
    nbr_rows = pieces * part
    whole = pl.BlockSpec(memory_space=pltpu.VMEM)
    flops = 2 * spans * nbr_rows * head_cols * (4 * width + 12 * SPAN)
    return pl.pallas_call(
        functools.partial(attend_kernel, group, pieces, bool(sums)),
        out_shape=(
            jax.ShapeDtypeStruct((tokens, head_cols), BF16),
            jax.ShapeDtypeStruct((tokens, head_cols), BF16),
            jax.ShapeDtypeStruct((heads, width, HEAD_DIM), F32),
            jax.ShapeDtypeStruct((heads, width, HEAD_DIM), BF16 if last else F32),
        ),
        in_specs=[SMEM] + [ANY] * (pieces + 2) + [whole] * (2 + len(sums)),
        out_specs=(whole,) * 4,
        scratch_shapes=[
            pltpu.VMEM((spans, nbr_rows, width), BF16),
            pltpu.VMEM((tokens, head_cols), BF16),
            pltpu.VMEM((tokens, head_cols), BF16),
            pltpu.VMEM((spans * nbr_rows, 2 * head_cols), BF16),
            pltpu.SemaphoreType.DMA((spans, pieces)),
            pltpu.SemaphoreType.DMA((2,)),
        ],
        compiler_params=pltpu.CompilerParams(vmem_limit_bytes=28 << 20),
        cost_estimate=pl.CostEstimate(
            flops=flops, bytes_accessed=10 << 20, transcendentals=spans * SPAN * nbr_rows * heads
        ),
        name=f"attend{group}",
    )(ret_place, *shards, queries, d_attn, w_key, w_value, *sums)


def swap(x):
    return lax.ppermute(x, "ret", [(0, 1), (1, 0)])


def turn(x, by):
    count = lax.axis_size("tp")
    return lax.ppermute(x, "tp", [(i, (i + by) % count) for i in range(count)])


def collect(keep, got):
    keep_right, keep_left = turn(keep, 1), turn(keep, -1)
    got_right, got_left = turn(got, 1), turn(got, -1)
    return (
        keep,
        keep_right,
        keep_left,
        turn(keep_right, 1),
        got,
        got_right,
        got_left,
        turn(got_left, -1),
    )


def exchange(x):
    return lax.all_to_all(x, ("y", "z"), split_axis=0, concat_axis=0, tiled=True)


def body(queries, d_attn, pool, w_key, w_value, owners, picks, live_counts):
    ctx_count = lax.axis_size("y") * lax.axis_size("z")
    ctx_place = lax.axis_index("y") * lax.axis_size("z") + lax.axis_index("z")
    ret_place = lax.axis_index("ret")
    tp_place = lax.axis_index("tp")
    head_cols = w_key.shape[1]
    heads = head_cols // HEAD_DIM
    width = pool.shape[2]
    part = NBR_LEN // lax.axis_size("tp")
    half = CH_DEV // 2
    owner_col = lax.dynamic_index_in_dim(owners, ret_place, 1, keepdims=False)
    pick_col = lax.dynamic_index_in_dim(picks, ret_place, 1, keepdims=False)
    live = live_counts[ret_place, ctx_place]
    owner_grid = owner_col.reshape(ctx_count, CH_DEV)
    pick_grid = pick_col.reshape(ctx_count, CH_DEV)
    asked = jnp.sum(jnp.where(owner_grid == ctx_place, pick_grid, 0), axis=1)
    send_slot = asked % live
    mine = lax.dynamic_slice(owner_col, (ctx_place * CH_DEV + ret_place * half,), (half,))
    others = lax.dynamic_slice(owner_col, (ctx_place * CH_DEV + (1 - ret_place) * half,), (half,))
    wanted = jnp.concatenate([mine, others])

    pool_blocks = pool[0].reshape(-1, NBR_LEN, width)
    outgoing = pack(send_slot, tp_place.reshape(1), pool_blocks, part)
    incoming = exchange(outgoing)
    keep_a, keep_b, give_a, give_b = pick(wanted, incoming, 4)
    me = ret_place.reshape(1)
    tokens = (queries, d_attn, w_key, w_value)
    shards_a = collect(keep_a, swap(give_a))
    keep_b, give_b, _ = lax.optimization_barrier((keep_b, give_b, shards_a[1]))
    shards_b = collect(keep_b, swap(give_b))
    attn_a, dq_a, mine_a, other_a = attend(0, me, shards_a, *tokens, last=False)
    attn_b, dq_b, mine_sum, other_sum = attend(1, me, shards_b, *tokens, sums=(mine_a, other_a))
    pair = (mine_sum + swap(other_sum).astype(F32)).astype(BF16)
    chunk = heads * width // ctx_count
    terms = exchange(pair.reshape(ctx_count, chunk, HEAD_DIM))
    total = jnp.sum(terms.astype(F32), axis=0).astype(BF16)
    mine_full = exchange(jnp.broadcast_to(total[None], (ctx_count, chunk, HEAD_DIM)))
    mine_full = mine_full.reshape(heads, width, HEAD_DIM)
    other_full = swap(mine_full)
    low = ret_place == 0
    d_w_key = jnp.where(low, mine_full, other_full)
    d_w_value = jnp.where(low, other_full, mine_full)
    d_w_key = jnp.transpose(d_w_key, (1, 0, 2)).reshape(width, head_cols)
    d_w_value = jnp.transpose(d_w_value, (1, 0, 2)).reshape(width, head_cols)

    def joined(a, b):
        c, d = swap(a), swap(b)
        return jnp.concatenate(
            [jnp.where(low, x, y) for x, y in ((a, c), (b, d), (c, a), (d, b))], axis=0
        )

    return (joined(attn_a, attn_b), joined(dq_a, dq_b), d_w_key, d_w_value)


def solution(mesh):
    shape = (Y_CHIPS, mesh.shape["ctx"] // Y_CHIPS, mesh.shape["ret"], mesh.shape["tp"])
    fine = Mesh(mesh.devices.reshape(shape), ("y", "z", "ret", "tp"))
    ctx = ("y", "z")
    return jax.shard_map(
        body,
        mesh=fine,
        in_specs=(
            P(ctx, "tp"),
            P(ctx, "tp"),
            P("ret", ctx, None),
            P(None, "tp"),
            P(None, "tp"),
            P(),
            P(),
            P(),
        ),
        out_specs=(P(ctx, "tp"), P(ctx, "tp"), P(None, "tp"), P(None, "tp")),
        check_vma=False,
    )
```

```python
import functools
import math

import jax
import jax.numpy as jnp
from jax import lax
from jax.experimental import pallas as pl
from jax.experimental.pallas import tpu as pltpu
from jax.sharding import Mesh
from jax.sharding import PartitionSpec as P

HEAD_DIM = 128
SPAN = 64
NBR_LEN = 128
CH_DEV = 16
Y_CHIPS = 4


FIRST = 5

BF16 = jnp.bfloat16
F32 = jnp.float32
ANY = pl.BlockSpec(memory_space=pl.ANY)
SMEM = pl.BlockSpec(memory_space=pltpu.SMEM)
WHOLE = pl.BlockSpec(memory_space=pltpu.VMEM)


def pack_kernel(slots, place, pool, out, held, in_sem, out_sem):
    part = held.shape[1]
    start = pl.multiple_of(place[0] * part, part)
    load = pltpu.make_async_copy(pool.at[:, pl.ds(start, part), :], held, in_sem)
    load.start()
    load.wait()
    copies = [
        pltpu.make_async_copy(held.at[slots[d]], out.at[d], out_sem.at[d])
        for d in range(out.shape[0])
    ]
    for copy in copies:
        copy.start()
    for copy in copies:
        copy.wait()


def pack(send_slot, tp_place, pool_blocks, part):
    blocks, _, width = pool_blocks.shape
    count = send_slot.shape[0]
    return pl.pallas_call(
        pack_kernel,
        out_shape=jax.ShapeDtypeStruct((count, part, width), BF16),
        in_specs=[SMEM, SMEM, ANY],
        out_specs=ANY,
        scratch_shapes=[
            pltpu.VMEM((blocks, part, width), BF16),
            pltpu.SemaphoreType.DMA,
            pltpu.SemaphoreType.DMA((count,)),
        ],
        compiler_params=pltpu.CompilerParams(vmem_limit_bytes=60 << 20),
        name="pack",
    )(send_slot, tp_place, pool_blocks)


def give_kernel(wanted, incoming, give):
    for k in range(give.shape[0]):
        give[k] = incoming[wanted[k]]


def own_kernel(wanted, incoming, got, own_a, own_b):
    split = own_a.shape[1]
    for k in range(split):
        own_a[0, k] = incoming[wanted[k]]
    for k in range(own_b.shape[1]):
        own_b[0, k] = incoming[wanted[split + k]]
    own_a[1] = got[:split]
    own_b[1] = got[split:]


def give_blocks(wanted, incoming):
    shape = wanted.shape + incoming.shape[1:]
    return pl.pallas_call(
        give_kernel,
        out_shape=jax.ShapeDtypeStruct(shape, BF16),
        in_specs=[SMEM, WHOLE],
        out_specs=WHOLE,
        compiler_params=pltpu.CompilerParams(vmem_limit_bytes=8 << 20),
        name="give",
    )(wanted, incoming)


def own_blocks(wanted, incoming, got):
    count = wanted.shape[0]
    return pl.pallas_call(
        own_kernel,
        out_shape=tuple(
            jax.ShapeDtypeStruct((2, spans) + incoming.shape[1:], BF16)
            for spans in (FIRST, count - FIRST)
        ),
        in_specs=[SMEM, WHOLE, WHOLE],
        out_specs=(WHOLE, WHOLE),
        compiler_params=pltpu.CompilerParams(vmem_limit_bytes=8 << 20),
        name="own",
    )(wanted, incoming, got)


def dot(a, b, dims=((1,), (0,))):
    return lax.dot_general(a, b, (dims, ((), ())), preferred_element_type=F32)


ROWS = ((1,), (1,))
DOWN = ((0,), (0,))


def two_heads(x):
    col = lax.broadcasted_iota(jnp.int32, x.shape, 1)
    zero = jnp.zeros_like(x)
    return jnp.concatenate(
        [jnp.where(col < HEAD_DIM, x, zero), jnp.where(col < HEAD_DIM, zero, x)], axis=0
    )


def own_heads(x):
    return jnp.concatenate([x[:SPAN, :HEAD_DIM], x[SPAN:, HEAD_DIM:]], axis=1)


def attend_kernel(group, pieces, has_sum, *refs):
    place = refs[0]
    shards = refs[1 : 1 + pieces]
    queries, d_attn, w_key, w_value = refs[1 + pieces : 5 + pieces]
    refs = refs[5 + pieces :]
    if has_sum:
        mine_in, other_in = refs[:2]
        refs = refs[2:]
    tokens_out, mine, other, rows, grads = refs
    spans, part, width = shards[-1].shape
    head_cols = w_key.shape[1]
    heads = head_cols // HEAD_DIM
    nbr_rows = rows.shape[1]
    scale = 1.0 / math.sqrt(HEAD_DIM)
    raise_by = scale / math.log(2.0)
    me = place[0]
    first = me * (queries.shape[0] // 2) + group * FIRST * SPAN
    for j in range(spans):
        for p in range(2 * pieces - 2):
            held = shards[p // 2][p % 2, j] if p < 2 * pieces - 4 else shards[p - pieces + 2][j]
            rows[j, p * part : (p + 1) * part, :] = held
        span_rows = rows[j]
        at = slice(j * SPAN, (j + 1) * SPAN)
        to = slice(j * nbr_rows, (j + 1) * nbr_rows)
        read = pl.ds(pl.multiple_of(first + j * SPAN, SPAN), SPAN)
        for h in range(0, heads, 2):
            cut = slice(h * HEAD_DIM, (h + 2) * HEAD_DIM)
            past = slice(head_cols + h * HEAD_DIM, head_cols + (h + 2) * HEAD_DIM)
            k = dot(span_rows, w_key[:, cut]).astype(BF16)
            v = dot(span_rows, w_value[:, cut]).astype(BF16)
            q = two_heads(queries[read, cut])
            g = two_heads(d_attn[read, cut])
            scores = dot(k, q, ROWS)
            top = jnp.max(scores, axis=0, keepdims=True)
            raised = jnp.exp2((scores - top) * raise_by)
            total = jnp.sum(raised, axis=0, keepdims=True)
            prob = raised * (1.0 / total)
            prob_b = prob.astype(BF16)
            grad_prob = dot(v, g, ROWS)
            out_dot = jnp.sum(prob * grad_prob, axis=0, keepdims=True)
            dscore = (prob * ((grad_prob - out_dot) * scale)).astype(BF16)
            tokens_out[0, at, cut] = own_heads(dot(prob_b, v, DOWN)).astype(BF16)
            tokens_out[1, at, cut] = own_heads(dot(dscore, k, DOWN)).astype(BF16)
            grads[to, cut] = dot(dscore, q).astype(BF16)
            grads[to, past] = dot(prob_b, g).astype(BF16)
    mean_share = 1.0 / (CH_DEV * 32)
    flat = rows[...].reshape(spans * nbr_rows, width)
    sums = dot(flat, grads[...], DOWN) * mean_share
    for h in range(heads):
        key_part = sums[:, h * HEAD_DIM : (h + 1) * HEAD_DIM]
        value_part = sums[:, head_cols + h * HEAD_DIM : head_cols + (h + 1) * HEAD_DIM]
        low = me == 0
        kept = jnp.where(low, key_part, value_part)
        sent = jnp.where(low, value_part, key_part)
        if has_sum:
            kept = kept + mine_in[h]
            sent = sent + other_in[h]
        mine[h] = kept
        other[h] = sent.astype(other.dtype)


def attend(group, ret_place, shards, queries, d_attn, w_key, w_value, sums=(), last=True):
    spans, part, width = shards[-1].shape
    refs = len(shards)
    pieces = 2 * refs - 2
    head_cols = w_key.shape[1]
    heads = head_cols // HEAD_DIM
    tokens = spans * SPAN
    nbr_rows = pieces * part
    flops = 2 * spans * nbr_rows * head_cols * (4 * width + 12 * SPAN)
    return pl.pallas_call(
        functools.partial(attend_kernel, group, refs, bool(sums)),
        out_shape=(
            jax.ShapeDtypeStruct((2, tokens, head_cols), BF16),
            jax.ShapeDtypeStruct((heads, width, HEAD_DIM), F32),
            jax.ShapeDtypeStruct((heads, width, HEAD_DIM), BF16 if last else F32),
        ),
        in_specs=[SMEM] + [WHOLE] * (refs + 4 + len(sums)),
        out_specs=(WHOLE,) * 3,
        scratch_shapes=[
            pltpu.VMEM((spans, nbr_rows, width), BF16),
            pltpu.VMEM((spans * nbr_rows, 2 * head_cols), BF16),
        ],
        compiler_params=pltpu.CompilerParams(vmem_limit_bytes=28 << 20),
        cost_estimate=pl.CostEstimate(
            flops=flops, bytes_accessed=10 << 20, transcendentals=spans * SPAN * nbr_rows * heads
        ),
        name=f"attend{group}",
    )(ret_place, *shards, queries, d_attn, w_key, w_value, *sums)


def swap(x):
    return lax.ppermute(x, "ret", [(0, 1), (1, 0)])


def turn(x, by):
    count = lax.axis_size("tp")
    return lax.ppermute(x, "tp", [(i, (i + by) % count) for i in range(count)])


def near(own):
    return turn(own, 1), turn(own, -1)


def far(right, left):
    return turn(right[0], 1), turn(left[1], -1)


def exchange(x, axis):
    return lax.all_to_all(x, axis, split_axis=0, concat_axis=0, tiled=True)


def added(x):
    return jnp.sum(x.astype(F32), axis=0).astype(BF16)


def spread(x, axis):
    return exchange(jnp.broadcast_to(x[None], (lax.axis_size(axis),) + x.shape), axis)


def join_kernel(place, mine_a, mine_b, other_a, other_b, attn_out, d_queries, sem):
    me = place[0]
    half = attn_out.shape[0] // 2
    copies = []
    for side, pair in ((me, (mine_a, mine_b)), (1 - me, (other_a, other_b))):
        for group, held in enumerate(pair):
            tokens = held.shape[1]
            start = pl.multiple_of(side * half + group * FIRST * SPAN, SPAN)
            for which, out in enumerate((attn_out, d_queries)):
                copies.append(
                    pltpu.make_async_copy(
                        held.at[which], out.at[pl.ds(start, tokens), :], sem.at[len(copies)]
                    )
                )
    for copy in copies:
        copy.start()
    for copy in copies:
        copy.wait()


def join(place, mine_a, mine_b, other_a, other_b):
    rows = 2 * (mine_a.shape[1] + mine_b.shape[1])
    out = jax.ShapeDtypeStruct((rows, mine_a.shape[2]), BF16)
    return pl.pallas_call(
        join_kernel,
        out_shape=(out, out),
        in_specs=[SMEM] + [ANY] * 4,
        out_specs=(ANY, ANY),
        scratch_shapes=[pltpu.SemaphoreType.DMA((8,))],
        compiler_params=pltpu.CompilerParams(vmem_limit_bytes=4 << 20),
        name="join",
    )(place, mine_a, mine_b, other_a, other_b)


def lay_kernel(place, mine, other, d_w_key, d_w_value):
    low = place[0] == 0
    for h in range(mine.shape[0]):
        cut = slice(h * HEAD_DIM, (h + 1) * HEAD_DIM)
        d_w_key[:, cut] = jnp.where(low, mine[h], other[h])
        d_w_value[:, cut] = jnp.where(low, other[h], mine[h])


def lay(place, mine, other):
    heads, width, cols = mine.shape
    out = jax.ShapeDtypeStruct((width, heads * cols), BF16)
    return pl.pallas_call(
        lay_kernel,
        out_shape=(out, out),
        in_specs=[SMEM, WHOLE, WHOLE],
        out_specs=(WHOLE, WHOLE),
        compiler_params=pltpu.CompilerParams(vmem_limit_bytes=12 << 20),
        name="lay",
    )(place, mine, other)


def body(queries, d_attn, pool, w_key, w_value, owners, picks, live_counts):
    ctx_count = lax.axis_size("y") * lax.axis_size("z")
    ctx_place = lax.axis_index("y") * lax.axis_size("z") + lax.axis_index("z")
    ret_place = lax.axis_index("ret")
    tp_place = lax.axis_index("tp")
    z_count = lax.axis_size("z")
    width = pool.shape[2]
    part = NBR_LEN // lax.axis_size("tp")
    half = CH_DEV // 2
    low = ret_place == 0
    owner_col = jnp.where(low, owners[:, 0], owners[:, 1])
    pick_col = jnp.where(low, picks[:, 0], picks[:, 1])
    live_row = jnp.where(low, live_counts[0], live_counts[1])
    live = jnp.sum(jnp.where(jnp.arange(ctx_count) == ctx_place, live_row, 0))
    owner_grid = owner_col.reshape(ctx_count, CH_DEV)
    pick_grid = pick_col.reshape(ctx_count, CH_DEV)
    asked = jnp.sum(jnp.where(owner_grid == ctx_place, pick_grid, 0), axis=1)
    send_slot = asked % live
    mine = lax.dynamic_slice(owner_col, (ctx_place * CH_DEV + ret_place * half,), (half,))
    others = lax.dynamic_slice(owner_col, (ctx_place * CH_DEV + (1 - ret_place) * half,), (half,))
    me = ret_place.reshape(1)

    pool_blocks = pool[0].reshape(-1, NBR_LEN, width)
    outgoing = pack(send_slot, tp_place.reshape(1), pool_blocks, part)
    incoming = exchange(outgoing, ("y", "z"))
    got = swap(give_blocks(others, incoming))
    own_a, own_b = own_blocks(mine, incoming, got)
    tokens = (queries, d_attn, w_key, w_value)
    near_a = near(own_a)
    far_a = far(*near_a)
    own_b, near_a, far_a = lax.optimization_barrier((own_b, near_a, far_a))
    near_b = near(own_b)
    tokens_a, mine_a, other_a = attend(0, me, (own_a, *near_a, *far_a), *tokens, last=False)
    near_b, tokens_a, mine_a = lax.optimization_barrier((near_b, tokens_a, mine_a))
    far_b = far(*near_b)
    tokens_b, mine_sum, other_sum = attend(
        1, me, (own_b, *near_b, *far_b), *tokens, sums=(mine_a, other_a)
    )
    pair = (mine_sum + swap(other_sum).astype(F32)).astype(BF16)
    by_y = added(exchange(pair, "y"))
    attn_out, d_queries = join(me, tokens_a, tokens_b, swap(tokens_a), swap(tokens_b))
    by_z = added(exchange(by_y.reshape(z_count, width // z_count, HEAD_DIM), "z"))
    by_z, attn_out, d_queries = lax.optimization_barrier((by_z, attn_out, d_queries))
    z_full = spread(by_z, "z").reshape(width, HEAD_DIM)
    mine_full = spread(z_full, "y")
    d_w_key, d_w_value = lay(me, mine_full, swap(mine_full))
    return (attn_out, d_queries, d_w_key, d_w_value)


def solution(mesh):
    shape = (Y_CHIPS, mesh.shape["ctx"] // Y_CHIPS, mesh.shape["ret"], mesh.shape["tp"])
    fine = Mesh(mesh.devices.reshape(shape), ("y", "z", "ret", "tp"))
    ctx = ("y", "z")
    return jax.shard_map(
        body,
        mesh=fine,
        in_specs=(
            P(ctx, "tp"),
            P(ctx, "tp"),
            P("ret", ctx, None),
            P(None, "tp"),
            P(None, "tp"),
            P(),
            P(),
            P(),
        ),
        out_specs=(P(ctx, "tp"), P(ctx, "tp"), P(None, "tp"), P(None, "tp")),
        check_vma=False,
    )
```

```python
import functools
import math

import jax
import jax.numpy as jnp
from jax import lax
from jax.experimental import pallas as pl
from jax.experimental.pallas import tpu as pltpu
from jax.sharding import Mesh
from jax.sharding import PartitionSpec as P

HEAD_DIM = 128
SPAN = 64
NBR_LEN = 128
CH_DEV = 16
Y_CHIPS = 4


CHUNKS = 2

BF16 = jnp.bfloat16
F32 = jnp.float32
ANY = pl.BlockSpec(memory_space=pl.ANY)
SMEM = pl.BlockSpec(memory_space=pltpu.SMEM)
WHOLE = pl.BlockSpec(memory_space=pltpu.VMEM)


def ctx_index():
    return lax.axis_index("y") * lax.axis_size("z") + lax.axis_index("z")


def pack_kernel(row, asked, live_counts, pool, out, held, in_sem, out_sem):
    part = held.shape[1]
    chunk = lax.axis_index("tp") * CHUNKS + row
    start = pl.multiple_of(chunk * part, part)
    load = pltpu.make_async_copy(pool.at[:, pl.ds(start, part), :], held, in_sem)
    load.start()
    live = live_counts[lax.axis_index("ret"), ctx_index()]
    slots = [lax.rem(asked[d], live) for d in range(out.shape[0])]
    copies = [
        pltpu.make_async_copy(held.at[slots[d]], out.at[d], out_sem.at[d])
        for d in range(out.shape[0])
    ]
    load.wait()
    for copy in copies:
        copy.start()
    for copy in copies:
        copy.wait()


def pack(row, asked, live_counts, pool_blocks, part):
    blocks, _, width = pool_blocks.shape
    count = asked.shape[0]
    return pl.pallas_call(
        functools.partial(pack_kernel, row),
        out_shape=jax.ShapeDtypeStruct((count, part, width), BF16),
        in_specs=[SMEM, SMEM, ANY],
        out_specs=ANY,
        scratch_shapes=[
            pltpu.VMEM((blocks, part, width), BF16),
            pltpu.SemaphoreType.DMA,
            pltpu.SemaphoreType.DMA((count,)),
        ],
        compiler_params=pltpu.CompilerParams(vmem_limit_bytes=60 << 20),
        name=f"pack{row}",
    )(asked, live_counts, pool_blocks)


def give_kernel(owner_col, incoming, give):
    half = give.shape[0]
    first = ctx_index() * (2 * half) + (1 - lax.axis_index("ret")) * half
    for k in range(half):
        give[k] = incoming[owner_col[first + k]]


def own_kernel(owner_col, incoming, got, own):
    half = got.shape[0]
    first = ctx_index() * (2 * half) + lax.axis_index("ret") * half
    for k in range(half):
        own[0, k] = incoming[owner_col[first + k]]
    own[1] = got[...]


def give_blocks(owner_col, incoming):
    return pl.pallas_call(
        give_kernel,
        out_shape=jax.ShapeDtypeStruct((CH_DEV // 2,) + incoming.shape[1:], BF16),
        in_specs=[SMEM, WHOLE],
        out_specs=WHOLE,
        compiler_params=pltpu.CompilerParams(vmem_limit_bytes=8 << 20),
        name="give",
    )(owner_col, incoming)


def own_blocks(owner_col, incoming, got):
    return pl.pallas_call(
        own_kernel,
        out_shape=jax.ShapeDtypeStruct((2,) + got.shape, BF16),
        in_specs=[SMEM, WHOLE, WHOLE],
        out_specs=WHOLE,
        compiler_params=pltpu.CompilerParams(vmem_limit_bytes=8 << 20),
        name="own",
    )(owner_col, incoming, got)


def dot(a, b, dims=((1,), (0,))):
    return lax.dot_general(a, b, (dims, ((), ())), preferred_element_type=F32)


ROWS = ((1,), (1,))
DOWN = ((0,), (0,))


def two_heads(x):
    col = lax.broadcasted_iota(jnp.int32, x.shape, 1)
    zero = jnp.zeros_like(x)
    return jnp.concatenate(
        [jnp.where(col < HEAD_DIM, x, zero), jnp.where(col < HEAD_DIM, zero, x)], axis=0
    )


def own_heads(x):
    return jnp.concatenate([x[:SPAN, :HEAD_DIM], x[SPAN:, HEAD_DIM:]], axis=1)


def gather_rows(shards, rows, j):
    p = 0
    for shard in shards:
        pieces = [shard[j]] if len(shard.shape) == 3 else [shard[0, j], shard[1, j]]
        for piece in pieces:
            rows[j, p : p + piece.shape[0], :] = piece
            p += piece.shape[0]


def early_kernel(count, *refs):
    shards = refs[:count]
    queries, d_attn, w_key, w_value, q_out, g_out, k_out, v_out, rows, pairs, sem = refs[count:]
    spans, _, head_cols = pairs.shape
    head_cols //= 2
    tokens = q_out.shape[0]
    place = pl.ds(pl.multiple_of(lax.axis_index("ret") * tokens, tokens), tokens)
    loads = [
        pltpu.make_async_copy(w_key, k_out, sem.at[0]),
        pltpu.make_async_copy(w_value, v_out, sem.at[1]),
        pltpu.make_async_copy(queries.at[place, :], q_out, sem.at[2]),
        pltpu.make_async_copy(d_attn.at[place, :], g_out, sem.at[3]),
    ]
    for load in loads:
        load.start()
    for j in range(spans):
        gather_rows(shards, rows, j)
    flat = rows[...].reshape(spans * rows.shape[1], rows.shape[2])
    for load, weight, side in ((loads[0], k_out, 0), (loads[1], v_out, 1)):
        load.wait()
        made = dot(flat, weight[...]).astype(BF16).reshape(spans, rows.shape[1], head_cols)
        pairs[:, :, side * head_cols : (side + 1) * head_cols] = made
    for load in loads[2:]:
        load.wait()


def early(shards, queries, d_attn, w_key, w_value):
    spans, _, width = shards[-1].shape
    head_cols = w_key.shape[1]
    count = NBR_LEN
    half = jax.ShapeDtypeStruct((spans * SPAN, head_cols), BF16)
    weight = jax.ShapeDtypeStruct((width, head_cols), BF16)
    return pl.pallas_call(
        functools.partial(early_kernel, len(shards)),
        out_shape=(
            half,
            half,
            weight,
            weight,
            jax.ShapeDtypeStruct((spans, count, width), BF16),
            jax.ShapeDtypeStruct((spans, count, 2 * head_cols), BF16),
        ),
        in_specs=[WHOLE] * len(shards) + [ANY] * 4,
        out_specs=(WHOLE,) * 6,
        scratch_shapes=[pltpu.SemaphoreType.DMA((4,))],
        compiler_params=pltpu.CompilerParams(vmem_limit_bytes=24 << 20),
        cost_estimate=pl.CostEstimate(
            flops=4 * spans * count * width * head_cols, bytes_accessed=8 << 20, transcendentals=0
        ),
        name="early",
    )(*shards, queries, d_attn, w_key, w_value)


def attend_kernel(count, *refs):
    shards = refs[:count]
    queries, d_attn, w_key, w_value, rows_a, pairs_a, tokens_out, mine, other, rows_b, grads = refs[
        count:
    ]
    spans, near_rows, width = rows_a.shape
    head_cols = w_key.shape[1]
    heads = head_cols // HEAD_DIM
    scale = 1.0 / math.sqrt(HEAD_DIM)
    raise_by = scale / math.log(2.0)
    for j in range(spans):
        gather_rows(shards, rows_b, j)
        span_rows = rows_b[j]
        at = slice(j * SPAN, (j + 1) * SPAN)
        to = slice(j * near_rows, (j + 1) * near_rows)
        for h in range(0, heads, 2):
            cut = slice(h * HEAD_DIM, (h + 2) * HEAD_DIM)
            past = slice(head_cols + h * HEAD_DIM, head_cols + (h + 2) * HEAD_DIM)
            k_late = dot(span_rows, w_key[:, cut]).astype(BF16)
            v_late = dot(span_rows, w_value[:, cut]).astype(BF16)
            k = jnp.concatenate([pairs_a[j, :, cut], k_late], axis=0)
            v = jnp.concatenate([pairs_a[j, :, past], v_late], axis=0)
            q = two_heads(queries[at, cut])
            g = two_heads(d_attn[at, cut])
            scores = dot(k, q, ROWS)
            top = jnp.max(scores, axis=0, keepdims=True)
            raised = jnp.exp2((scores - top) * raise_by)
            total = jnp.sum(raised, axis=0, keepdims=True)
            prob = raised * (1.0 / total)
            prob_b = prob.astype(BF16)
            grad_prob = dot(v, g, ROWS)
            out_dot = jnp.sum(prob * grad_prob, axis=0, keepdims=True)
            dscore = (prob * ((grad_prob - out_dot) * scale)).astype(BF16)
            tokens_out[0, at, cut] = own_heads(dot(prob_b, v, DOWN)).astype(BF16)
            tokens_out[1, at, cut] = own_heads(dot(dscore, k, DOWN)).astype(BF16)
            k_grad = dot(dscore, q).astype(BF16)
            v_grad = dot(prob_b, g).astype(BF16)
            for side in range(2):
                part = slice(side * near_rows, (side + 1) * near_rows)
                grads[side, to, cut] = k_grad[part]
                grads[side, to, past] = v_grad[part]
    mean_share = 1.0 / (CH_DEV * 32)
    low = lax.axis_index("ret") == 0
    flat_a = rows_a[...].reshape(spans * near_rows, width)
    flat_b = rows_b[...].reshape(spans * near_rows, width)
    sums = (dot(flat_a, grads[0], DOWN) + dot(flat_b, grads[1], DOWN)) * mean_share
    for h in range(heads):
        key_part = sums[:, h * HEAD_DIM : (h + 1) * HEAD_DIM]
        value_part = sums[:, head_cols + h * HEAD_DIM : head_cols + (h + 1) * HEAD_DIM]
        mine[h] = jnp.where(low, key_part, value_part)
        other[h] = jnp.where(low, value_part, key_part).astype(other.dtype)


def attend(shards, queries, d_attn, w_key, w_value, rows_a, pairs_a):
    spans, near_rows, width = rows_a.shape
    nbr_rows = 2 * NBR_LEN
    head_cols = w_key.shape[1]
    heads = head_cols // HEAD_DIM
    tokens = spans * SPAN
    flops = 2 * spans * nbr_rows * head_cols * (3 * width + 12 * SPAN)
    return pl.pallas_call(
        functools.partial(attend_kernel, len(shards)),
        out_shape=(
            jax.ShapeDtypeStruct((2, tokens, head_cols), BF16),
            jax.ShapeDtypeStruct((heads, width, HEAD_DIM), F32),
            jax.ShapeDtypeStruct((heads, width, HEAD_DIM), BF16),
        ),
        in_specs=[WHOLE] * (len(shards) + 6),
        out_specs=(WHOLE,) * 3,
        scratch_shapes=[
            pltpu.VMEM((spans, near_rows, width), BF16),
            pltpu.VMEM((2, spans * near_rows, 2 * head_cols), BF16),
        ],
        compiler_params=pltpu.CompilerParams(vmem_limit_bytes=30 << 20),
        cost_estimate=pl.CostEstimate(
            flops=flops, bytes_accessed=10 << 20, transcendentals=spans * SPAN * nbr_rows * heads
        ),
        name="attend",
    )(*shards, queries, d_attn, w_key, w_value, rows_a, pairs_a)


def join_kernel(mine, other, attn_out, d_queries, sem):
    me = lax.axis_index("ret")
    tokens = mine.shape[1]
    copies = []
    for side, held in ((me, mine), (1 - me, other)):
        place = pl.ds(pl.multiple_of(side * tokens, tokens), tokens)
        for which, out in enumerate((attn_out, d_queries)):
            copies.append(
                pltpu.make_async_copy(held.at[which], out.at[place, :], sem.at[len(copies)])
            )
    for copy in copies:
        copy.start()
    for copy in copies:
        copy.wait()


def join(mine, other):
    out = jax.ShapeDtypeStruct((2 * mine.shape[1], mine.shape[2]), BF16)
    return pl.pallas_call(
        join_kernel,
        out_shape=(out, out),
        in_specs=[ANY] * 2,
        out_specs=(ANY, ANY),
        scratch_shapes=[pltpu.SemaphoreType.DMA((4,))],
        compiler_params=pltpu.CompilerParams(vmem_limit_bytes=4 << 20),
        name="join",
    )(mine, other)


def lay_kernel(hops, *refs):
    mine, other = refs[: len(hops)], refs[len(hops) : -2]
    d_w_key, d_w_value = refs[-2:]
    low = lax.axis_index("ret") == 0
    count = lax.axis_size("y")
    for hop, x, y in zip(hops, mine, other):
        h = lax.rem(lax.axis_index("y") + (count - hop), count)
        cut = pl.ds(pl.multiple_of(h * HEAD_DIM, HEAD_DIM), HEAD_DIM)
        d_w_key[:, cut] = jnp.where(low, x[...], y[...])
        d_w_value[:, cut] = jnp.where(low, y[...], x[...])


def lay(hops, mine, other):
    width, cols = mine[0].shape
    out = jax.ShapeDtypeStruct((width, len(hops) * cols), BF16)
    return pl.pallas_call(
        functools.partial(lay_kernel, hops),
        out_shape=(out, out),
        in_specs=[WHOLE] * (2 * len(hops)),
        out_specs=(WHOLE, WHOLE),
        compiler_params=pltpu.CompilerParams(vmem_limit_bytes=12 << 20),
        name="lay",
    )(*mine, *other)


def turn(x, axis, by):
    count = lax.axis_size(axis)
    return lax.ppermute(x, axis, [(i, (i + by) % count) for i in range(count)])


def swap(x):
    return turn(x, "ret", 1)


def near(own):
    return turn(own, "tp", 1), turn(own, "tp", -1)


def far(right, left):
    return turn(right[0], "tp", 1), turn(left[1], "tp", -1)


def exchange(x, axis):
    return lax.all_to_all(x, axis, split_axis=0, concat_axis=0, tiled=True)


def added(x):
    return jnp.sum(x.astype(F32), axis=0).astype(BF16)


def body(queries, d_attn, pool, w_key, w_value, owners, picks, live_counts):
    y_count = lax.axis_size("y")
    z_count = lax.axis_size("z")
    ctx_count = y_count * z_count
    width = pool.shape[2]
    part = NBR_LEN // lax.axis_size("tp") // CHUNKS
    low = lax.axis_index("ret") == 0
    owner_col = jnp.where(low, owners[:, 0], owners[:, 1])
    pick_col = jnp.where(low, picks[:, 0], picks[:, 1])
    asked = jnp.sum(
        jnp.where(owner_col == ctx_index(), pick_col, 0).reshape(ctx_count, CH_DEV), axis=1
    )
    pool_blocks = pool[0].reshape(-1, NBR_LEN, width)

    first = pack(0, asked, live_counts, pool_blocks, part)
    second = pack(1, asked, live_counts, pool_blocks, part)
    incoming = exchange(first, ("y", "z"))
    second, incoming = lax.optimization_barrier((second, incoming))
    late = exchange(second, ("y", "z"))
    own = own_blocks(owner_col, incoming, swap(give_blocks(owner_col, incoming)))
    sides = near(own)
    late, *shards = lax.optimization_barrier((late, own, *sides, *far(*sides)))
    held = early(shards, queries, d_attn, w_key, w_value)
    own = own_blocks(owner_col, late, swap(give_blocks(owner_col, late)))
    sides, held = lax.optimization_barrier((near(own), held))
    tokens, mine, other = attend((own, *sides, *far(*sides)), *held)
    pair = (mine + swap(other).astype(F32)).astype(BF16)
    by_y = added(exchange(pair, "y"))
    attn_out, d_queries = join(tokens, swap(tokens))
    by_z = added(exchange(by_y.reshape(z_count, width // z_count, HEAD_DIM), "z"))
    by_z, attn_out, d_queries = lax.optimization_barrier((by_z, attn_out, d_queries))
    by_z = jnp.broadcast_to(by_z[None], (z_count,) + by_z.shape)
    z_full = exchange(by_z, "z").reshape(width, HEAD_DIM)
    hops = (0, 1, y_count - 1) + tuple(range(2, y_count - 1))
    pieces = [turn(z_full, "y", hop) if hop else z_full for hop in hops]
    d_w_key, d_w_value = lay(hops, pieces, [swap(x) for x in pieces])
    return (attn_out, d_queries, d_w_key, d_w_value)


def solution(mesh):
    shape = (Y_CHIPS, mesh.shape["ctx"] // Y_CHIPS, mesh.shape["ret"], mesh.shape["tp"])
    fine = Mesh(mesh.devices.reshape(shape), ("y", "z", "ret", "tp"))
    ctx = ("y", "z")
    return jax.shard_map(
        body,
        mesh=fine,
        in_specs=(
            P(ctx, "tp"),
            P(ctx, "tp"),
            P("ret", ctx, None),
            P(None, "tp"),
            P(None, "tp"),
            P(),
            P(),
            P(),
        ),
        out_specs=(P(ctx, "tp"), P(ctx, "tp"), P(None, "tp"), P(None, "tp")),
        check_vma=False,
    )
```

```python
import functools
import math

import jax
import jax.numpy as jnp
from jax import lax
from jax.experimental import pallas as pl
from jax.experimental.pallas import tpu as pltpu
from jax.sharding import Mesh
from jax.sharding import PartitionSpec as P

HEAD_DIM = 128
SPAN = 64
NBR_LEN = 128
CH_DEV = 16
Y_CHIPS = 4


CHUNKS = 2
TOGETHER = 2

BF16 = jnp.bfloat16
F32 = jnp.float32
ANY = pl.BlockSpec(memory_space=pl.ANY)
SMEM = pl.BlockSpec(memory_space=pltpu.SMEM)
WHOLE = pl.BlockSpec(memory_space=pltpu.VMEM)


def ctx_index():
    return lax.axis_index("y") * lax.axis_size("z") + lax.axis_index("z")


def pack_kernel(row, asked, live_counts, pool, out, held, in_sem, out_sem):
    part = held.shape[1]
    chunk = lax.axis_index("tp") * CHUNKS + row
    start = pl.multiple_of(chunk * part, part)
    load = pltpu.make_async_copy(pool.at[:, pl.ds(start, part), :], held, in_sem)
    load.start()
    live = live_counts[lax.axis_index("ret"), ctx_index()]
    slots = [lax.rem(asked[d], live) for d in range(out.shape[0])]
    copies = [
        pltpu.make_async_copy(held.at[slots[d]], out.at[d], out_sem.at[d])
        for d in range(out.shape[0])
    ]
    load.wait()
    for copy in copies:
        copy.start()
    for copy in copies:
        copy.wait()


def pack(row, asked, live_counts, pool_blocks, part):
    blocks, _, width = pool_blocks.shape
    count = asked.shape[0]
    return pl.pallas_call(
        functools.partial(pack_kernel, row),
        out_shape=jax.ShapeDtypeStruct((count, part, width), BF16),
        in_specs=[SMEM, SMEM, ANY],
        out_specs=ANY,
        scratch_shapes=[
            pltpu.VMEM((blocks, part, width), BF16),
            pltpu.SemaphoreType.DMA,
            pltpu.SemaphoreType.DMA((count,)),
        ],
        compiler_params=pltpu.CompilerParams(vmem_limit_bytes=60 << 20),
        name=f"pack{row}",
    )(asked, live_counts, pool_blocks)


def pick_kernel(owner_col, incoming, keep, give):
    half = keep.shape[0]
    me = lax.axis_index("ret")
    first = ctx_index() * (2 * half)
    for k in range(half):
        keep[k] = incoming[owner_col[first + me * half + k]]
        give[k] = incoming[owner_col[first + (1 - me) * half + k]]


def pick(owner_col, incoming):
    half = jax.ShapeDtypeStruct((CH_DEV // 2,) + incoming.shape[1:], BF16)
    return pl.pallas_call(
        pick_kernel,
        out_shape=(half, half),
        in_specs=[SMEM, WHOLE],
        out_specs=(WHOLE, WHOLE),
        compiler_params=pltpu.CompilerParams(vmem_limit_bytes=8 << 20),
        name="pick",
    )(owner_col, incoming)


def dot(a, b, dims=((1,), (0,))):
    return lax.dot_general(a, b, (dims, ((), ())), preferred_element_type=F32)


ROWS = ((1,), (1,))
DOWN = ((0,), (0,))


def two_heads(x):
    col = lax.broadcasted_iota(jnp.int32, x.shape, 1)
    zero = jnp.zeros_like(x)
    return jnp.concatenate(
        [jnp.where(col < HEAD_DIM, x, zero), jnp.where(col < HEAD_DIM, zero, x)], axis=0
    )


def own_heads(x):
    return jnp.concatenate([x[:SPAN, :HEAD_DIM], x[SPAN:, HEAD_DIM:]], axis=1)


def gather_rows(shards, rows, j):
    part = shards[0].shape[1]
    for p, shard in enumerate(shards):
        rows[j, p * part : (p + 1) * part, :] = shard[j]


def early_kernel(count, *refs):
    shards = refs[:count]
    queries, d_attn, w_key, w_value, q_out, g_out, k_out, v_out, rows, pairs, sem = refs[count:]
    spans, _, head_cols = pairs.shape
    head_cols //= 2
    tokens = q_out.shape[0]
    place = pl.ds(pl.multiple_of(lax.axis_index("ret") * tokens, tokens), tokens)
    loads = [
        pltpu.make_async_copy(w_key, k_out, sem.at[0]),
        pltpu.make_async_copy(w_value, v_out, sem.at[1]),
        pltpu.make_async_copy(queries.at[place, :], q_out, sem.at[2]),
        pltpu.make_async_copy(d_attn.at[place, :], g_out, sem.at[3]),
    ]
    for load in loads:
        load.start()
    for j in range(spans):
        gather_rows(shards, rows, j)
    flat = rows[...].reshape(spans * rows.shape[1], rows.shape[2])
    for load, weight, side in ((loads[0], k_out, 0), (loads[1], v_out, 1)):
        load.wait()
        made = dot(flat, weight[...]).astype(BF16).reshape(spans, rows.shape[1], head_cols)
        pairs[:, :, side * head_cols : (side + 1) * head_cols] = made
    for load in loads[2:]:
        load.wait()


def early(shards, queries, d_attn, w_key, w_value):
    spans, _, width = shards[-1].shape
    head_cols = w_key.shape[1]
    count = NBR_LEN
    half = jax.ShapeDtypeStruct((spans * SPAN, head_cols), BF16)
    weight = jax.ShapeDtypeStruct((width, head_cols), BF16)
    return pl.pallas_call(
        functools.partial(early_kernel, len(shards)),
        out_shape=(
            half,
            half,
            weight,
            weight,
            jax.ShapeDtypeStruct((spans, count, width), BF16),
            jax.ShapeDtypeStruct((spans, count, 2 * head_cols), BF16),
        ),
        in_specs=[WHOLE] * len(shards) + [ANY] * 4,
        out_specs=(WHOLE,) * 6,
        scratch_shapes=[pltpu.SemaphoreType.DMA((4,))],
        compiler_params=pltpu.CompilerParams(vmem_limit_bytes=12 << 20),
        cost_estimate=pl.CostEstimate(
            flops=4 * spans * count * width * head_cols, bytes_accessed=8 << 20, transcendentals=0
        ),
        name="early",
    )(*shards, queries, d_attn, w_key, w_value)


def weight_sum(rows_a, rows_b, grads, side):
    head_cols = grads.shape[2] // 2
    cut = pl.ds(pl.multiple_of(side * head_cols, head_cols), head_cols)
    total = None
    for at, rows in enumerate((rows_a, rows_b)):
        flat = rows[...].reshape(-1, rows.shape[2])
        term = dot(flat, grads[at, :, cut], DOWN)
        total = term if total is None else total + term
    return total * (1.0 / (CH_DEV * 32))


def attend_kernel(count, *refs):
    shards = refs[:count]
    queries, d_attn, w_key, w_value, rows_a, pairs_a, tokens_out, other, rows_b, grads = refs[count:]
    spans, near_rows, width = rows_a.shape
    head_cols = w_key.shape[1]
    heads = head_cols // HEAD_DIM
    scale = 1.0 / math.sqrt(HEAD_DIM)
    raise_by = scale / math.log(2.0)
    for start in range(0, spans, TOGETHER):
        units = []
        for j in range(start, start + TOGETHER):
            gather_rows(shards, rows_b, j)
            units += [
                (
                    j,
                    slice(h * HEAD_DIM, (h + 2) * HEAD_DIM),
                    slice(head_cols + h * HEAD_DIM, head_cols + (h + 2) * HEAD_DIM),
                    slice(j * SPAN, (j + 1) * SPAN),
                    slice(j * near_rows, (j + 1) * near_rows),
                )
                for h in range(0, heads, 2)
            ]

        def made(weight, j, cut, early_cut):
            late = dot(rows_b[j], weight[:, cut]).astype(BF16)
            return jnp.concatenate([pairs_a[j, :, early_cut], late], axis=0)

        keys = [made(w_key, j, cut, cut) for j, cut, _, _, _ in units]
        values = [made(w_value, j, cut, past) for j, cut, past, _, _ in units]
        qs = [two_heads(queries[at, cut]) for _, cut, _, at, _ in units]
        gs = [two_heads(d_attn[at, cut]) for _, cut, _, at, _ in units]
        scores = [dot(k, q, ROWS) for k, q in zip(keys, qs)]
        grad_probs = [dot(v, g, ROWS) for v, g in zip(values, gs)]
        tops = [jnp.max(x, axis=0, keepdims=True) for x in scores]
        raised = [jnp.exp2((x - top) * raise_by) for x, top in zip(scores, tops)]
        probs = [x * (1.0 / jnp.sum(x, axis=0, keepdims=True)) for x in raised]
        probs_b = [x.astype(BF16) for x in probs]
        out_dots = [jnp.sum(p * g, axis=0, keepdims=True) for p, g in zip(probs, grad_probs)]
        dscores = [
            (p * ((g - o) * scale)).astype(BF16) for p, g, o in zip(probs, grad_probs, out_dots)
        ]
        for i, (_, cut, past, at, to) in enumerate(units):
            k_grad = dot(dscores[i], qs[i]).astype(BF16)
            v_grad = dot(probs_b[i], gs[i]).astype(BF16)
            for side in range(2):
                part = slice(side * near_rows, (side + 1) * near_rows)
                grads[side, to, cut] = k_grad[part]
                grads[side, to, past] = v_grad[part]
            tokens_out[0, at, cut] = own_heads(dot(probs_b[i], values[i], DOWN)).astype(BF16)
            tokens_out[1, at, cut] = own_heads(dot(dscores[i], keys[i], DOWN)).astype(BF16)
    sums = weight_sum(rows_a, rows_b, grads, 1 - lax.axis_index("ret"))
    for h in range(heads):
        other[h] = sums[:, h * HEAD_DIM : (h + 1) * HEAD_DIM].astype(other.dtype)


def attend(shards, queries, d_attn, w_key, w_value, rows_a, pairs_a):
    spans, near_rows, width = rows_a.shape
    nbr_rows = 2 * NBR_LEN
    head_cols = w_key.shape[1]
    heads = head_cols // HEAD_DIM
    tokens = spans * SPAN
    flops = 2 * spans * nbr_rows * head_cols * (2 * width + 12 * SPAN)
    return pl.pallas_call(
        functools.partial(attend_kernel, len(shards)),
        out_shape=(
            jax.ShapeDtypeStruct((2, tokens, head_cols), BF16),
            jax.ShapeDtypeStruct((heads, width, HEAD_DIM), BF16),
            jax.ShapeDtypeStruct((spans, near_rows, width), BF16),
            jax.ShapeDtypeStruct((2, spans * near_rows, 2 * head_cols), BF16),
        ),
        in_specs=[WHOLE] * (len(shards) + 6),
        out_specs=(WHOLE,) * 4,
        compiler_params=pltpu.CompilerParams(vmem_limit_bytes=16 << 20),
        cost_estimate=pl.CostEstimate(
            flops=flops, bytes_accessed=10 << 20, transcendentals=spans * SPAN * nbr_rows * heads
        ),
        name="attend",
    )(*shards, queries, d_attn, w_key, w_value, rows_a, pairs_a)


def own_sum_kernel(rows_a, rows_b, grads, mine):
    sums = weight_sum(rows_a, rows_b, grads, lax.axis_index("ret"))
    for h in range(mine.shape[0]):
        mine[h] = sums[:, h * HEAD_DIM : (h + 1) * HEAD_DIM]


def own_sum(rows_a, rows_b, grads):
    width = rows_a.shape[2]
    heads = grads.shape[2] // 2 // HEAD_DIM
    return pl.pallas_call(
        own_sum_kernel,
        out_shape=jax.ShapeDtypeStruct((heads, width, HEAD_DIM), F32),
        in_specs=[WHOLE] * 3,
        out_specs=WHOLE,
        compiler_params=pltpu.CompilerParams(vmem_limit_bytes=16 << 20),
        cost_estimate=pl.CostEstimate(
            flops=4 * grads.shape[1] * width * heads * HEAD_DIM,
            bytes_accessed=4 << 20,
            transcendentals=0,
        ),
        name="own_sum",
    )(rows_a, rows_b, grads)


def join_kernel(mine, other, attn_out, d_queries, sem):
    me = lax.axis_index("ret")
    tokens = mine.shape[1]
    copies = []
    for side, held in ((me, mine), (1 - me, other)):
        place = pl.ds(pl.multiple_of(side * tokens, tokens), tokens)
        for which, out in enumerate((attn_out, d_queries)):
            copies.append(
                pltpu.make_async_copy(held.at[which], out.at[place, :], sem.at[len(copies)])
            )
    for copy in copies:
        copy.start()
    for copy in copies:
        copy.wait()


def join(mine, other):
    out = jax.ShapeDtypeStruct((2 * mine.shape[1], mine.shape[2]), BF16)
    return pl.pallas_call(
        join_kernel,
        out_shape=(out, out),
        in_specs=[ANY] * 2,
        out_specs=(ANY, ANY),
        scratch_shapes=[pltpu.SemaphoreType.DMA((4,))],
        compiler_params=pltpu.CompilerParams(vmem_limit_bytes=4 << 20),
        name="join",
    )(mine, other)


def lay_kernel(hops, *refs):
    mine, other = refs[: len(hops)], refs[len(hops) : -2]
    d_w_key, d_w_value = refs[-2:]
    low = lax.axis_index("ret") == 0
    count = lax.axis_size("y")
    for hop, x, y in zip(hops, mine, other):
        h = lax.rem(lax.axis_index("y") + (count - hop), count)
        cut = pl.ds(pl.multiple_of(h * HEAD_DIM, HEAD_DIM), HEAD_DIM)
        d_w_key[:, cut] = jnp.where(low, x[...], y[...])
        d_w_value[:, cut] = jnp.where(low, y[...], x[...])


def lay(hops, mine, other):
    width, cols = mine[0].shape
    out = jax.ShapeDtypeStruct((width, len(hops) * cols), BF16)
    return pl.pallas_call(
        functools.partial(lay_kernel, hops),
        out_shape=(out, out),
        in_specs=[WHOLE] * (2 * len(hops)),
        out_specs=(WHOLE, WHOLE),
        compiler_params=pltpu.CompilerParams(vmem_limit_bytes=12 << 20),
        name="lay",
    )(*mine, *other)


def turn(x, axis, by):
    count = lax.axis_size(axis)
    return lax.ppermute(x, axis, [(i, (i + by) % count) for i in range(count)])


def swap(x):
    return turn(x, "ret", 1)


def cross(x, by):
    count = lax.axis_size("tp")
    return lax.ppermute(
        x,
        ("ret", "tp"),
        [(r * count + i, (1 - r) * count + (i + by) % count) for r in range(2) for i in range(count)],
    )


def near(keep, give):
    return turn(keep, "tp", 1), cross(give, -1), turn(keep, "tp", -1), cross(give, 1), cross(give, 0)


def far(keep_right, got_left):
    return turn(keep_right, "tp", 1), turn(got_left, "tp", -1)


def exchange(x, axis):
    return lax.all_to_all(x, axis, split_axis=0, concat_axis=0, tiled=True)


def added(x):
    return jnp.sum(x.astype(F32), axis=0).astype(BF16)


def body(queries, d_attn, pool, w_key, w_value, owners, picks, live_counts):
    y_count = lax.axis_size("y")
    z_count = lax.axis_size("z")
    ctx_count = y_count * z_count
    width = pool.shape[2]
    part = NBR_LEN // lax.axis_size("tp") // CHUNKS
    low = lax.axis_index("ret") == 0
    owner_col = jnp.where(low, owners[:, 0], owners[:, 1])
    pick_col = jnp.where(low, picks[:, 0], picks[:, 1])
    asked = jnp.sum(
        jnp.where(owner_col == ctx_index(), pick_col, 0).reshape(ctx_count, CH_DEV), axis=1
    )
    pool_blocks = pool[0].reshape(-1, NBR_LEN, width)

    first = pack(0, asked, live_counts, pool_blocks, part)
    second = pack(1, asked, live_counts, pool_blocks, part)
    incoming = exchange(first, ("y", "z"))
    second, incoming = lax.optimization_barrier((second, incoming))
    late = exchange(second, ("y", "z"))
    keep, give = pick(owner_col, incoming)
    sides = near(keep, give)
    late, *shards = lax.optimization_barrier((late, keep, *sides, *far(*sides[:2])))
    held = early(shards, queries, d_attn, w_key, w_value)
    keep, give = pick(owner_col, late)
    sides = near(keep, give)
    sides, held = lax.optimization_barrier((sides, held))
    tokens, other, rows, grads = attend((keep, *sides, *far(*sides[:2])), *held)
    pair = (own_sum(held[4], rows, grads) + swap(other).astype(F32)).astype(BF16)
    by_y = added(exchange(pair, "y"))
    attn_out, d_queries = join(tokens, swap(tokens))
    by_z = added(exchange(by_y.reshape(z_count, width // z_count, HEAD_DIM), "z"))
    by_z, attn_out, d_queries = lax.optimization_barrier((by_z, attn_out, d_queries))
    by_z = jnp.broadcast_to(by_z[None], (z_count,) + by_z.shape)
    z_full = exchange(by_z, "z").reshape(width, HEAD_DIM)
    hops = (0, 1, y_count - 1) + tuple(range(2, y_count - 1))
    pieces = [turn(z_full, "y", hop) if hop else z_full for hop in hops]
    d_w_key, d_w_value = lay(hops, pieces, [swap(x) for x in pieces])
    return (attn_out, d_queries, d_w_key, d_w_value)


def solution(mesh):
    shape = (Y_CHIPS, mesh.shape["ctx"] // Y_CHIPS, mesh.shape["ret"], mesh.shape["tp"])
    fine = Mesh(mesh.devices.reshape(shape), ("y", "z", "ret", "tp"))
    ctx = ("y", "z")
    return jax.shard_map(
        body,
        mesh=fine,
        in_specs=(
            P(ctx, "tp"),
            P(ctx, "tp"),
            P("ret", ctx, None),
            P(None, "tp"),
            P(None, "tp"),
            P(),
            P(),
            P(),
        ),
        out_specs=(P(ctx, "tp"), P(ctx, "tp"), P(None, "tp"), P(None, "tp")),
        check_vma=False,
    )
```

```python
import functools
import math

import jax
import jax.numpy as jnp
from jax import lax
from jax.experimental import pallas as pl
from jax.experimental.pallas import tpu as pltpu
from jax.sharding import Mesh
from jax.sharding import PartitionSpec as P

HEAD_DIM = 128
SPAN = 64
NBR_LEN = 128
CH_DEV = 16
Y_CHIPS = 4


CHUNKS = 2
TOGETHER = 2

BF16 = jnp.bfloat16
F32 = jnp.float32
ANY = pl.BlockSpec(memory_space=pl.ANY)
SMEM = pl.BlockSpec(memory_space=pltpu.SMEM)
WHOLE = pl.BlockSpec(memory_space=pltpu.VMEM)


def ctx_index():
    return lax.axis_index("y") * lax.axis_size("z") + lax.axis_index("z")


def pack_kernel(row, asked, live_counts, pool, out, held, in_sem, out_sem):
    part = held.shape[1]
    chunk = lax.axis_index("tp") * CHUNKS + row
    start = pl.multiple_of(chunk * part, part)
    load = pltpu.make_async_copy(pool.at[:, pl.ds(start, part), :], held, in_sem)
    load.start()
    live = live_counts[lax.axis_index("ret"), ctx_index()]
    slots = [lax.rem(asked[d], live) for d in range(out.shape[0])]
    copies = [
        pltpu.make_async_copy(held.at[slots[d]], out.at[d], out_sem.at[d])
        for d in range(out.shape[0])
    ]
    load.wait()
    for copy in copies:
        copy.start()
    for copy in copies:
        copy.wait()


def pack(row, asked, live_counts, pool_blocks, part):
    blocks, _, width = pool_blocks.shape
    count = asked.shape[0]
    return pl.pallas_call(
        functools.partial(pack_kernel, row),
        out_shape=jax.ShapeDtypeStruct((count, part, width), BF16),
        in_specs=[SMEM, SMEM, ANY],
        out_specs=ANY,
        scratch_shapes=[
            pltpu.VMEM((blocks, part, width), BF16),
            pltpu.SemaphoreType.DMA,
            pltpu.SemaphoreType.DMA((count,)),
        ],
        compiler_params=pltpu.CompilerParams(vmem_limit_bytes=60 << 20),
        name=f"pack{row}",
    )(asked, live_counts, pool_blocks)


def pick_kernel(owner_col, incoming, keep, give):
    half = keep.shape[0]
    me = lax.axis_index("ret")
    first = ctx_index() * (2 * half)
    for k in range(half):
        keep[k] = incoming[owner_col[first + me * half + k]]
        give[k] = incoming[owner_col[first + (1 - me) * half + k]]


def pick(owner_col, incoming):
    half = jax.ShapeDtypeStruct((CH_DEV // 2,) + incoming.shape[1:], BF16)
    return pl.pallas_call(
        pick_kernel,
        out_shape=(half, half),
        in_specs=[SMEM, WHOLE],
        out_specs=(WHOLE, WHOLE),
        compiler_params=pltpu.CompilerParams(vmem_limit_bytes=8 << 20),
        name="pick",
    )(owner_col, incoming)


def dot(a, b, dims=((1,), (0,))):
    return lax.dot_general(a, b, (dims, ((), ())), preferred_element_type=F32)


ROWS = ((1,), (1,))
DOWN = ((0,), (0,))


def two_heads(x):
    col = lax.broadcasted_iota(jnp.int32, x.shape, 1)
    zero = jnp.zeros_like(x)
    return jnp.concatenate(
        [jnp.where(col < HEAD_DIM, x, zero), jnp.where(col < HEAD_DIM, zero, x)], axis=0
    )


def own_heads(x):
    return jnp.concatenate([x[:SPAN, :HEAD_DIM], x[SPAN:, HEAD_DIM:]], axis=1)


def gather_rows(shards, rows, j):
    part = shards[0].shape[1]
    for p, shard in enumerate(shards):
        rows[j, p * part : (p + 1) * part, :] = shard[j]


def hold_kernel(queries, d_attn, w_key, w_value, q_out, g_out, k_out, v_out, sem):
    tokens = q_out.shape[0]
    place = pl.ds(pl.multiple_of(lax.axis_index("ret") * tokens, tokens), tokens)
    loads = [
        pltpu.make_async_copy(queries.at[place, :], q_out, sem.at[0]),
        pltpu.make_async_copy(d_attn.at[place, :], g_out, sem.at[1]),
        pltpu.make_async_copy(w_key, k_out, sem.at[2]),
        pltpu.make_async_copy(w_value, v_out, sem.at[3]),
    ]
    for load in loads:
        load.start()
    for load in loads:
        load.wait()


def hold(queries, d_attn, w_key, w_value):
    half = jax.ShapeDtypeStruct((queries.shape[0] // 2, queries.shape[1]), BF16)
    weight = jax.ShapeDtypeStruct(w_key.shape, BF16)
    return pl.pallas_call(
        hold_kernel,
        out_shape=(half, half, weight, weight),
        in_specs=[ANY] * 4,
        out_specs=(WHOLE,) * 4,
        scratch_shapes=[pltpu.SemaphoreType.DMA((4,))],
        compiler_params=pltpu.CompilerParams(vmem_limit_bytes=60 << 20),
        cost_estimate=pl.CostEstimate(flops=0, bytes_accessed=6 << 20, transcendentals=0),
        name="hold",
    )(queries, d_attn, w_key, w_value)


def project_kernel(count, *refs):
    shards = refs[:count]
    w_key, w_value, rows, pairs = refs[count:]
    spans, held, head_cols = pairs.shape
    head_cols //= 2
    for j in range(spans):
        gather_rows(shards, rows, j)
    flat = rows[...].reshape(spans * held, rows.shape[2])
    for side, weight in enumerate((w_key, w_value)):
        made = dot(flat, weight[...]).astype(BF16).reshape(spans, held, head_cols)
        pairs[:, :, side * head_cols : (side + 1) * head_cols] = made


def project(shards, w_key, w_value, name):
    spans, part, width = shards[0].shape
    head_cols = w_key.shape[1]
    count = len(shards) * part
    return pl.pallas_call(
        functools.partial(project_kernel, len(shards)),
        out_shape=(
            jax.ShapeDtypeStruct((spans, count, width), BF16),
            jax.ShapeDtypeStruct((spans, count, 2 * head_cols), BF16),
        ),
        in_specs=[WHOLE] * (len(shards) + 2),
        out_specs=(WHOLE,) * 2,
        compiler_params=pltpu.CompilerParams(vmem_limit_bytes=12 << 20),
        cost_estimate=pl.CostEstimate(
            flops=4 * spans * count * width * head_cols, bytes_accessed=4 << 20, transcendentals=0
        ),
        name=name,
    )(*shards, w_key, w_value)


def weight_sum(rows_a, rows_b, grads, side):
    head_cols = grads.shape[2] // 2
    cut = pl.ds(pl.multiple_of(side * head_cols, head_cols), head_cols)
    total = None
    for at, rows in enumerate((rows_a, rows_b)):
        flat = rows[...].reshape(-1, rows.shape[2])
        term = dot(flat, grads[at, :, cut], DOWN)
        total = term if total is None else total + term
    return total * (1.0 / (CH_DEV * 32))


def attend_kernel(count, *refs):
    shards = refs[:count]
    queries, d_attn, w_key, w_value, rows_a, pairs_a, rows_m, pairs_m = refs[count : count + 8]
    tokens_out, other, rows_b, grads, far_rows = refs[count + 8 :]
    spans, near_rows, width = rows_a.shape
    far_count = far_rows.shape[1]
    head_cols = w_key.shape[1]
    heads = head_cols // HEAD_DIM
    scale = 1.0 / math.sqrt(HEAD_DIM)
    raise_by = scale / math.log(2.0)
    for j in range(spans):
        gather_rows(shards, far_rows, j)
        rows_b[j, : near_rows - far_count, :] = rows_m[j]
        rows_b[j, near_rows - far_count :, :] = far_rows[j]
    far_flat = far_rows[...].reshape(spans * far_count, width)
    far_keys = dot(far_flat, w_key[...]).astype(BF16)
    far_values = dot(far_flat, w_value[...]).astype(BF16)
    for start in range(0, spans, TOGETHER):
        units = []
        for j in range(start, start + TOGETHER):
            units += [
                (
                    j,
                    slice(h * HEAD_DIM, (h + 2) * HEAD_DIM),
                    slice(head_cols + h * HEAD_DIM, head_cols + (h + 2) * HEAD_DIM),
                    slice(j * SPAN, (j + 1) * SPAN),
                    slice(j * near_rows, (j + 1) * near_rows),
                )
                for h in range(0, heads, 2)
            ]

        def made(far, j, cut, side_cut):
            late = far[j * far_count : (j + 1) * far_count, cut]
            return jnp.concatenate([pairs_a[j, :, side_cut], pairs_m[j, :, side_cut], late], axis=0)

        keys = [made(far_keys, j, cut, cut) for j, cut, _, _, _ in units]
        values = [made(far_values, j, cut, past) for j, cut, past, _, _ in units]
        qs = [two_heads(queries[at, cut]) for _, cut, _, at, _ in units]
        gs = [two_heads(d_attn[at, cut]) for _, cut, _, at, _ in units]
        scores = [dot(k, q, ROWS) for k, q in zip(keys, qs)]
        grad_probs = [dot(v, g, ROWS) for v, g in zip(values, gs)]
        tops = [jnp.max(x, axis=0, keepdims=True) for x in scores]
        raised = [jnp.exp2((x - top) * raise_by) for x, top in zip(scores, tops)]
        probs = [x * (1.0 / jnp.sum(x, axis=0, keepdims=True)) for x in raised]
        probs_b = [x.astype(BF16) for x in probs]
        out_dots = [jnp.sum(p * g, axis=0, keepdims=True) for p, g in zip(probs, grad_probs)]
        dscores = [
            (p * ((g - o) * scale)).astype(BF16) for p, g, o in zip(probs, grad_probs, out_dots)
        ]
        for i, (_, cut, past, at, to) in enumerate(units):
            k_grad = dot(dscores[i], qs[i]).astype(BF16)
            v_grad = dot(probs_b[i], gs[i]).astype(BF16)
            for side in range(2):
                part = slice(side * near_rows, (side + 1) * near_rows)
                grads[side, to, cut] = k_grad[part]
                grads[side, to, past] = v_grad[part]
            tokens_out[0, at, cut] = own_heads(dot(probs_b[i], values[i], DOWN)).astype(BF16)
            tokens_out[1, at, cut] = own_heads(dot(dscores[i], keys[i], DOWN)).astype(BF16)
    sums = weight_sum(rows_a, rows_b, grads, 1 - lax.axis_index("ret"))
    for h in range(heads):
        other[h] = sums[:, h * HEAD_DIM : (h + 1) * HEAD_DIM].astype(other.dtype)


def attend(shards, queries, d_attn, w_key, w_value, rows_a, pairs_a, rows_m, pairs_m):
    spans, near_rows, width = rows_a.shape
    nbr_rows = 2 * NBR_LEN
    head_cols = w_key.shape[1]
    heads = head_cols // HEAD_DIM
    tokens = spans * SPAN
    flops = 2 * spans * nbr_rows * head_cols * (2 * width + 12 * SPAN)
    return pl.pallas_call(
        functools.partial(attend_kernel, len(shards)),
        out_shape=(
            jax.ShapeDtypeStruct((2, tokens, head_cols), BF16),
            jax.ShapeDtypeStruct((heads, width, HEAD_DIM), BF16),
            jax.ShapeDtypeStruct((spans, near_rows, width), BF16),
            jax.ShapeDtypeStruct((2, spans * near_rows, 2 * head_cols), BF16),
        ),
        in_specs=[WHOLE] * (len(shards) + 8),
        out_specs=(WHOLE,) * 4,
        scratch_shapes=[pltpu.VMEM((spans, near_rows - rows_m.shape[1], width), BF16)],
        compiler_params=pltpu.CompilerParams(vmem_limit_bytes=16 << 20),
        cost_estimate=pl.CostEstimate(
            flops=flops, bytes_accessed=10 << 20, transcendentals=spans * SPAN * nbr_rows * heads
        ),
        name="attend",
    )(*shards, queries, d_attn, w_key, w_value, rows_a, pairs_a, rows_m, pairs_m)


def own_sum_kernel(rows_a, rows_b, grads, mine):
    sums = weight_sum(rows_a, rows_b, grads, lax.axis_index("ret"))
    for h in range(mine.shape[0]):
        mine[h] = sums[:, h * HEAD_DIM : (h + 1) * HEAD_DIM]


def own_sum(rows_a, rows_b, grads):
    width = rows_a.shape[2]
    heads = grads.shape[2] // 2 // HEAD_DIM
    return pl.pallas_call(
        own_sum_kernel,
        out_shape=jax.ShapeDtypeStruct((heads, width, HEAD_DIM), F32),
        in_specs=[WHOLE] * 3,
        out_specs=WHOLE,
        compiler_params=pltpu.CompilerParams(vmem_limit_bytes=16 << 20),
        cost_estimate=pl.CostEstimate(
            flops=4 * grads.shape[1] * width * heads * HEAD_DIM,
            bytes_accessed=4 << 20,
            transcendentals=0,
        ),
        name="own_sum",
    )(rows_a, rows_b, grads)


def join_kernel(mine, other, attn_out, d_queries, sem):
    me = lax.axis_index("ret")
    tokens = mine.shape[1]
    copies = []
    for side, held in ((me, mine), (1 - me, other)):
        place = pl.ds(pl.multiple_of(side * tokens, tokens), tokens)
        for which, out in enumerate((attn_out, d_queries)):
            copies.append(
                pltpu.make_async_copy(held.at[which], out.at[place, :], sem.at[len(copies)])
            )
    for copy in copies:
        copy.start()
    for copy in copies:
        copy.wait()


def join(mine, other):
    out = jax.ShapeDtypeStruct((2 * mine.shape[1], mine.shape[2]), BF16)
    return pl.pallas_call(
        join_kernel,
        out_shape=(out, out),
        in_specs=[ANY] * 2,
        out_specs=(ANY, ANY),
        scratch_shapes=[pltpu.SemaphoreType.DMA((4,))],
        compiler_params=pltpu.CompilerParams(vmem_limit_bytes=4 << 20),
        name="join",
    )(mine, other)


def lay_kernel(hops, *refs):
    mine, other = refs[: len(hops)], refs[len(hops) : -2]
    d_w_key, d_w_value = refs[-2:]
    low = lax.axis_index("ret") == 0
    count = lax.axis_size("y")
    for hop, x, y in zip(hops, mine, other):
        h = lax.rem(lax.axis_index("y") + (count - hop), count)
        cut = pl.ds(pl.multiple_of(h * HEAD_DIM, HEAD_DIM), HEAD_DIM)
        d_w_key[:, cut] = jnp.where(low, x[...], y[...])
        d_w_value[:, cut] = jnp.where(low, y[...], x[...])


def lay(hops, mine, other):
    width, cols = mine[0].shape
    out = jax.ShapeDtypeStruct((width, len(hops) * cols), BF16)
    return pl.pallas_call(
        functools.partial(lay_kernel, hops),
        out_shape=(out, out),
        in_specs=[WHOLE] * (2 * len(hops)),
        out_specs=(WHOLE, WHOLE),
        compiler_params=pltpu.CompilerParams(vmem_limit_bytes=12 << 20),
        name="lay",
    )(*mine, *other)


def turn(x, axis, by):
    count = lax.axis_size(axis)
    return lax.ppermute(x, axis, [(i, (i + by) % count) for i in range(count)])


def swap(x):
    return turn(x, "ret", 1)


def cross(x, by):
    count = lax.axis_size("tp")
    return lax.ppermute(
        x,
        ("ret", "tp"),
        [(r * count + i, (1 - r) * count + (i + by) % count) for r in range(2) for i in range(count)],
    )


def near(keep, give):
    return turn(keep, "tp", 1), cross(give, -1), turn(keep, "tp", -1), cross(give, 1), cross(give, 0)


def far(keep_right, got_left):
    return turn(keep_right, "tp", 1), turn(got_left, "tp", -1)


def exchange(x, axis):
    return lax.all_to_all(x, axis, split_axis=0, concat_axis=0, tiled=True)


def added(x):
    return jnp.sum(x.astype(F32), axis=0).astype(BF16)


def body(queries, d_attn, pool, w_key, w_value, owners, picks, live_counts):
    y_count = lax.axis_size("y")
    z_count = lax.axis_size("z")
    ctx_count = y_count * z_count
    width = pool.shape[2]
    part = NBR_LEN // lax.axis_size("tp") // CHUNKS
    low = lax.axis_index("ret") == 0
    owner_col = jnp.where(low, owners[:, 0], owners[:, 1])
    pick_col = jnp.where(low, picks[:, 0], picks[:, 1])
    asked = jnp.sum(
        jnp.where(owner_col == ctx_index(), pick_col, 0).reshape(ctx_count, CH_DEV), axis=1
    )
    pool_blocks = pool[0].reshape(-1, NBR_LEN, width)

    first = pack(0, asked, live_counts, pool_blocks, part)
    second = pack(1, asked, live_counts, pool_blocks, part)
    incoming = exchange(first, ("y", "z"))
    held = hold(queries, d_attn, w_key, w_value)
    second, incoming, held = lax.optimization_barrier((second, incoming, held))
    late = exchange(second, ("y", "z"))
    keep, give = pick(owner_col, incoming)
    sides = near(keep, give)
    late, *shards = lax.optimization_barrier((late, keep, *sides, *far(*sides[:2])))
    first_rows = project(shards, *held[2:], "project_first")
    keep, give = pick(owner_col, late)
    keep_right, got_left, *sides = near(keep, give)
    keep_right, got_left, first_rows = lax.optimization_barrier((keep_right, got_left, first_rows))
    ends = far(keep_right, got_left)
    near_rows = project((keep, keep_right, got_left, *sides), *held[2:], "project_near")
    tokens, other, rows, grads = attend(ends, *held, *first_rows, *near_rows)
    pair = (own_sum(first_rows[0], rows, grads) + swap(other).astype(F32)).astype(BF16)
    by_y = added(exchange(pair, "y"))
    attn_out, d_queries = join(tokens, swap(tokens))
    by_z = added(exchange(by_y.reshape(z_count, width // z_count, HEAD_DIM), "z"))
    by_z, attn_out, d_queries = lax.optimization_barrier((by_z, attn_out, d_queries))
    by_z = jnp.broadcast_to(by_z[None], (z_count,) + by_z.shape)
    z_full = exchange(by_z, "z").reshape(width, HEAD_DIM)
    hops = (0, 1, y_count - 1) + tuple(range(2, y_count - 1))
    pieces = [turn(z_full, "y", hop) if hop else z_full for hop in hops]
    d_w_key, d_w_value = lay(hops, pieces, [swap(x) for x in pieces])
    return (attn_out, d_queries, d_w_key, d_w_value)


def solution(mesh):
    shape = (Y_CHIPS, mesh.shape["ctx"] // Y_CHIPS, mesh.shape["ret"], mesh.shape["tp"])
    fine = Mesh(mesh.devices.reshape(shape), ("y", "z", "ret", "tp"))
    ctx = ("y", "z")
    return jax.shard_map(
        body,
        mesh=fine,
        in_specs=(
            P(ctx, "tp"),
            P(ctx, "tp"),
            P("ret", ctx, None),
            P(None, "tp"),
            P(None, "tp"),
            P(),
            P(),
            P(),
        ),
        out_specs=(P(ctx, "tp"), P(ctx, "tp"), P(None, "tp"), P(None, "tp")),
        check_vma=False,
    )
```

```python
import functools
import math

import jax
import jax.numpy as jnp
from jax import lax
from jax.experimental import pallas as pl
from jax.experimental.pallas import tpu as pltpu
from jax.sharding import Mesh
from jax.sharding import PartitionSpec as P

HEAD_DIM = 128
SPAN = 64
NBR_LEN = 128
CH_DEV = 16
Y_CHIPS = 4
Z_PAIR = 2
CTX = ("y", "zh", "zl")


CHUNKS = 2
TOGETHER = 2

BF16 = jnp.bfloat16
F32 = jnp.float32
ANY = pl.BlockSpec(memory_space=pl.ANY)
SMEM = pl.BlockSpec(memory_space=pltpu.SMEM)
WHOLE = pl.BlockSpec(memory_space=pltpu.VMEM)


def ctx_index():
    z = lax.axis_index("zh") * lax.axis_size("zl") + lax.axis_index("zl")
    return lax.axis_index("y") * (lax.axis_size("zh") * lax.axis_size("zl")) + z


def pack_kernel(row, asked, live_counts, pool, out, held, in_sem, out_sem):
    part = held.shape[1]
    chunk = lax.axis_index("tp") * CHUNKS + row
    start = pl.multiple_of(chunk * part, part)
    load = pltpu.make_async_copy(pool.at[:, pl.ds(start, part), :], held, in_sem)
    load.start()
    live = live_counts[lax.axis_index("ret"), ctx_index()]
    slots = [lax.rem(asked[d], live) for d in range(out.shape[0])]
    copies = [
        pltpu.make_async_copy(held.at[slots[d]], out.at[d], out_sem.at[d])
        for d in range(out.shape[0])
    ]
    load.wait()
    for copy in copies:
        copy.start()
    for copy in copies:
        copy.wait()


def pack(row, asked, live_counts, pool_blocks, part):
    blocks, _, width = pool_blocks.shape
    count = asked.shape[0]
    return pl.pallas_call(
        functools.partial(pack_kernel, row),
        out_shape=jax.ShapeDtypeStruct((count, part, width), BF16),
        in_specs=[SMEM, SMEM, ANY],
        out_specs=ANY,
        scratch_shapes=[
            pltpu.VMEM((blocks, part, width), BF16),
            pltpu.SemaphoreType.DMA,
            pltpu.SemaphoreType.DMA((count,)),
        ],
        compiler_params=pltpu.CompilerParams(vmem_limit_bytes=60 << 20),
        name=f"pack{row}",
    )(asked, live_counts, pool_blocks)


def pick_kernel(owner_col, incoming, keep, give):
    half = keep.shape[0]
    me = lax.axis_index("ret")
    first = ctx_index() * (2 * half)
    for k in range(half):
        keep[k] = incoming[owner_col[first + me * half + k]]
        give[k] = incoming[owner_col[first + (1 - me) * half + k]]


def pick(owner_col, incoming):
    half = jax.ShapeDtypeStruct((CH_DEV // 2,) + incoming.shape[1:], BF16)
    return pl.pallas_call(
        pick_kernel,
        out_shape=(half, half),
        in_specs=[SMEM, WHOLE],
        out_specs=(WHOLE, WHOLE),
        compiler_params=pltpu.CompilerParams(vmem_limit_bytes=8 << 20),
        name="pick",
    )(owner_col, incoming)


def dot(a, b, dims=((1,), (0,))):
    return lax.dot_general(a, b, (dims, ((), ())), preferred_element_type=F32)


ROWS = ((1,), (1,))
DOWN = ((0,), (0,))


def two_heads(x):
    col = lax.broadcasted_iota(jnp.int32, x.shape, 1)
    zero = jnp.zeros_like(x)
    return jnp.concatenate(
        [jnp.where(col < HEAD_DIM, x, zero), jnp.where(col < HEAD_DIM, zero, x)], axis=0
    )


def own_heads(x):
    return jnp.concatenate([x[:SPAN, :HEAD_DIM], x[SPAN:, HEAD_DIM:]], axis=1)


def gather_rows(shards, rows, j):
    part = shards[0].shape[1]
    for p, shard in enumerate(shards):
        rows[j, p * part : (p + 1) * part, :] = shard[j]


def hold_kernel(queries, d_attn, w_key, w_value, q_out, g_out, k_out, v_out, sem):
    tokens = q_out.shape[0]
    place = pl.ds(pl.multiple_of(lax.axis_index("ret") * tokens, tokens), tokens)
    loads = [
        pltpu.make_async_copy(queries.at[place, :], q_out, sem.at[0]),
        pltpu.make_async_copy(d_attn.at[place, :], g_out, sem.at[1]),
        pltpu.make_async_copy(w_key, k_out, sem.at[2]),
        pltpu.make_async_copy(w_value, v_out, sem.at[3]),
    ]
    for load in loads:
        load.start()
    for load in loads:
        load.wait()


def hold(queries, d_attn, w_key, w_value):
    half = jax.ShapeDtypeStruct((queries.shape[0] // 2, queries.shape[1]), BF16)
    weight = jax.ShapeDtypeStruct(w_key.shape, BF16)
    return pl.pallas_call(
        hold_kernel,
        out_shape=(half, half, weight, weight),
        in_specs=[ANY] * 4,
        out_specs=(WHOLE,) * 4,
        scratch_shapes=[pltpu.SemaphoreType.DMA((4,))],
        compiler_params=pltpu.CompilerParams(vmem_limit_bytes=60 << 20),
        cost_estimate=pl.CostEstimate(flops=0, bytes_accessed=6 << 20, transcendentals=0),
        name="hold",
    )(queries, d_attn, w_key, w_value)


def project_kernel(count, *refs):
    shards = refs[:count]
    w_key, w_value, rows, pairs = refs[count:]
    spans, held, head_cols = pairs.shape
    head_cols //= 2
    for j in range(spans):
        gather_rows(shards, rows, j)
    flat = rows[...].reshape(spans * held, rows.shape[2])
    for side, weight in enumerate((w_key, w_value)):
        made = dot(flat, weight[...]).astype(BF16).reshape(spans, held, head_cols)
        pairs[:, :, side * head_cols : (side + 1) * head_cols] = made


def project(shards, w_key, w_value, name):
    spans, part, width = shards[0].shape
    head_cols = w_key.shape[1]
    count = len(shards) * part
    return pl.pallas_call(
        functools.partial(project_kernel, len(shards)),
        out_shape=(
            jax.ShapeDtypeStruct((spans, count, width), BF16),
            jax.ShapeDtypeStruct((spans, count, 2 * head_cols), BF16),
        ),
        in_specs=[WHOLE] * (len(shards) + 2),
        out_specs=(WHOLE,) * 2,
        compiler_params=pltpu.CompilerParams(vmem_limit_bytes=12 << 20),
        cost_estimate=pl.CostEstimate(
            flops=4 * spans * count * width * head_cols, bytes_accessed=4 << 20, transcendentals=0
        ),
        name=name,
    )(*shards, w_key, w_value)


def weight_sum(rows_a, rows_b, grads, side):
    head_cols = grads.shape[2] // 2
    cut = pl.ds(pl.multiple_of(side * head_cols, head_cols), head_cols)
    total = None
    for at, rows in enumerate((rows_a, rows_b)):
        flat = rows[...].reshape(-1, rows.shape[2])
        term = dot(flat, grads[at, :, cut], DOWN)
        total = term if total is None else total + term
    return total * (1.0 / (CH_DEV * 32))


def attend_kernel(count, *refs):
    shards = refs[:count]
    queries, d_attn, w_key, w_value, rows_a, pairs_a, rows_m, pairs_m = refs[count : count + 8]
    tokens_out, other, rows_b, grads, far_rows = refs[count + 8 :]
    spans, near_rows, width = rows_a.shape
    far_count = far_rows.shape[1]
    head_cols = w_key.shape[1]
    heads = head_cols // HEAD_DIM
    scale = 1.0 / math.sqrt(HEAD_DIM)
    raise_by = scale / math.log(2.0)
    for j in range(spans):
        gather_rows(shards, far_rows, j)
        rows_b[j, : near_rows - far_count, :] = rows_m[j]
        rows_b[j, near_rows - far_count :, :] = far_rows[j]
    far_flat = far_rows[...].reshape(spans * far_count, width)
    far_keys = dot(far_flat, w_key[...]).astype(BF16)
    far_values = dot(far_flat, w_value[...]).astype(BF16)
    for start in range(0, spans, TOGETHER):
        units = []
        for j in range(start, start + TOGETHER):
            units += [
                (
                    j,
                    slice(h * HEAD_DIM, (h + 2) * HEAD_DIM),
                    slice(head_cols + h * HEAD_DIM, head_cols + (h + 2) * HEAD_DIM),
                    slice(j * SPAN, (j + 1) * SPAN),
                    slice(j * near_rows, (j + 1) * near_rows),
                )
                for h in range(0, heads, 2)
            ]

        def made(far, j, cut, side_cut):
            late = far[j * far_count : (j + 1) * far_count, cut]
            return jnp.concatenate([pairs_a[j, :, side_cut], pairs_m[j, :, side_cut], late], axis=0)

        keys = [made(far_keys, j, cut, cut) for j, cut, _, _, _ in units]
        values = [made(far_values, j, cut, past) for j, cut, past, _, _ in units]
        qs = [two_heads(queries[at, cut]) for _, cut, _, at, _ in units]
        gs = [two_heads(d_attn[at, cut]) for _, cut, _, at, _ in units]
        scores = [dot(k, q, ROWS) for k, q in zip(keys, qs)]
        grad_probs = [dot(v, g, ROWS) for v, g in zip(values, gs)]
        tops = [jnp.max(x, axis=0, keepdims=True) for x in scores]
        raised = [jnp.exp2((x - top) * raise_by) for x, top in zip(scores, tops)]
        probs = [x * (1.0 / jnp.sum(x, axis=0, keepdims=True)) for x in raised]
        probs_b = [x.astype(BF16) for x in probs]
        out_dots = [jnp.sum(p * g, axis=0, keepdims=True) for p, g in zip(probs, grad_probs)]
        dscores = [
            (p * ((g - o) * scale)).astype(BF16) for p, g, o in zip(probs, grad_probs, out_dots)
        ]
        for i, (_, cut, past, at, to) in enumerate(units):
            k_grad = dot(dscores[i], qs[i]).astype(BF16)
            v_grad = dot(probs_b[i], gs[i]).astype(BF16)
            for side in range(2):
                part = slice(side * near_rows, (side + 1) * near_rows)
                grads[side, to, cut] = k_grad[part]
                grads[side, to, past] = v_grad[part]
            tokens_out[0, at, cut] = own_heads(dot(probs_b[i], values[i], DOWN)).astype(BF16)
            tokens_out[1, at, cut] = own_heads(dot(dscores[i], keys[i], DOWN)).astype(BF16)
    sums = weight_sum(rows_a, rows_b, grads, 1 - lax.axis_index("ret"))
    for h in range(heads):
        other[h] = sums[:, h * HEAD_DIM : (h + 1) * HEAD_DIM].astype(other.dtype)


def attend(shards, queries, d_attn, w_key, w_value, rows_a, pairs_a, rows_m, pairs_m):
    spans, near_rows, width = rows_a.shape
    nbr_rows = 2 * NBR_LEN
    head_cols = w_key.shape[1]
    heads = head_cols // HEAD_DIM
    tokens = spans * SPAN
    flops = 2 * spans * nbr_rows * head_cols * (2 * width + 12 * SPAN)
    return pl.pallas_call(
        functools.partial(attend_kernel, len(shards)),
        out_shape=(
            jax.ShapeDtypeStruct((2, tokens, head_cols), BF16),
            jax.ShapeDtypeStruct((heads, width, HEAD_DIM), BF16),
            jax.ShapeDtypeStruct((spans, near_rows, width), BF16),
            jax.ShapeDtypeStruct((2, spans * near_rows, 2 * head_cols), BF16),
        ),
        in_specs=[WHOLE] * (len(shards) + 8),
        out_specs=(WHOLE,) * 4,
        scratch_shapes=[pltpu.VMEM((spans, near_rows - rows_m.shape[1], width), BF16)],
        compiler_params=pltpu.CompilerParams(vmem_limit_bytes=16 << 20),
        cost_estimate=pl.CostEstimate(
            flops=flops, bytes_accessed=10 << 20, transcendentals=spans * SPAN * nbr_rows * heads
        ),
        name="attend",
    )(*shards, queries, d_attn, w_key, w_value, rows_a, pairs_a, rows_m, pairs_m)


def own_sum_kernel(rows_a, rows_b, grads, mine):
    sums = weight_sum(rows_a, rows_b, grads, lax.axis_index("ret"))
    for h in range(mine.shape[0]):
        mine[h] = sums[:, h * HEAD_DIM : (h + 1) * HEAD_DIM]


def own_sum(rows_a, rows_b, grads):
    width = rows_a.shape[2]
    heads = grads.shape[2] // 2 // HEAD_DIM
    return pl.pallas_call(
        own_sum_kernel,
        out_shape=jax.ShapeDtypeStruct((heads, width, HEAD_DIM), F32),
        in_specs=[WHOLE] * 3,
        out_specs=WHOLE,
        compiler_params=pltpu.CompilerParams(vmem_limit_bytes=16 << 20),
        cost_estimate=pl.CostEstimate(
            flops=4 * grads.shape[1] * width * heads * HEAD_DIM,
            bytes_accessed=4 << 20,
            transcendentals=0,
        ),
        name="own_sum",
    )(rows_a, rows_b, grads)


def join_kernel(mine, other, attn_out, d_queries, sem):
    me = lax.axis_index("ret")
    tokens = mine.shape[1]
    copies = []
    for side, held in ((me, mine), (1 - me, other)):
        place = pl.ds(pl.multiple_of(side * tokens, tokens), tokens)
        for which, out in enumerate((attn_out, d_queries)):
            copies.append(
                pltpu.make_async_copy(held.at[which], out.at[place, :], sem.at[len(copies)])
            )
    for copy in copies:
        copy.start()
    for copy in copies:
        copy.wait()


def join(mine, other):
    out = jax.ShapeDtypeStruct((2 * mine.shape[1], mine.shape[2]), BF16)
    return pl.pallas_call(
        join_kernel,
        out_shape=(out, out),
        in_specs=[ANY] * 2,
        out_specs=(ANY, ANY),
        scratch_shapes=[pltpu.SemaphoreType.DMA((4,))],
        compiler_params=pltpu.CompilerParams(vmem_limit_bytes=4 << 20),
        name="join",
    )(mine, other)


def lay_kernel(spots, *refs):
    mine, other = refs[: len(spots)], refs[len(spots) : -2]
    d_w_key, d_w_value = refs[-2:]
    low = lax.axis_index("ret") == 0
    count = lax.axis_size("y")
    for (hop, first), x, y in zip(spots, mine, other):
        h = lax.rem(lax.axis_index("y") + (count - hop), count)
        cut = pl.ds(pl.multiple_of(h * HEAD_DIM, HEAD_DIM), HEAD_DIM)
        rows = slice(first, first + x.shape[0])
        d_w_key[rows, cut] = jnp.where(low, x[...], y[...])
        d_w_value[rows, cut] = jnp.where(low, y[...], x[...])


def lay(spots, mine, other):
    width, cols = mine[0].shape
    out = jax.ShapeDtypeStruct((width, Y_CHIPS * cols), BF16)
    return pl.pallas_call(
        functools.partial(lay_kernel, spots),
        out_shape=(out, out),
        in_specs=[WHOLE] * (2 * len(spots)),
        out_specs=(WHOLE, WHOLE),
        compiler_params=pltpu.CompilerParams(vmem_limit_bytes=12 << 20),
        name="lay",
    )(*mine, *other)


def turn(x, axis, by):
    count = lax.axis_size(axis)
    return lax.ppermute(x, axis, [(i, (i + by) % count) for i in range(count)])


def swap(x):
    return turn(x, "ret", 1)


def cross(x, by):
    count = lax.axis_size("tp")
    return lax.ppermute(
        x,
        ("ret", "tp"),
        [(r * count + i, (1 - r) * count + (i + by) % count) for r in range(2) for i in range(count)],
    )


def near(keep, give):
    return turn(keep, "tp", 1), cross(give, -1), turn(keep, "tp", -1), cross(give, 1), cross(give, 0)


def far(keep_right, got_left):
    return turn(keep_right, "tp", 1), turn(got_left, "tp", -1)


def exchange(x, axis):
    return lax.all_to_all(x, axis, split_axis=0, concat_axis=0, tiled=True)


def added(x):
    return jnp.sum(x.astype(F32), axis=0).astype(BF16)


def body(queries, d_attn, pool, w_key, w_value, owners, picks, live_counts):
    y_count = lax.axis_size("y")
    z_high = lax.axis_size("zh")
    z_low = lax.axis_size("zl")
    ctx_count = y_count * z_high * z_low
    width = pool.shape[2]
    part = NBR_LEN // lax.axis_size("tp") // CHUNKS
    low = lax.axis_index("ret") == 0
    owner_col = jnp.where(low, owners[:, 0], owners[:, 1])
    pick_col = jnp.where(low, picks[:, 0], picks[:, 1])
    asked = jnp.sum(
        jnp.where(owner_col == ctx_index(), pick_col, 0).reshape(ctx_count, CH_DEV), axis=1
    )
    pool_blocks = pool[0].reshape(-1, NBR_LEN, width)

    first = pack(0, asked, live_counts, pool_blocks, part)
    second = pack(1, asked, live_counts, pool_blocks, part)
    incoming = exchange(first, CTX)
    held = hold(queries, d_attn, w_key, w_value)
    second, incoming, held = lax.optimization_barrier((second, incoming, held))
    late = exchange(second, CTX)
    keep, give = pick(owner_col, incoming)
    sides = near(keep, give)
    late, *shards = lax.optimization_barrier((late, keep, *sides, *far(*sides[:2])))
    first_rows = project(shards, *held[2:], "project_first")
    keep, give = pick(owner_col, late)
    keep_right, got_left, *sides = near(keep, give)
    ends = far(keep_right, got_left)
    near_rows = project((keep, keep_right, got_left, *sides), *held[2:], "project_near")
    tokens, other, rows, grads = attend(ends, *held, *first_rows, *near_rows)
    pair = (own_sum(first_rows[0], rows, grads) + swap(other).astype(F32)).astype(BF16)
    half = width // z_low
    by_y = added(exchange(pair.reshape(y_count * z_low, half, HEAD_DIM), ("y", "zl")))
    attn_out, d_queries = join(tokens, swap(tokens))
    by_z = added(exchange(by_y.reshape(z_high, half // z_high, HEAD_DIM), "zh"))
    by_z, attn_out, d_queries = lax.optimization_barrier((by_z, attn_out, d_queries))
    by_z = jnp.broadcast_to(by_z[None], (z_low * z_high,) + by_z.shape)
    z_full = exchange(by_z, ("zl", "zh")).reshape(width, HEAD_DIM)
    right, left = turn(z_full, "y", 1), turn(z_full, "y", -1)
    pieces = [z_full, right, left, turn(right[:half], "y", 1), turn(left[half:], "y", -1)]
    spots = ((0, 0), (1, 0), (3, 0), (2, 0), (2, half))
    d_w_key, d_w_value = lay(spots, pieces, [swap(x) for x in pieces])
    return (attn_out, d_queries, d_w_key, d_w_value)


def solution(mesh):
    z_high = mesh.shape["ctx"] // (Y_CHIPS * Z_PAIR)
    shape = (Y_CHIPS, z_high, Z_PAIR, mesh.shape["ret"], mesh.shape["tp"])
    fine = Mesh(mesh.devices.reshape(shape), CTX + ("ret", "tp"))
    ctx = CTX
    return jax.shard_map(
        body,
        mesh=fine,
        in_specs=(
            P(ctx, "tp"),
            P(ctx, "tp"),
            P("ret", ctx, None),
            P(None, "tp"),
            P(None, "tp"),
            P(),
            P(),
            P(),
        ),
        out_specs=(P(ctx, "tp"), P(ctx, "tp"), P(None, "tp"), P(None, "tp")),
        check_vma=False,
    )
```

```python
import functools
import math

import jax
import jax.numpy as jnp
from jax import lax
from jax.experimental import pallas as pl
from jax.experimental.pallas import tpu as pltpu
from jax.sharding import Mesh
from jax.sharding import PartitionSpec as P

HEAD_DIM = 128
SPAN = 64
NBR_LEN = 128
CH_DEV = 16
Y_CHIPS = 4
Z_PAIR = 2
CTX = ("y", "zh", "zl")


CHUNKS = 2
TOGETHER = 2

BF16 = jnp.bfloat16
F32 = jnp.float32
ANY = pl.BlockSpec(memory_space=pl.ANY)
SMEM = pl.BlockSpec(memory_space=pltpu.SMEM)
WHOLE = pl.BlockSpec(memory_space=pltpu.VMEM)


def ctx_index():
    z = lax.axis_index("zh") * lax.axis_size("zl") + lax.axis_index("zl")
    return lax.axis_index("y") * (lax.axis_size("zh") * lax.axis_size("zl")) + z


def pack_kernel(row, asked, live_counts, pool, out, held, in_sem, out_sem):
    part = held.shape[1]
    chunk = lax.axis_index("tp") * CHUNKS + row
    start = pl.multiple_of(chunk * part, part)
    load = pltpu.make_async_copy(pool.at[:, pl.ds(start, part), :], held, in_sem)
    load.start()
    live = live_counts[lax.axis_index("ret"), ctx_index()]
    slots = [lax.rem(asked[d], live) for d in range(out.shape[0])]
    copies = [
        pltpu.make_async_copy(held.at[slots[d]], out.at[d], out_sem.at[d])
        for d in range(out.shape[0])
    ]
    load.wait()
    for copy in copies:
        copy.start()
    for copy in copies:
        copy.wait()


def pack(row, asked, live_counts, pool_blocks, part):
    blocks, _, width = pool_blocks.shape
    count = asked.shape[0]
    return pl.pallas_call(
        functools.partial(pack_kernel, row),
        out_shape=jax.ShapeDtypeStruct((count, part, width), BF16),
        in_specs=[SMEM, SMEM, ANY],
        out_specs=ANY,
        scratch_shapes=[
            pltpu.VMEM((blocks, part, width), BF16),
            pltpu.SemaphoreType.DMA,
            pltpu.SemaphoreType.DMA((count,)),
        ],
        compiler_params=pltpu.CompilerParams(vmem_limit_bytes=60 << 20),
        name=f"pack{row}",
    )(asked, live_counts, pool_blocks)


def pick_kernel(owner_col, incoming, keep, give):
    half = keep.shape[0]
    me = lax.axis_index("ret")
    first = ctx_index() * (2 * half)
    for k in range(half):
        keep[k] = incoming[owner_col[first + me * half + k]]
        give[k] = incoming[owner_col[first + (1 - me) * half + k]]


def pick(owner_col, incoming):
    half = jax.ShapeDtypeStruct((CH_DEV // 2,) + incoming.shape[1:], BF16)
    return pl.pallas_call(
        pick_kernel,
        out_shape=(half, half),
        in_specs=[SMEM, WHOLE],
        out_specs=(WHOLE, WHOLE),
        compiler_params=pltpu.CompilerParams(vmem_limit_bytes=8 << 20),
        name="pick",
    )(owner_col, incoming)


def dot(a, b, dims=((1,), (0,))):
    return lax.dot_general(a, b, (dims, ((), ())), preferred_element_type=F32)


ROWS = ((1,), (1,))
DOWN = ((0,), (0,))


def two_heads(x):
    col = lax.broadcasted_iota(jnp.int32, x.shape, 1)
    zero = jnp.zeros_like(x)
    return jnp.concatenate(
        [jnp.where(col < HEAD_DIM, x, zero), jnp.where(col < HEAD_DIM, zero, x)], axis=0
    )


def own_heads(x):
    return jnp.concatenate([x[:SPAN, :HEAD_DIM], x[SPAN:, HEAD_DIM:]], axis=1)


def gather_rows(shards, rows, j):
    part = shards[0].shape[1]
    for p, shard in enumerate(shards):
        rows[j, p * part : (p + 1) * part, :] = shard[j]


def hold_kernel(queries, d_attn, w_key, w_value, q_out, g_out, k_out, v_out, sem):
    tokens = q_out.shape[0]
    place = pl.ds(pl.multiple_of(lax.axis_index("ret") * tokens, tokens), tokens)
    loads = [
        pltpu.make_async_copy(queries.at[place, :], q_out, sem.at[0]),
        pltpu.make_async_copy(d_attn.at[place, :], g_out, sem.at[1]),
        pltpu.make_async_copy(w_key, k_out, sem.at[2]),
        pltpu.make_async_copy(w_value, v_out, sem.at[3]),
    ]
    for load in loads:
        load.start()
    for load in loads:
        load.wait()


def hold(queries, d_attn, w_key, w_value):
    half = jax.ShapeDtypeStruct((queries.shape[0] // 2, queries.shape[1]), BF16)
    weight = jax.ShapeDtypeStruct(w_key.shape, BF16)
    return pl.pallas_call(
        hold_kernel,
        out_shape=(half, half, weight, weight),
        in_specs=[ANY] * 4,
        out_specs=(WHOLE,) * 4,
        scratch_shapes=[pltpu.SemaphoreType.DMA((4,))],
        compiler_params=pltpu.CompilerParams(vmem_limit_bytes=60 << 20),
        cost_estimate=pl.CostEstimate(flops=0, bytes_accessed=6 << 20, transcendentals=0),
        name="hold",
    )(queries, d_attn, w_key, w_value)


def project_kernel(count, *refs):
    shards = refs[:count]
    w_key, w_value, rows, pairs = refs[count:]
    spans, held, head_cols = pairs.shape
    head_cols //= 2
    for j in range(spans):
        gather_rows(shards, rows, j)
    flat = rows[...].reshape(spans * held, rows.shape[2])
    for side, weight in enumerate((w_key, w_value)):
        made = dot(flat, weight[...]).astype(BF16).reshape(spans, held, head_cols)
        pairs[:, :, side * head_cols : (side + 1) * head_cols] = made


def project(shards, w_key, w_value, name):
    spans, part, width = shards[0].shape
    head_cols = w_key.shape[1]
    count = len(shards) * part
    return pl.pallas_call(
        functools.partial(project_kernel, len(shards)),
        out_shape=(
            jax.ShapeDtypeStruct((spans, count, width), BF16),
            jax.ShapeDtypeStruct((spans, count, 2 * head_cols), BF16),
        ),
        in_specs=[WHOLE] * (len(shards) + 2),
        out_specs=(WHOLE,) * 2,
        compiler_params=pltpu.CompilerParams(vmem_limit_bytes=12 << 20),
        cost_estimate=pl.CostEstimate(
            flops=4 * spans * count * width * head_cols, bytes_accessed=4 << 20, transcendentals=0
        ),
        name=name,
    )(*shards, w_key, w_value)


def weight_sum(rows_a, rows_b, grads, side):
    head_cols = grads.shape[2] // 2
    cut = pl.ds(pl.multiple_of(side * head_cols, head_cols), head_cols)
    total = None
    for at, rows in enumerate((rows_a, rows_b)):
        flat = rows[...].reshape(-1, rows.shape[2])
        term = dot(flat, grads[at, :, cut], DOWN)
        total = term if total is None else total + term
    return total * (1.0 / (CH_DEV * 32))


def attend_kernel(count, *refs):
    shards = refs[:count]
    queries, d_attn, w_key, w_value, rows_a, pairs_a, rows_m, pairs_m = refs[count : count + 8]
    tokens_out, other, rows_b, grads, far_rows = refs[count + 8 :]
    spans, near_rows, width = rows_a.shape
    far_count = far_rows.shape[1]
    head_cols = w_key.shape[1]
    heads = head_cols // HEAD_DIM
    scale = 1.0 / math.sqrt(HEAD_DIM)
    raise_by = scale / math.log(2.0)
    for j in range(spans):
        gather_rows(shards, far_rows, j)
        rows_b[j, : near_rows - far_count, :] = rows_m[j]
        rows_b[j, near_rows - far_count :, :] = far_rows[j]
    far_flat = far_rows[...].reshape(spans * far_count, width)
    far_keys = dot(far_flat, w_key[...]).astype(BF16)
    far_values = dot(far_flat, w_value[...]).astype(BF16)
    for start in range(0, spans, TOGETHER):
        units = []
        for j in range(start, start + TOGETHER):
            units += [
                (
                    j,
                    slice(h * HEAD_DIM, (h + 2) * HEAD_DIM),
                    slice(head_cols + h * HEAD_DIM, head_cols + (h + 2) * HEAD_DIM),
                    slice(j * SPAN, (j + 1) * SPAN),
                    slice(j * near_rows, (j + 1) * near_rows),
                )
                for h in range(0, heads, 2)
            ]

        def made(far, j, cut, side_cut):
            late = far[j * far_count : (j + 1) * far_count, cut]
            return jnp.concatenate([pairs_a[j, :, side_cut], pairs_m[j, :, side_cut], late], axis=0)

        keys = [made(far_keys, j, cut, cut) for j, cut, _, _, _ in units]
        values = [made(far_values, j, cut, past) for j, cut, past, _, _ in units]
        qs = [two_heads(queries[at, cut]) for _, cut, _, at, _ in units]
        gs = [two_heads(d_attn[at, cut]) for _, cut, _, at, _ in units]
        scores = [dot(k, q, ROWS) for k, q in zip(keys, qs)]
        grad_probs = [dot(v, g, ROWS) for v, g in zip(values, gs)]
        tops = [jnp.max(x, axis=0, keepdims=True) for x in scores]
        raised = [jnp.exp2((x - top) * raise_by) for x, top in zip(scores, tops)]
        probs = [x * (1.0 / jnp.sum(x, axis=0, keepdims=True)) for x in raised]
        probs_b = [x.astype(BF16) for x in probs]
        out_dots = [jnp.sum(p * g, axis=0, keepdims=True) for p, g in zip(probs, grad_probs)]
        dscores = [
            (p * ((g - o) * scale)).astype(BF16) for p, g, o in zip(probs, grad_probs, out_dots)
        ]
        for i, (_, cut, past, at, to) in enumerate(units):
            k_grad = dot(dscores[i], qs[i]).astype(BF16)
            v_grad = dot(probs_b[i], gs[i]).astype(BF16)
            for side in range(2):
                part = slice(side * near_rows, (side + 1) * near_rows)
                grads[side, to, cut] = k_grad[part]
                grads[side, to, past] = v_grad[part]
            tokens_out[0, at, cut] = own_heads(dot(probs_b[i], values[i], DOWN)).astype(BF16)
            tokens_out[1, at, cut] = own_heads(dot(dscores[i], keys[i], DOWN)).astype(BF16)
    sums = weight_sum(rows_a, rows_b, grads, 1 - lax.axis_index("ret"))
    for h in range(heads):
        other[h] = sums[:, h * HEAD_DIM : (h + 1) * HEAD_DIM].astype(other.dtype)


def attend(shards, queries, d_attn, w_key, w_value, rows_a, pairs_a, rows_m, pairs_m):
    spans, near_rows, width = rows_a.shape
    nbr_rows = 2 * NBR_LEN
    head_cols = w_key.shape[1]
    heads = head_cols // HEAD_DIM
    tokens = spans * SPAN
    flops = 2 * spans * nbr_rows * head_cols * (2 * width + 12 * SPAN)
    return pl.pallas_call(
        functools.partial(attend_kernel, len(shards)),
        out_shape=(
            jax.ShapeDtypeStruct((2, tokens, head_cols), BF16),
            jax.ShapeDtypeStruct((heads, width, HEAD_DIM), BF16),
            jax.ShapeDtypeStruct((spans, near_rows, width), BF16),
            jax.ShapeDtypeStruct((2, spans * near_rows, 2 * head_cols), BF16),
        ),
        in_specs=[WHOLE] * (len(shards) + 8),
        out_specs=(WHOLE,) * 4,
        scratch_shapes=[pltpu.VMEM((spans, near_rows - rows_m.shape[1], width), BF16)],
        compiler_params=pltpu.CompilerParams(vmem_limit_bytes=16 << 20),
        cost_estimate=pl.CostEstimate(
            flops=flops, bytes_accessed=10 << 20, transcendentals=spans * SPAN * nbr_rows * heads
        ),
        name="attend",
    )(*shards, queries, d_attn, w_key, w_value, rows_a, pairs_a, rows_m, pairs_m)


def own_sum_kernel(rows_a, rows_b, grads, mine):
    sums = weight_sum(rows_a, rows_b, grads, lax.axis_index("ret"))
    for h in range(mine.shape[0]):
        mine[h] = sums[:, h * HEAD_DIM : (h + 1) * HEAD_DIM]


def own_sum(rows_a, rows_b, grads):
    width = rows_a.shape[2]
    heads = grads.shape[2] // 2 // HEAD_DIM
    return pl.pallas_call(
        own_sum_kernel,
        out_shape=jax.ShapeDtypeStruct((heads, width, HEAD_DIM), F32),
        in_specs=[WHOLE] * 3,
        out_specs=WHOLE,
        compiler_params=pltpu.CompilerParams(vmem_limit_bytes=16 << 20),
        cost_estimate=pl.CostEstimate(
            flops=4 * grads.shape[1] * width * heads * HEAD_DIM,
            bytes_accessed=4 << 20,
            transcendentals=0,
        ),
        name="own_sum",
    )(rows_a, rows_b, grads)


def join_kernel(mine, other, attn_out, d_queries, sem):
    me = lax.axis_index("ret")
    tokens = mine.shape[1]
    copies = []
    for side, held in ((me, mine), (1 - me, other)):
        place = pl.ds(pl.multiple_of(side * tokens, tokens), tokens)
        for which, out in enumerate((attn_out, d_queries)):
            copies.append(
                pltpu.make_async_copy(held.at[which], out.at[place, :], sem.at[len(copies)])
            )
    for copy in copies:
        copy.start()
    for copy in copies:
        copy.wait()


def join(mine, other):
    out = jax.ShapeDtypeStruct((2 * mine.shape[1], mine.shape[2]), BF16)
    return pl.pallas_call(
        join_kernel,
        out_shape=(out, out),
        in_specs=[ANY] * 2,
        out_specs=(ANY, ANY),
        scratch_shapes=[pltpu.SemaphoreType.DMA((4,))],
        compiler_params=pltpu.CompilerParams(vmem_limit_bytes=4 << 20),
        name="join",
    )(mine, other)


def lay_kernel(spots, *refs):
    mine, other = refs[: len(spots)], refs[len(spots) : -2]
    d_w_key, d_w_value = refs[-2:]
    low = lax.axis_index("ret") == 0
    count = lax.axis_size("y")
    for (hop, first), x, y in zip(spots, mine, other):
        h = lax.rem(lax.axis_index("y") + (count - hop), count)
        cut = pl.ds(pl.multiple_of(h * HEAD_DIM, HEAD_DIM), HEAD_DIM)
        rows = slice(first, first + x.shape[0])
        d_w_key[rows, cut] = jnp.where(low, x[...], y[...])
        d_w_value[rows, cut] = jnp.where(low, y[...], x[...])


def lay(spots, mine, other):
    width, cols = mine[0].shape
    out = jax.ShapeDtypeStruct((width, Y_CHIPS * cols), BF16)
    return pl.pallas_call(
        functools.partial(lay_kernel, spots),
        out_shape=(out, out),
        in_specs=[WHOLE] * (2 * len(spots)),
        out_specs=(WHOLE, WHOLE),
        compiler_params=pltpu.CompilerParams(vmem_limit_bytes=12 << 20),
        name="lay",
    )(*mine, *other)


def turn(x, axis, by):
    count = lax.axis_size(axis)
    return lax.ppermute(x, axis, [(i, (i + by) % count) for i in range(count)])


def swap(x):
    return turn(x, "ret", 1)


def cross(x, by):
    count = lax.axis_size("tp")
    return lax.ppermute(
        x,
        ("ret", "tp"),
        [(r * count + i, (1 - r) * count + (i + by) % count) for r in range(2) for i in range(count)],
    )


def near(keep, give):
    return turn(keep, "tp", 1), cross(give, -1), turn(keep, "tp", -1), cross(give, 1), cross(give, 0)


def far(keep_right, got_left):
    return turn(keep_right, "tp", 1), turn(got_left, "tp", -1)


def exchange(x, axis):
    return lax.all_to_all(x, axis, split_axis=0, concat_axis=0, tiled=True)


def added(x):
    return jnp.sum(x.astype(F32), axis=0).astype(BF16)


def body(queries, d_attn, pool, w_key, w_value, owners, picks, live_counts):
    y_count = lax.axis_size("y")
    z_high = lax.axis_size("zh")
    z_low = lax.axis_size("zl")
    ctx_count = y_count * z_high * z_low
    width = pool.shape[2]
    part = NBR_LEN // lax.axis_size("tp") // CHUNKS
    low = lax.axis_index("ret") == 0
    owner_col = jnp.where(low, owners[:, 0], owners[:, 1])
    pick_col = jnp.where(low, picks[:, 0], picks[:, 1])
    asked = jnp.sum(
        jnp.where(owner_col == ctx_index(), pick_col, 0).reshape(ctx_count, CH_DEV), axis=1
    )
    pool_blocks = pool[0].reshape(-1, NBR_LEN, width)

    first = pack(0, asked, live_counts, pool_blocks, part)
    second = pack(1, asked, live_counts, pool_blocks, part)
    incoming = exchange(first, CTX)
    held = hold(queries, d_attn, w_key, w_value)
    second, incoming, held = lax.optimization_barrier((second, incoming, held))
    late = exchange(second, CTX)
    keep, give = pick(owner_col, incoming)
    sides = near(keep, give)
    late, *shards = lax.optimization_barrier((late, keep, *sides, *far(*sides[:2])))
    first_rows = project(shards, *held[2:], "project_first")
    keep, give = pick(owner_col, late)
    keep_right, got_left, *sides = near(keep, give)
    ends = far(keep_right, got_left)
    near_rows = project((keep, keep_right, got_left, *sides), *held[2:], "project_near")
    tokens, other, rows, grads = attend(ends, *held, *first_rows, *near_rows)
    pair = (own_sum(first_rows[0], rows, grads) + swap(other).astype(F32)).astype(BF16)
    half = width // z_low
    by_y = added(exchange(pair.reshape(y_count * z_low, half, HEAD_DIM), ("y", "zl")))
    attn_out, d_queries = join(tokens, swap(tokens))
    terms = exchange(jnp.broadcast_to(by_y[None], (z_high,) + by_y.shape), "zh")
    terms, attn_out, d_queries = lax.optimization_barrier((terms, attn_out, d_queries))
    by_z = added(terms)
    pair_z = turn(by_z, "zl", 1)
    first = lax.axis_index("zl") == 0
    z_full = jnp.concatenate(
        [jnp.where(first, by_z, pair_z), jnp.where(first, pair_z, by_z)], axis=0
    )
    hops = (0, 1, y_count - 1) + tuple(range(2, y_count - 1))
    pieces = [turn(z_full, "y", hop) if hop else z_full for hop in hops]
    d_w_key, d_w_value = lay([(hop, 0) for hop in hops], pieces, [swap(x) for x in pieces])
    return (attn_out, d_queries, d_w_key, d_w_value)


def solution(mesh):
    z_high = mesh.shape["ctx"] // (Y_CHIPS * Z_PAIR)
    shape = (Y_CHIPS, z_high, Z_PAIR, mesh.shape["ret"], mesh.shape["tp"])
    fine = Mesh(mesh.devices.reshape(shape), CTX + ("ret", "tp"))
    ctx = CTX
    return jax.shard_map(
        body,
        mesh=fine,
        in_specs=(
            P(ctx, "tp"),
            P(ctx, "tp"),
            P("ret", ctx, None),
            P(None, "tp"),
            P(None, "tp"),
            P(),
            P(),
            P(),
        ),
        out_specs=(P(ctx, "tp"), P(ctx, "tp"), P(None, "tp"), P(None, "tp")),
        check_vma=False,
    )
```

```python
import functools
import math

import jax
import jax.numpy as jnp
from jax import lax
from jax.experimental import pallas as pl
from jax.experimental.pallas import tpu as pltpu
from jax.sharding import Mesh
from jax.sharding import PartitionSpec as P

HEAD_DIM = 128
SPAN = 64
NBR_LEN = 128
CH_DEV = 16
Y_CHIPS = 4
Z_PAIR = 2
CTX = ("y", "zh", "zl")


CHUNKS = 2
TOGETHER = 2

BF16 = jnp.bfloat16
F32 = jnp.float32
ANY = pl.BlockSpec(memory_space=pl.ANY)
SMEM = pl.BlockSpec(memory_space=pltpu.SMEM)
WHOLE = pl.BlockSpec(memory_space=pltpu.VMEM)


def ctx_index():
    z = lax.axis_index("zh") * lax.axis_size("zl") + lax.axis_index("zl")
    return lax.axis_index("y") * (lax.axis_size("zh") * lax.axis_size("zl")) + z


def pack_kernel(row, asked, live_counts, pool, out, held, in_sem, out_sem):
    part = held.shape[1]
    chunk = lax.axis_index("tp") * CHUNKS + row
    start = pl.multiple_of(chunk * part, part)
    load = pltpu.make_async_copy(pool.at[:, pl.ds(start, part), :], held, in_sem)
    load.start()
    live = live_counts[lax.axis_index("ret"), ctx_index()]
    slots = [lax.rem(asked[d], live) for d in range(out.shape[0])]
    copies = [
        pltpu.make_async_copy(held.at[slots[d]], out.at[d], out_sem.at[d])
        for d in range(out.shape[0])
    ]
    load.wait()
    for copy in copies:
        copy.start()
    for copy in copies:
        copy.wait()


def pack(row, asked, live_counts, pool_blocks, part):
    blocks, _, width = pool_blocks.shape
    count = asked.shape[0]
    return pl.pallas_call(
        functools.partial(pack_kernel, row),
        out_shape=jax.ShapeDtypeStruct((count, part, width), BF16),
        in_specs=[SMEM, SMEM, ANY],
        out_specs=ANY,
        scratch_shapes=[
            pltpu.VMEM((blocks, part, width), BF16),
            pltpu.SemaphoreType.DMA,
            pltpu.SemaphoreType.DMA((count,)),
        ],
        compiler_params=pltpu.CompilerParams(vmem_limit_bytes=60 << 20),
        name=f"pack{row}",
    )(asked, live_counts, pool_blocks)


def pick_kernel(owner_col, incoming, keep, give):
    half = keep.shape[0]
    me = lax.axis_index("ret")
    first = ctx_index() * (2 * half)
    for k in range(half):
        keep[k] = incoming[owner_col[first + me * half + k]]
        give[k] = incoming[owner_col[first + (1 - me) * half + k]]


def pick(owner_col, incoming):
    half = jax.ShapeDtypeStruct((CH_DEV // 2,) + incoming.shape[1:], BF16)
    return pl.pallas_call(
        pick_kernel,
        out_shape=(half, half),
        in_specs=[SMEM, WHOLE],
        out_specs=(WHOLE, WHOLE),
        compiler_params=pltpu.CompilerParams(vmem_limit_bytes=8 << 20),
        name="pick",
    )(owner_col, incoming)


def dot(a, b, dims=((1,), (0,))):
    return lax.dot_general(a, b, (dims, ((), ())), preferred_element_type=F32)


ROWS = ((1,), (1,))
DOWN = ((0,), (0,))


def two_heads(x):
    col = lax.broadcasted_iota(jnp.int32, x.shape, 1)
    zero = jnp.zeros_like(x)
    return jnp.concatenate(
        [jnp.where(col < HEAD_DIM, x, zero), jnp.where(col < HEAD_DIM, zero, x)], axis=0
    )


def own_heads(x):
    return jnp.concatenate([x[:SPAN, :HEAD_DIM], x[SPAN:, HEAD_DIM:]], axis=1)


def gather_rows(shards, rows, j):
    part = shards[0].shape[1]
    for p, shard in enumerate(shards):
        rows[j, p * part : (p + 1) * part, :] = shard[j]


def hold_kernel(queries, d_attn, w_key, w_value, q_out, g_out, k_out, v_out, sem):
    tokens = q_out.shape[0]
    place = pl.ds(pl.multiple_of(lax.axis_index("ret") * tokens, tokens), tokens)
    loads = [
        pltpu.make_async_copy(queries.at[place, :], q_out, sem.at[0]),
        pltpu.make_async_copy(d_attn.at[place, :], g_out, sem.at[1]),
        pltpu.make_async_copy(w_key, k_out, sem.at[2]),
        pltpu.make_async_copy(w_value, v_out, sem.at[3]),
    ]
    for load in loads:
        load.start()
    for load in loads:
        load.wait()


def hold(queries, d_attn, w_key, w_value):
    half = jax.ShapeDtypeStruct((queries.shape[0] // 2, queries.shape[1]), BF16)
    weight = jax.ShapeDtypeStruct(w_key.shape, BF16)
    return pl.pallas_call(
        hold_kernel,
        out_shape=(half, half, weight, weight),
        in_specs=[ANY] * 4,
        out_specs=(WHOLE,) * 4,
        scratch_shapes=[pltpu.SemaphoreType.DMA((4,))],
        compiler_params=pltpu.CompilerParams(vmem_limit_bytes=60 << 20),
        cost_estimate=pl.CostEstimate(flops=0, bytes_accessed=6 << 20, transcendentals=0),
        name="hold",
    )(queries, d_attn, w_key, w_value)


def project_kernel(count, *refs):
    shards = refs[:count]
    w_key, w_value, rows, pairs = refs[count:]
    spans, held, head_cols = pairs.shape
    head_cols //= 2
    for j in range(spans):
        gather_rows(shards, rows, j)
    flat = rows[...].reshape(spans * held, rows.shape[2])
    for side, weight in enumerate((w_key, w_value)):
        made = dot(flat, weight[...]).astype(BF16).reshape(spans, held, head_cols)
        pairs[:, :, side * head_cols : (side + 1) * head_cols] = made


def project(shards, w_key, w_value, name):
    spans, part, width = shards[0].shape
    head_cols = w_key.shape[1]
    count = len(shards) * part
    return pl.pallas_call(
        functools.partial(project_kernel, len(shards)),
        out_shape=(
            jax.ShapeDtypeStruct((spans, count, width), BF16),
            jax.ShapeDtypeStruct((spans, count, 2 * head_cols), BF16),
        ),
        in_specs=[WHOLE] * (len(shards) + 2),
        out_specs=(WHOLE,) * 2,
        compiler_params=pltpu.CompilerParams(vmem_limit_bytes=12 << 20),
        cost_estimate=pl.CostEstimate(
            flops=4 * spans * count * width * head_cols, bytes_accessed=4 << 20, transcendentals=0
        ),
        name=name,
    )(*shards, w_key, w_value)


def weight_sum(rows_a, rows_b, grads, side):
    head_cols = grads.shape[2] // 2
    cut = pl.ds(pl.multiple_of(side * head_cols, head_cols), head_cols)
    total = None
    for at, rows in enumerate((rows_a, rows_b)):
        flat = rows[...].reshape(-1, rows.shape[2])
        term = dot(flat, grads[at, :, cut], DOWN)
        total = term if total is None else total + term
    return total * (1.0 / (CH_DEV * 32))


def attend_kernel(count, *refs):
    shards = refs[:count]
    queries, d_attn, w_key, w_value, rows_a, pairs_a, rows_m, pairs_m = refs[count : count + 8]
    tokens_out, other, rows_b, grads, far_rows = refs[count + 8 :]
    spans, near_rows, width = rows_a.shape
    far_count = far_rows.shape[1]
    head_cols = w_key.shape[1]
    heads = head_cols // HEAD_DIM
    scale = 1.0 / math.sqrt(HEAD_DIM)
    raise_by = scale / math.log(2.0)
    for j in range(spans):
        gather_rows(shards, far_rows, j)
        rows_b[j, : near_rows - far_count, :] = rows_m[j]
        rows_b[j, near_rows - far_count :, :] = far_rows[j]
    far_flat = far_rows[...].reshape(spans * far_count, width)
    far_keys = dot(far_flat, w_key[...]).astype(BF16)
    far_values = dot(far_flat, w_value[...]).astype(BF16)
    for start in range(0, spans, TOGETHER):
        units = []
        for j in range(start, start + TOGETHER):
            units += [
                (
                    j,
                    slice(h * HEAD_DIM, (h + 2) * HEAD_DIM),
                    slice(head_cols + h * HEAD_DIM, head_cols + (h + 2) * HEAD_DIM),
                    slice(j * SPAN, (j + 1) * SPAN),
                    slice(j * near_rows, (j + 1) * near_rows),
                )
                for h in range(0, heads, 2)
            ]

        def made(far, j, cut, side_cut):
            late = far[j * far_count : (j + 1) * far_count, cut]
            return jnp.concatenate([pairs_a[j, :, side_cut], pairs_m[j, :, side_cut], late], axis=0)

        keys = [made(far_keys, j, cut, cut) for j, cut, _, _, _ in units]
        values = [made(far_values, j, cut, past) for j, cut, past, _, _ in units]
        qs = [two_heads(queries[at, cut]) for _, cut, _, at, _ in units]
        gs = [two_heads(d_attn[at, cut]) for _, cut, _, at, _ in units]
        scores = [dot(k, q, ROWS) for k, q in zip(keys, qs)]
        grad_probs = [dot(v, g, ROWS) for v, g in zip(values, gs)]
        tops = [jnp.max(x, axis=0, keepdims=True) for x in scores]
        raised = [jnp.exp2((x - top) * raise_by) for x, top in zip(scores, tops)]
        probs = [x * (1.0 / jnp.sum(x, axis=0, keepdims=True)) for x in raised]
        probs_b = [x.astype(BF16) for x in probs]
        out_dots = [jnp.sum(p * g, axis=0, keepdims=True) for p, g in zip(probs, grad_probs)]
        dscores = [
            (p * ((g - o) * scale)).astype(BF16) for p, g, o in zip(probs, grad_probs, out_dots)
        ]
        for i, (_, cut, past, at, to) in enumerate(units):
            k_grad = dot(dscores[i], qs[i]).astype(BF16)
            v_grad = dot(probs_b[i], gs[i]).astype(BF16)
            for side in range(2):
                part = slice(side * near_rows, (side + 1) * near_rows)
                grads[side, to, cut] = k_grad[part]
                grads[side, to, past] = v_grad[part]
            tokens_out[0, at, cut] = own_heads(dot(probs_b[i], values[i], DOWN)).astype(BF16)
            tokens_out[1, at, cut] = own_heads(dot(dscores[i], keys[i], DOWN)).astype(BF16)
    sums = weight_sum(rows_a, rows_b, grads, 1 - lax.axis_index("ret"))
    for h in range(heads):
        other[h] = sums[:, h * HEAD_DIM : (h + 1) * HEAD_DIM].astype(other.dtype)


def attend(shards, queries, d_attn, w_key, w_value, rows_a, pairs_a, rows_m, pairs_m):
    spans, near_rows, width = rows_a.shape
    nbr_rows = 2 * NBR_LEN
    head_cols = w_key.shape[1]
    heads = head_cols // HEAD_DIM
    tokens = spans * SPAN
    flops = 2 * spans * nbr_rows * head_cols * (2 * width + 12 * SPAN)
    return pl.pallas_call(
        functools.partial(attend_kernel, len(shards)),
        out_shape=(
            jax.ShapeDtypeStruct((2, tokens, head_cols), BF16),
            jax.ShapeDtypeStruct((heads, width, HEAD_DIM), BF16),
            jax.ShapeDtypeStruct((spans, near_rows, width), BF16),
            jax.ShapeDtypeStruct((2, spans * near_rows, 2 * head_cols), BF16),
        ),
        in_specs=[WHOLE] * (len(shards) + 8),
        out_specs=(WHOLE,) * 4,
        scratch_shapes=[pltpu.VMEM((spans, near_rows - rows_m.shape[1], width), BF16)],
        compiler_params=pltpu.CompilerParams(vmem_limit_bytes=16 << 20),
        cost_estimate=pl.CostEstimate(
            flops=flops, bytes_accessed=10 << 20, transcendentals=spans * SPAN * nbr_rows * heads
        ),
        name="attend",
    )(*shards, queries, d_attn, w_key, w_value, rows_a, pairs_a, rows_m, pairs_m)


def own_sum_kernel(rows_a, rows_b, grads, mine):
    sums = weight_sum(rows_a, rows_b, grads, lax.axis_index("ret"))
    for h in range(mine.shape[0]):
        mine[h] = sums[:, h * HEAD_DIM : (h + 1) * HEAD_DIM]


def own_sum(rows_a, rows_b, grads):
    width = rows_a.shape[2]
    heads = grads.shape[2] // 2 // HEAD_DIM
    return pl.pallas_call(
        own_sum_kernel,
        out_shape=jax.ShapeDtypeStruct((heads, width, HEAD_DIM), F32),
        in_specs=[WHOLE] * 3,
        out_specs=WHOLE,
        compiler_params=pltpu.CompilerParams(vmem_limit_bytes=16 << 20),
        cost_estimate=pl.CostEstimate(
            flops=4 * grads.shape[1] * width * heads * HEAD_DIM,
            bytes_accessed=4 << 20,
            transcendentals=0,
        ),
        name="own_sum",
    )(rows_a, rows_b, grads)


def join_kernel(mine, other, attn_out, d_queries, sem):
    me = lax.axis_index("ret")
    tokens = mine.shape[1]
    copies = []
    for side, held in ((me, mine), (1 - me, other)):
        place = pl.ds(pl.multiple_of(side * tokens, tokens), tokens)
        for which, out in enumerate((attn_out, d_queries)):
            copies.append(
                pltpu.make_async_copy(held.at[which], out.at[place, :], sem.at[len(copies)])
            )
    for copy in copies:
        copy.start()
    for copy in copies:
        copy.wait()


def join(mine, other):
    out = jax.ShapeDtypeStruct((2 * mine.shape[1], mine.shape[2]), BF16)
    return pl.pallas_call(
        join_kernel,
        out_shape=(out, out),
        in_specs=[ANY] * 2,
        out_specs=(ANY, ANY),
        scratch_shapes=[pltpu.SemaphoreType.DMA((4,))],
        compiler_params=pltpu.CompilerParams(vmem_limit_bytes=4 << 20),
        name="join",
    )(mine, other)


def lay_kernel(mine, other, d_w_key, d_w_value):
    low = lax.axis_index("ret") == 0
    for h in range(mine.shape[0]):
        cut = slice(h * HEAD_DIM, (h + 1) * HEAD_DIM)
        d_w_key[:, cut] = jnp.where(low, mine[h], other[h])
        d_w_value[:, cut] = jnp.where(low, other[h], mine[h])


def lay(mine, other):
    heads, width, cols = mine.shape
    out = jax.ShapeDtypeStruct((width, heads * cols), BF16)
    return pl.pallas_call(
        lay_kernel,
        out_shape=(out, out),
        in_specs=[WHOLE, WHOLE],
        out_specs=(WHOLE, WHOLE),
        compiler_params=pltpu.CompilerParams(vmem_limit_bytes=12 << 20),
        name="lay",
    )(mine, other)


def turn(x, axis, by):
    count = lax.axis_size(axis)
    return lax.ppermute(x, axis, [(i, (i + by) % count) for i in range(count)])


def swap(x):
    return turn(x, "ret", 1)


def cross(x, by):
    count = lax.axis_size("tp")
    return lax.ppermute(
        x,
        ("ret", "tp"),
        [(r * count + i, (1 - r) * count + (i + by) % count) for r in range(2) for i in range(count)],
    )


def near(keep, give):
    return turn(keep, "tp", 1), cross(give, -1), turn(keep, "tp", -1), cross(give, 1), cross(give, 0)


def far(keep_right, got_left):
    return turn(keep_right, "tp", 1), turn(got_left, "tp", -1)


def exchange(x, axis):
    return lax.all_to_all(x, axis, split_axis=0, concat_axis=0, tiled=True)


def added(x):
    return jnp.sum(x.astype(F32), axis=0).astype(BF16)


def body(queries, d_attn, pool, w_key, w_value, owners, picks, live_counts):
    y_count = lax.axis_size("y")
    z_high = lax.axis_size("zh")
    z_low = lax.axis_size("zl")
    ctx_count = y_count * z_high * z_low
    width = pool.shape[2]
    part = NBR_LEN // lax.axis_size("tp") // CHUNKS
    low = lax.axis_index("ret") == 0
    owner_col = jnp.where(low, owners[:, 0], owners[:, 1])
    pick_col = jnp.where(low, picks[:, 0], picks[:, 1])
    asked = jnp.sum(
        jnp.where(owner_col == ctx_index(), pick_col, 0).reshape(ctx_count, CH_DEV), axis=1
    )
    pool_blocks = pool[0].reshape(-1, NBR_LEN, width)

    first = pack(0, asked, live_counts, pool_blocks, part)
    second = pack(1, asked, live_counts, pool_blocks, part)
    incoming = exchange(first, CTX)
    held = hold(queries, d_attn, w_key, w_value)
    second, incoming, held = lax.optimization_barrier((second, incoming, held))
    late = exchange(second, CTX)
    keep, give = pick(owner_col, incoming)
    sides = near(keep, give)
    late, *shards = lax.optimization_barrier((late, keep, *sides, *far(*sides[:2])))
    first_rows = project(shards, *held[2:], "project_first")
    keep, give = pick(owner_col, late)
    keep_right, got_left, *sides = near(keep, give)
    ends = far(keep_right, got_left)
    near_rows = project((keep, keep_right, got_left, *sides), *held[2:], "project_near")
    tokens, other, rows, grads = attend(ends, *held, *first_rows, *near_rows)
    pair = (own_sum(first_rows[0], rows, grads) + swap(other).astype(F32)).astype(BF16)
    half = width // z_low
    by_y = added(exchange(pair.reshape(y_count * z_low, half, HEAD_DIM), ("y", "zl")))
    attn_out, d_queries = join(tokens, swap(tokens))
    terms = exchange(jnp.broadcast_to(by_y[None], (z_high,) + by_y.shape), "zh")
    terms, attn_out, d_queries = lax.optimization_barrier((terms, attn_out, d_queries))
    by_z = added(terms)
    mine_full = exchange(
        jnp.broadcast_to(by_z[None], (y_count * z_low,) + by_z.shape), ("y", "zl")
    ).reshape(y_count, width, HEAD_DIM)
    d_w_key, d_w_value = lay(mine_full, swap(mine_full))
    return (attn_out, d_queries, d_w_key, d_w_value)


def solution(mesh):
    z_high = mesh.shape["ctx"] // (Y_CHIPS * Z_PAIR)
    shape = (Y_CHIPS, z_high, Z_PAIR, mesh.shape["ret"], mesh.shape["tp"])
    fine = Mesh(mesh.devices.reshape(shape), CTX + ("ret", "tp"))
    ctx = CTX
    return jax.shard_map(
        body,
        mesh=fine,
        in_specs=(
            P(ctx, "tp"),
            P(ctx, "tp"),
            P("ret", ctx, None),
            P(None, "tp"),
            P(None, "tp"),
            P(),
            P(),
            P(),
        ),
        out_specs=(P(ctx, "tp"), P(ctx, "tp"), P(None, "tp"), P(None, "tp")),
        check_vma=False,
    )
```

```python
import functools
import math

import jax
import jax.numpy as jnp
from jax import lax
from jax.experimental import pallas as pl
from jax.experimental.pallas import tpu as pltpu
from jax.sharding import Mesh
from jax.sharding import PartitionSpec as P

HEAD_DIM = 128
SPAN = 64
NBR_LEN = 128
CH_DEV = 16
Y_CHIPS = 4
Z_PAIR = 2
CTX = ("y", "zh", "zl")


CHUNKS = 2
TOGETHER = 2

BF16 = jnp.bfloat16
F32 = jnp.float32
ANY = pl.BlockSpec(memory_space=pl.ANY)
SMEM = pl.BlockSpec(memory_space=pltpu.SMEM)
WHOLE = pl.BlockSpec(memory_space=pltpu.VMEM)


def ctx_index():
    z = lax.axis_index("zh") * lax.axis_size("zl") + lax.axis_index("zl")
    return lax.axis_index("y") * (lax.axis_size("zh") * lax.axis_size("zl")) + z


def pack_kernel(row, asked, live_counts, pool, out, held, in_sem, out_sem):
    part = held.shape[1]
    chunk = lax.axis_index("tp") * CHUNKS + row
    start = pl.multiple_of(chunk * part, part)
    load = pltpu.make_async_copy(pool.at[:, pl.ds(start, part), :], held, in_sem)
    load.start()
    live = live_counts[lax.axis_index("ret"), ctx_index()]
    slots = [lax.rem(asked[d], live) for d in range(out.shape[0])]
    copies = [
        pltpu.make_async_copy(held.at[slots[d]], out.at[d], out_sem.at[d])
        for d in range(out.shape[0])
    ]
    load.wait()
    for copy in copies:
        copy.start()
    for copy in copies:
        copy.wait()


def pack(row, asked, live_counts, pool_blocks, part):
    blocks, _, width = pool_blocks.shape
    count = asked.shape[0]
    return pl.pallas_call(
        functools.partial(pack_kernel, row),
        out_shape=jax.ShapeDtypeStruct((count, part, width), BF16),
        in_specs=[SMEM, SMEM, ANY],
        out_specs=ANY,
        scratch_shapes=[
            pltpu.VMEM((blocks, part, width), BF16),
            pltpu.SemaphoreType.DMA,
            pltpu.SemaphoreType.DMA((count,)),
        ],
        compiler_params=pltpu.CompilerParams(vmem_limit_bytes=60 << 20),
        name=f"pack{row}",
    )(asked, live_counts, pool_blocks)


def pick_kernel(owner_col, incoming, keep, give):
    half = keep.shape[0]
    me = lax.axis_index("ret")
    first = ctx_index() * (2 * half)
    for k in range(half):
        keep[k] = incoming[owner_col[first + me * half + k]]
        give[k] = incoming[owner_col[first + (1 - me) * half + k]]


def pick(owner_col, incoming):
    half = jax.ShapeDtypeStruct((CH_DEV // 2,) + incoming.shape[1:], BF16)
    return pl.pallas_call(
        pick_kernel,
        out_shape=(half, half),
        in_specs=[SMEM, WHOLE],
        out_specs=(WHOLE, WHOLE),
        compiler_params=pltpu.CompilerParams(vmem_limit_bytes=8 << 20),
        name="pick",
    )(owner_col, incoming)


def dot(a, b, dims=((1,), (0,))):
    return lax.dot_general(a, b, (dims, ((), ())), preferred_element_type=F32)


ROWS = ((1,), (1,))
DOWN = ((0,), (0,))


def two_heads(x):
    col = lax.broadcasted_iota(jnp.int32, x.shape, 1)
    zero = jnp.zeros_like(x)
    return jnp.concatenate(
        [jnp.where(col < HEAD_DIM, x, zero), jnp.where(col < HEAD_DIM, zero, x)], axis=0
    )


def own_heads(x):
    return jnp.concatenate([x[:SPAN, :HEAD_DIM], x[SPAN:, HEAD_DIM:]], axis=1)


def gather_rows(shards, rows, j):
    part = shards[0].shape[1]
    for p, shard in enumerate(shards):
        rows[j, p * part : (p + 1) * part, :] = shard[j]


def hold_kernel(queries, d_attn, w_key, w_value, q_out, g_out, k_out, v_out, sem):
    tokens = q_out.shape[0]
    place = pl.ds(pl.multiple_of(lax.axis_index("ret") * tokens, tokens), tokens)
    loads = [
        pltpu.make_async_copy(queries.at[place, :], q_out, sem.at[0]),
        pltpu.make_async_copy(d_attn.at[place, :], g_out, sem.at[1]),
        pltpu.make_async_copy(w_key, k_out, sem.at[2]),
        pltpu.make_async_copy(w_value, v_out, sem.at[3]),
    ]
    for load in loads:
        load.start()
    for load in loads:
        load.wait()


def hold(queries, d_attn, w_key, w_value):
    half = jax.ShapeDtypeStruct((queries.shape[0] // 2, queries.shape[1]), BF16)
    weight = jax.ShapeDtypeStruct(w_key.shape, BF16)
    return pl.pallas_call(
        hold_kernel,
        out_shape=(half, half, weight, weight),
        in_specs=[ANY] * 4,
        out_specs=(WHOLE,) * 4,
        scratch_shapes=[pltpu.SemaphoreType.DMA((4,))],
        compiler_params=pltpu.CompilerParams(vmem_limit_bytes=60 << 20),
        cost_estimate=pl.CostEstimate(flops=0, bytes_accessed=6 << 20, transcendentals=0),
        name="hold",
    )(queries, d_attn, w_key, w_value)


def project_kernel(count, *refs):
    shards = refs[:count]
    w_key, w_value, rows, pairs = refs[count:]
    spans, held, head_cols = pairs.shape
    head_cols //= 2
    for j in range(spans):
        gather_rows(shards, rows, j)
    flat = rows[...].reshape(spans * held, rows.shape[2])
    for side, weight in enumerate((w_key, w_value)):
        made = dot(flat, weight[...]).astype(BF16).reshape(spans, held, head_cols)
        pairs[:, :, side * head_cols : (side + 1) * head_cols] = made


def project(shards, w_key, w_value, name):
    spans, part, width = shards[0].shape
    head_cols = w_key.shape[1]
    count = len(shards) * part
    return pl.pallas_call(
        functools.partial(project_kernel, len(shards)),
        out_shape=(
            jax.ShapeDtypeStruct((spans, count, width), BF16),
            jax.ShapeDtypeStruct((spans, count, 2 * head_cols), BF16),
        ),
        in_specs=[WHOLE] * (len(shards) + 2),
        out_specs=(WHOLE,) * 2,
        compiler_params=pltpu.CompilerParams(vmem_limit_bytes=12 << 20),
        cost_estimate=pl.CostEstimate(
            flops=4 * spans * count * width * head_cols, bytes_accessed=4 << 20, transcendentals=0
        ),
        name=name,
    )(*shards, w_key, w_value)


def weight_sum(rows_a, rows_b, grads, side):
    head_cols = grads.shape[2] // 2
    cut = pl.ds(pl.multiple_of(side * head_cols, head_cols), head_cols)
    total = None
    for at, rows in enumerate((rows_a, rows_b)):
        flat = rows[...].reshape(-1, rows.shape[2])
        term = dot(flat, grads[at, :, cut], DOWN)
        total = term if total is None else total + term
    return total * (1.0 / (CH_DEV * 32))


def attend_kernel(count, *refs):
    shards = refs[:count]
    queries, d_attn, w_key, w_value, rows_a, pairs_a, rows_m, pairs_m = refs[count : count + 8]
    tokens_out, other, rows_b, grads, far_rows = refs[count + 8 :]
    spans, near_rows, width = rows_a.shape
    far_count = far_rows.shape[1]
    head_cols = w_key.shape[1]
    heads = head_cols // HEAD_DIM
    scale = 1.0 / math.sqrt(HEAD_DIM)
    raise_by = scale / math.log(2.0)
    for j in range(spans):
        gather_rows(shards, far_rows, j)
        rows_b[j, : near_rows - far_count, :] = rows_m[j]
        rows_b[j, near_rows - far_count :, :] = far_rows[j]
    far_flat = far_rows[...].reshape(spans * far_count, width)
    far_keys = dot(far_flat, w_key[...]).astype(BF16)
    far_values = dot(far_flat, w_value[...]).astype(BF16)
    for start in range(0, spans, TOGETHER):
        units = []
        for j in range(start, start + TOGETHER):
            units += [
                (
                    j,
                    slice(h * HEAD_DIM, (h + 2) * HEAD_DIM),
                    slice(head_cols + h * HEAD_DIM, head_cols + (h + 2) * HEAD_DIM),
                    slice(j * SPAN, (j + 1) * SPAN),
                    slice(j * near_rows, (j + 1) * near_rows),
                )
                for h in range(0, heads, 2)
            ]

        def made(far, j, cut, side_cut):
            late = far[j * far_count : (j + 1) * far_count, cut]
            return jnp.concatenate([pairs_a[j, :, side_cut], pairs_m[j, :, side_cut], late], axis=0)

        keys = [made(far_keys, j, cut, cut) for j, cut, _, _, _ in units]
        values = [made(far_values, j, cut, past) for j, cut, past, _, _ in units]
        qs = [two_heads(queries[at, cut]) for _, cut, _, at, _ in units]
        gs = [two_heads(d_attn[at, cut]) for _, cut, _, at, _ in units]
        scores = [dot(k, q, ROWS) for k, q in zip(keys, qs)]
        grad_probs = [dot(v, g, ROWS) for v, g in zip(values, gs)]
        tops = [jnp.max(x, axis=0, keepdims=True) for x in scores]
        raised = [jnp.exp2((x - top) * raise_by) for x, top in zip(scores, tops)]
        probs = [x * (1.0 / jnp.sum(x, axis=0, keepdims=True)) for x in raised]
        probs_b = [x.astype(BF16) for x in probs]
        out_dots = [jnp.sum(p * g, axis=0, keepdims=True) for p, g in zip(probs, grad_probs)]
        dscores = [
            (p * ((g - o) * scale)).astype(BF16) for p, g, o in zip(probs, grad_probs, out_dots)
        ]
        for i, (_, cut, past, at, to) in enumerate(units):
            k_grad = dot(dscores[i], qs[i]).astype(BF16)
            v_grad = dot(probs_b[i], gs[i]).astype(BF16)
            for side in range(2):
                part = slice(side * near_rows, (side + 1) * near_rows)
                grads[side, to, cut] = k_grad[part]
                grads[side, to, past] = v_grad[part]
            tokens_out[0, at, cut] = own_heads(dot(probs_b[i], values[i], DOWN)).astype(BF16)
            tokens_out[1, at, cut] = own_heads(dot(dscores[i], keys[i], DOWN)).astype(BF16)
    sums = weight_sum(rows_a, rows_b, grads, 1 - lax.axis_index("ret"))
    for h in range(heads):
        other[h] = sums[:, h * HEAD_DIM : (h + 1) * HEAD_DIM].astype(other.dtype)


def attend(shards, queries, d_attn, w_key, w_value, rows_a, pairs_a, rows_m, pairs_m):
    spans, near_rows, width = rows_a.shape
    nbr_rows = 2 * NBR_LEN
    head_cols = w_key.shape[1]
    heads = head_cols // HEAD_DIM
    tokens = spans * SPAN
    flops = 2 * spans * nbr_rows * head_cols * (2 * width + 12 * SPAN)
    return pl.pallas_call(
        functools.partial(attend_kernel, len(shards)),
        out_shape=(
            jax.ShapeDtypeStruct((2, tokens, head_cols), BF16),
            jax.ShapeDtypeStruct((heads, width, HEAD_DIM), BF16),
            jax.ShapeDtypeStruct((spans, near_rows, width), BF16),
            jax.ShapeDtypeStruct((2, spans * near_rows, 2 * head_cols), BF16),
        ),
        in_specs=[WHOLE] * (len(shards) + 8),
        out_specs=(WHOLE,) * 4,
        scratch_shapes=[pltpu.VMEM((spans, near_rows - rows_m.shape[1], width), BF16)],
        compiler_params=pltpu.CompilerParams(vmem_limit_bytes=16 << 20),
        cost_estimate=pl.CostEstimate(
            flops=flops, bytes_accessed=10 << 20, transcendentals=spans * SPAN * nbr_rows * heads
        ),
        name="attend",
    )(*shards, queries, d_attn, w_key, w_value, rows_a, pairs_a, rows_m, pairs_m)


def own_sum_kernel(rows_a, rows_b, grads, mine):
    sums = weight_sum(rows_a, rows_b, grads, lax.axis_index("ret"))
    for h in range(mine.shape[0]):
        mine[h] = sums[:, h * HEAD_DIM : (h + 1) * HEAD_DIM]


def own_sum(rows_a, rows_b, grads):
    width = rows_a.shape[2]
    heads = grads.shape[2] // 2 // HEAD_DIM
    return pl.pallas_call(
        own_sum_kernel,
        out_shape=jax.ShapeDtypeStruct((heads, width, HEAD_DIM), F32),
        in_specs=[WHOLE] * 3,
        out_specs=WHOLE,
        compiler_params=pltpu.CompilerParams(vmem_limit_bytes=16 << 20),
        cost_estimate=pl.CostEstimate(
            flops=4 * grads.shape[1] * width * heads * HEAD_DIM,
            bytes_accessed=4 << 20,
            transcendentals=0,
        ),
        name="own_sum",
    )(rows_a, rows_b, grads)


def join_kernel(mine, other, attn_out, d_queries, sem):
    me = lax.axis_index("ret")
    tokens = mine.shape[1]
    copies = []
    for side, held in ((me, mine), (1 - me, other)):
        place = pl.ds(pl.multiple_of(side * tokens, tokens), tokens)
        for which, out in enumerate((attn_out, d_queries)):
            copies.append(
                pltpu.make_async_copy(held.at[which], out.at[place, :], sem.at[len(copies)])
            )
    for copy in copies:
        copy.start()
    for copy in copies:
        copy.wait()


def join(mine, other):
    out = jax.ShapeDtypeStruct((2 * mine.shape[1], mine.shape[2]), BF16)
    return pl.pallas_call(
        join_kernel,
        out_shape=(out, out),
        in_specs=[ANY] * 2,
        out_specs=(ANY, ANY),
        scratch_shapes=[pltpu.SemaphoreType.DMA((4,))],
        compiler_params=pltpu.CompilerParams(vmem_limit_bytes=4 << 20),
        name="join",
    )(mine, other)


def stack_kernel(hops, *refs):
    near_z, far_z, out = refs[: len(hops)], refs[len(hops) : -1], refs[-1]
    half = near_z[0].shape[0]
    count = lax.axis_size("y")
    me = lax.axis_index("zl")
    for hop, x, y in zip(hops, near_z, far_z):
        h = lax.rem(lax.axis_index("y") + (count - hop), count)
        for side, piece in ((me, x), (1 - me, y)):
            out[h, pl.ds(pl.multiple_of(side * half, half), half), :] = piece[...]


def stack(hops, near_z, far_z):
    half, cols = near_z[0].shape
    return pl.pallas_call(
        functools.partial(stack_kernel, hops),
        out_shape=jax.ShapeDtypeStruct((len(hops), 2 * half, cols), BF16),
        in_specs=[WHOLE] * (2 * len(hops)),
        out_specs=WHOLE,
        compiler_params=pltpu.CompilerParams(vmem_limit_bytes=8 << 20),
        name="stack",
    )(*near_z, *far_z)


def lay_kernel(mine, other, d_w_key, d_w_value):
    low = lax.axis_index("ret") == 0
    for h in range(mine.shape[0]):
        cut = slice(h * HEAD_DIM, (h + 1) * HEAD_DIM)
        d_w_key[:, cut] = jnp.where(low, mine[h], other[h])
        d_w_value[:, cut] = jnp.where(low, other[h], mine[h])


def lay(mine, other):
    heads, width, cols = mine.shape
    out = jax.ShapeDtypeStruct((width, heads * cols), BF16)
    return pl.pallas_call(
        lay_kernel,
        out_shape=(out, out),
        in_specs=[WHOLE, WHOLE],
        out_specs=(WHOLE, WHOLE),
        compiler_params=pltpu.CompilerParams(vmem_limit_bytes=12 << 20),
        name="lay",
    )(mine, other)


def turn(x, axis, by):
    count = lax.axis_size(axis)
    return lax.ppermute(x, axis, [(i, (i + by) % count) for i in range(count)])


def swap(x):
    return turn(x, "ret", 1)


def cross(x, by):
    count = lax.axis_size("tp")
    return lax.ppermute(
        x,
        ("ret", "tp"),
        [(r * count + i, (1 - r) * count + (i + by) % count) for r in range(2) for i in range(count)],
    )


def near(keep, give):
    return turn(keep, "tp", 1), cross(give, -1), turn(keep, "tp", -1), cross(give, 1), cross(give, 0)


def far(keep_right, got_left):
    return turn(keep_right, "tp", 1), turn(got_left, "tp", -1)


def exchange(x, axis):
    return lax.all_to_all(x, axis, split_axis=0, concat_axis=0, tiled=True)


def added(x):
    return jnp.sum(x.astype(F32), axis=0).astype(BF16)


def body(queries, d_attn, pool, w_key, w_value, owners, picks, live_counts):
    y_count = lax.axis_size("y")
    z_high = lax.axis_size("zh")
    z_low = lax.axis_size("zl")
    ctx_count = y_count * z_high * z_low
    width = pool.shape[2]
    part = NBR_LEN // lax.axis_size("tp") // CHUNKS
    low = lax.axis_index("ret") == 0
    owner_col = jnp.where(low, owners[:, 0], owners[:, 1])
    pick_col = jnp.where(low, picks[:, 0], picks[:, 1])
    asked = jnp.sum(
        jnp.where(owner_col == ctx_index(), pick_col, 0).reshape(ctx_count, CH_DEV), axis=1
    )
    pool_blocks = pool[0].reshape(-1, NBR_LEN, width)

    first = pack(0, asked, live_counts, pool_blocks, part)
    second = pack(1, asked, live_counts, pool_blocks, part)
    incoming = exchange(first, CTX)
    held = hold(queries, d_attn, w_key, w_value)
    second, incoming, held = lax.optimization_barrier((second, incoming, held))
    late = exchange(second, CTX)
    keep, give = pick(owner_col, incoming)
    sides = near(keep, give)
    late, *shards = lax.optimization_barrier((late, keep, *sides, *far(*sides[:2])))
    first_rows = project(shards, *held[2:], "project_first")
    keep, give = pick(owner_col, late)
    keep_right, got_left, *sides = near(keep, give)
    ends = far(keep_right, got_left)
    near_rows = project((keep, keep_right, got_left, *sides), *held[2:], "project_near")
    tokens, other, rows, grads = attend(ends, *held, *first_rows, *near_rows)
    pair = (own_sum(first_rows[0], rows, grads) + swap(other).astype(F32)).astype(BF16)
    half = width // z_low
    by_y = added(exchange(pair.reshape(y_count * z_low, half, HEAD_DIM), ("y", "zl")))
    attn_out, d_queries = join(tokens, swap(tokens))
    terms = exchange(jnp.broadcast_to(by_y[None], (z_high,) + by_y.shape), "zh")
    terms, attn_out, d_queries = lax.optimization_barrier((terms, attn_out, d_queries))
    by_z = added(terms)
    hops = (0, 1, y_count - 1) + tuple(range(2, y_count - 1))
    near_z = [turn(by_z, "y", hop) if hop else by_z for hop in hops]
    mine_full = stack(hops, near_z, [turn(x, "zl", 1) for x in near_z])
    d_w_key, d_w_value = lay(mine_full, swap(mine_full))
    return (attn_out, d_queries, d_w_key, d_w_value)


def solution(mesh):
    z_high = mesh.shape["ctx"] // (Y_CHIPS * Z_PAIR)
    shape = (Y_CHIPS, z_high, Z_PAIR, mesh.shape["ret"], mesh.shape["tp"])
    fine = Mesh(mesh.devices.reshape(shape), CTX + ("ret", "tp"))
    ctx = CTX
    return jax.shard_map(
        body,
        mesh=fine,
        in_specs=(
            P(ctx, "tp"),
            P(ctx, "tp"),
            P("ret", ctx, None),
            P(None, "tp"),
            P(None, "tp"),
            P(),
            P(),
            P(),
        ),
        out_specs=(P(ctx, "tp"), P(ctx, "tp"), P(None, "tp"), P(None, "tp")),
        check_vma=False,
    )
```

```python
import functools
import math

import jax
import jax.numpy as jnp
from jax import lax
from jax.experimental import pallas as pl
from jax.experimental.pallas import tpu as pltpu
from jax.sharding import Mesh
from jax.sharding import PartitionSpec as P

HEAD_DIM = 128
SPAN = 64
NBR_LEN = 128
CH_DEV = 16
Y_CHIPS = 4
Z_PAIR = 2
CTX = ("y", "zh", "zl")


CHUNKS = 2
TOGETHER = 2

BF16 = jnp.bfloat16
F32 = jnp.float32
ANY = pl.BlockSpec(memory_space=pl.ANY)
SMEM = pl.BlockSpec(memory_space=pltpu.SMEM)
WHOLE = pl.BlockSpec(memory_space=pltpu.VMEM)


def ctx_index():
    z = lax.axis_index("zh") * lax.axis_size("zl") + lax.axis_index("zl")
    return lax.axis_index("y") * (lax.axis_size("zh") * lax.axis_size("zl")) + z


def pack_kernel(row, asked, live_counts, pool, out, held, in_sem, out_sem):
    part = held.shape[1]
    chunk = lax.axis_index("tp") * CHUNKS + row
    start = pl.multiple_of(chunk * part, part)
    load = pltpu.make_async_copy(pool.at[:, pl.ds(start, part), :], held, in_sem)
    load.start()
    live = live_counts[lax.axis_index("ret"), ctx_index()]
    slots = [lax.rem(asked[d], live) for d in range(out.shape[0])]
    copies = [
        pltpu.make_async_copy(held.at[slots[d]], out.at[d], out_sem.at[d])
        for d in range(out.shape[0])
    ]
    load.wait()
    for copy in copies:
        copy.start()
    for copy in copies:
        copy.wait()


def pack(row, asked, live_counts, pool_blocks, part):
    blocks, _, width = pool_blocks.shape
    count = asked.shape[0]
    return pl.pallas_call(
        functools.partial(pack_kernel, row),
        out_shape=jax.ShapeDtypeStruct((count, part, width), BF16),
        in_specs=[SMEM, SMEM, ANY],
        out_specs=ANY,
        scratch_shapes=[
            pltpu.VMEM((blocks, part, width), BF16),
            pltpu.SemaphoreType.DMA,
            pltpu.SemaphoreType.DMA((count,)),
        ],
        compiler_params=pltpu.CompilerParams(vmem_limit_bytes=60 << 20),
        name=f"pack{row}",
    )(asked, live_counts, pool_blocks)


def pick_kernel(owner_col, incoming, keep, give):
    half = keep.shape[0]
    me = lax.axis_index("ret")
    first = ctx_index() * (2 * half)
    for k in range(half):
        keep[k] = incoming[owner_col[first + me * half + k]]
        give[k] = incoming[owner_col[first + (1 - me) * half + k]]


def pick(owner_col, incoming):
    half = jax.ShapeDtypeStruct((CH_DEV // 2,) + incoming.shape[1:], BF16)
    return pl.pallas_call(
        pick_kernel,
        out_shape=(half, half),
        in_specs=[SMEM, WHOLE],
        out_specs=(WHOLE, WHOLE),
        compiler_params=pltpu.CompilerParams(vmem_limit_bytes=8 << 20),
        name="pick",
    )(owner_col, incoming)


def dot(a, b, dims=((1,), (0,))):
    return lax.dot_general(a, b, (dims, ((), ())), preferred_element_type=F32)


ROWS = ((1,), (1,))
DOWN = ((0,), (0,))


def two_heads(x):
    col = lax.broadcasted_iota(jnp.int32, x.shape, 1)
    zero = jnp.zeros_like(x)
    return jnp.concatenate(
        [jnp.where(col < HEAD_DIM, x, zero), jnp.where(col < HEAD_DIM, zero, x)], axis=0
    )


def own_heads(x):
    return jnp.concatenate([x[:SPAN, :HEAD_DIM], x[SPAN:, HEAD_DIM:]], axis=1)


def gather_rows(shards, rows, j):
    part = shards[0].shape[1]
    for p, shard in enumerate(shards):
        rows[j, p * part : (p + 1) * part, :] = shard[j]


def hold_kernel(queries, d_attn, w_key, w_value, q_out, g_out, k_out, v_out, sem):
    tokens = q_out.shape[0]
    place = pl.ds(pl.multiple_of(lax.axis_index("ret") * tokens, tokens), tokens)
    loads = [
        pltpu.make_async_copy(queries.at[place, :], q_out, sem.at[0]),
        pltpu.make_async_copy(d_attn.at[place, :], g_out, sem.at[1]),
        pltpu.make_async_copy(w_key, k_out, sem.at[2]),
        pltpu.make_async_copy(w_value, v_out, sem.at[3]),
    ]
    for load in loads:
        load.start()
    for load in loads:
        load.wait()


def hold(queries, d_attn, w_key, w_value):
    half = jax.ShapeDtypeStruct((queries.shape[0] // 2, queries.shape[1]), BF16)
    weight = jax.ShapeDtypeStruct(w_key.shape, BF16)
    return pl.pallas_call(
        hold_kernel,
        out_shape=(half, half, weight, weight),
        in_specs=[ANY] * 4,
        out_specs=(WHOLE,) * 4,
        scratch_shapes=[pltpu.SemaphoreType.DMA((4,))],
        compiler_params=pltpu.CompilerParams(vmem_limit_bytes=60 << 20),
        cost_estimate=pl.CostEstimate(flops=0, bytes_accessed=6 << 20, transcendentals=0),
        name="hold",
    )(queries, d_attn, w_key, w_value)


def project_kernel(count, *refs):
    shards = refs[:count]
    w_key, w_value, rows, pairs = refs[count:]
    spans, held, head_cols = pairs.shape
    head_cols //= 2
    for j in range(spans):
        gather_rows(shards, rows, j)
    flat = rows[...].reshape(spans * held, rows.shape[2])
    for side, weight in enumerate((w_key, w_value)):
        made = dot(flat, weight[...]).astype(BF16).reshape(spans, held, head_cols)
        pairs[:, :, side * head_cols : (side + 1) * head_cols] = made


def project(shards, w_key, w_value, name):
    spans, part, width = shards[0].shape
    head_cols = w_key.shape[1]
    count = len(shards) * part
    return pl.pallas_call(
        functools.partial(project_kernel, len(shards)),
        out_shape=(
            jax.ShapeDtypeStruct((spans, count, width), BF16),
            jax.ShapeDtypeStruct((spans, count, 2 * head_cols), BF16),
        ),
        in_specs=[WHOLE] * (len(shards) + 2),
        out_specs=(WHOLE,) * 2,
        compiler_params=pltpu.CompilerParams(vmem_limit_bytes=12 << 20),
        cost_estimate=pl.CostEstimate(
            flops=4 * spans * count * width * head_cols, bytes_accessed=4 << 20, transcendentals=0
        ),
        name=name,
    )(*shards, w_key, w_value)


def weight_sum(rows_a, rows_b, grads, side):
    head_cols = grads.shape[2] // 2
    cut = pl.ds(pl.multiple_of(side * head_cols, head_cols), head_cols)
    total = None
    for at, rows in enumerate((rows_a, rows_b)):
        flat = rows[...].reshape(-1, rows.shape[2])
        term = dot(flat, grads[at, :, cut], DOWN)
        total = term if total is None else total + term
    return total * (1.0 / (CH_DEV * 32))


def attend_kernel(count, *refs):
    shards = refs[:count]
    queries, d_attn, w_key, w_value, rows_a, pairs_a, rows_m, pairs_m = refs[count : count + 8]
    tokens_out, other, rows_b, grads, far_rows = refs[count + 8 :]
    spans, near_rows, width = rows_a.shape
    far_count = far_rows.shape[1]
    head_cols = w_key.shape[1]
    heads = head_cols // HEAD_DIM
    scale = 1.0 / math.sqrt(HEAD_DIM)
    raise_by = scale / math.log(2.0)
    for j in range(spans):
        gather_rows(shards, far_rows, j)
        rows_b[j, : near_rows - far_count, :] = rows_m[j]
        rows_b[j, near_rows - far_count :, :] = far_rows[j]
    far_flat = far_rows[...].reshape(spans * far_count, width)
    far_keys = dot(far_flat, w_key[...]).astype(BF16)
    far_values = dot(far_flat, w_value[...]).astype(BF16)
    for start in range(0, spans, TOGETHER):
        units = []
        for j in range(start, start + TOGETHER):
            units += [
                (
                    j,
                    slice(h * HEAD_DIM, (h + 2) * HEAD_DIM),
                    slice(head_cols + h * HEAD_DIM, head_cols + (h + 2) * HEAD_DIM),
                    slice(j * SPAN, (j + 1) * SPAN),
                    slice(j * near_rows, (j + 1) * near_rows),
                )
                for h in range(0, heads, 2)
            ]

        def made(far, j, cut, side_cut):
            late = far[j * far_count : (j + 1) * far_count, cut]
            return jnp.concatenate([pairs_a[j, :, side_cut], pairs_m[j, :, side_cut], late], axis=0)

        keys = [made(far_keys, j, cut, cut) for j, cut, _, _, _ in units]
        values = [made(far_values, j, cut, past) for j, cut, past, _, _ in units]
        qs = [two_heads(queries[at, cut]) for _, cut, _, at, _ in units]
        gs = [two_heads(d_attn[at, cut]) for _, cut, _, at, _ in units]
        scores = [dot(k, q, ROWS) for k, q in zip(keys, qs)]
        grad_probs = [dot(v, g, ROWS) for v, g in zip(values, gs)]
        tops = [jnp.max(x, axis=0, keepdims=True) for x in scores]
        raised = [jnp.exp2((x - top) * raise_by) for x, top in zip(scores, tops)]
        probs = [x * (1.0 / jnp.sum(x, axis=0, keepdims=True)) for x in raised]
        probs_b = [x.astype(BF16) for x in probs]
        out_dots = [jnp.sum(p * g, axis=0, keepdims=True) for p, g in zip(probs, grad_probs)]
        dscores = [
            (p * ((g - o) * scale)).astype(BF16) for p, g, o in zip(probs, grad_probs, out_dots)
        ]
        for i, (_, cut, past, at, to) in enumerate(units):
            k_grad = dot(dscores[i], qs[i]).astype(BF16)
            v_grad = dot(probs_b[i], gs[i]).astype(BF16)
            for side in range(2):
                part = slice(side * near_rows, (side + 1) * near_rows)
                grads[side, to, cut] = k_grad[part]
                grads[side, to, past] = v_grad[part]
            tokens_out[0, at, cut] = own_heads(dot(probs_b[i], values[i], DOWN)).astype(BF16)
            tokens_out[1, at, cut] = own_heads(dot(dscores[i], keys[i], DOWN)).astype(BF16)
    sums = weight_sum(rows_a, rows_b, grads, 1 - lax.axis_index("ret"))
    for h in range(heads):
        other[h] = sums[:, h * HEAD_DIM : (h + 1) * HEAD_DIM].astype(other.dtype)


def attend(shards, queries, d_attn, w_key, w_value, rows_a, pairs_a, rows_m, pairs_m):
    spans, near_rows, width = rows_a.shape
    nbr_rows = 2 * NBR_LEN
    head_cols = w_key.shape[1]
    heads = head_cols // HEAD_DIM
    tokens = spans * SPAN
    flops = 2 * spans * nbr_rows * head_cols * (2 * width + 12 * SPAN)
    return pl.pallas_call(
        functools.partial(attend_kernel, len(shards)),
        out_shape=(
            jax.ShapeDtypeStruct((2, tokens, head_cols), BF16),
            jax.ShapeDtypeStruct((heads, width, HEAD_DIM), BF16),
            jax.ShapeDtypeStruct((spans, near_rows, width), BF16),
            jax.ShapeDtypeStruct((2, spans * near_rows, 2 * head_cols), BF16),
        ),
        in_specs=[WHOLE] * (len(shards) + 8),
        out_specs=(WHOLE,) * 4,
        scratch_shapes=[pltpu.VMEM((spans, near_rows - rows_m.shape[1], width), BF16)],
        compiler_params=pltpu.CompilerParams(vmem_limit_bytes=16 << 20),
        cost_estimate=pl.CostEstimate(
            flops=flops, bytes_accessed=10 << 20, transcendentals=spans * SPAN * nbr_rows * heads
        ),
        name="attend",
    )(*shards, queries, d_attn, w_key, w_value, rows_a, pairs_a, rows_m, pairs_m)


def own_sum_kernel(rows_a, rows_b, grads, mine):
    sums = weight_sum(rows_a, rows_b, grads, lax.axis_index("ret"))
    for h in range(mine.shape[0]):
        mine[h] = sums[:, h * HEAD_DIM : (h + 1) * HEAD_DIM]


def own_sum(rows_a, rows_b, grads):
    width = rows_a.shape[2]
    heads = grads.shape[2] // 2 // HEAD_DIM
    return pl.pallas_call(
        own_sum_kernel,
        out_shape=jax.ShapeDtypeStruct((heads, width, HEAD_DIM), F32),
        in_specs=[WHOLE] * 3,
        out_specs=WHOLE,
        compiler_params=pltpu.CompilerParams(vmem_limit_bytes=16 << 20),
        cost_estimate=pl.CostEstimate(
            flops=4 * grads.shape[1] * width * heads * HEAD_DIM,
            bytes_accessed=4 << 20,
            transcendentals=0,
        ),
        name="own_sum",
    )(rows_a, rows_b, grads)


def join_kernel(mine, other, attn_out, d_queries, sem):
    me = lax.axis_index("ret")
    tokens = mine.shape[1]
    copies = []
    for side, held in ((me, mine), (1 - me, other)):
        place = pl.ds(pl.multiple_of(side * tokens, tokens), tokens)
        for which, out in enumerate((attn_out, d_queries)):
            copies.append(
                pltpu.make_async_copy(held.at[which], out.at[place, :], sem.at[len(copies)])
            )
    for copy in copies:
        copy.start()
    for copy in copies:
        copy.wait()


def join(mine, other):
    out = jax.ShapeDtypeStruct((2 * mine.shape[1], mine.shape[2]), BF16)
    return pl.pallas_call(
        join_kernel,
        out_shape=(out, out),
        in_specs=[ANY] * 2,
        out_specs=(ANY, ANY),
        scratch_shapes=[pltpu.SemaphoreType.DMA((4,))],
        compiler_params=pltpu.CompilerParams(vmem_limit_bytes=4 << 20),
        name="join",
    )(mine, other)


def lay_kernel(hops, *refs):
    d_w_key, d_w_value = refs[-2:]
    total = 2 * len(hops)
    half = refs[0].shape[0]
    low = lax.axis_index("ret") == 0
    count = lax.axis_size("y")
    for i in range(total):
        mine, other = refs[i], refs[total + i]
        h = lax.rem(lax.axis_index("y") + (count - hops[i % len(hops)]), count)
        side = lax.rem(lax.axis_index("zl") + i // len(hops), 2)
        place = (
            pl.ds(pl.multiple_of(side * half, half), half),
            pl.ds(pl.multiple_of(h * HEAD_DIM, HEAD_DIM), HEAD_DIM),
        )
        d_w_key[place] = jnp.where(low, mine[...], other[...])
        d_w_value[place] = jnp.where(low, other[...], mine[...])


def lay(hops, mine, other):
    half, cols = mine[0].shape
    out = jax.ShapeDtypeStruct((2 * half, len(hops) * cols), BF16)
    return pl.pallas_call(
        functools.partial(lay_kernel, hops),
        out_shape=(out, out),
        in_specs=[WHOLE] * (len(mine) + len(other)),
        out_specs=(WHOLE, WHOLE),
        compiler_params=pltpu.CompilerParams(vmem_limit_bytes=12 << 20),
        name="lay",
    )(*mine, *other)


def turn(x, axis, by):
    count = lax.axis_size(axis)
    return lax.ppermute(x, axis, [(i, (i + by) % count) for i in range(count)])


def swap(x):
    return turn(x, "ret", 1)


def cross(x, by):
    count = lax.axis_size("tp")
    return lax.ppermute(
        x,
        ("ret", "tp"),
        [(r * count + i, (1 - r) * count + (i + by) % count) for r in range(2) for i in range(count)],
    )


def near(keep, give):
    return turn(keep, "tp", 1), cross(give, -1), turn(keep, "tp", -1), cross(give, 1), cross(give, 0)


def far(keep_right, got_left):
    return turn(keep_right, "tp", 1), turn(got_left, "tp", -1)


def exchange(x, axis):
    return lax.all_to_all(x, axis, split_axis=0, concat_axis=0, tiled=True)


def added(x):
    return jnp.sum(x.astype(F32), axis=0).astype(BF16)


def body(queries, d_attn, pool, w_key, w_value, owners, picks, live_counts):
    y_count = lax.axis_size("y")
    z_high = lax.axis_size("zh")
    z_low = lax.axis_size("zl")
    ctx_count = y_count * z_high * z_low
    width = pool.shape[2]
    part = NBR_LEN // lax.axis_size("tp") // CHUNKS
    low = lax.axis_index("ret") == 0
    owner_col = jnp.where(low, owners[:, 0], owners[:, 1])
    pick_col = jnp.where(low, picks[:, 0], picks[:, 1])
    asked = jnp.sum(
        jnp.where(owner_col == ctx_index(), pick_col, 0).reshape(ctx_count, CH_DEV), axis=1
    )
    pool_blocks = pool[0].reshape(-1, NBR_LEN, width)

    first = pack(0, asked, live_counts, pool_blocks, part)
    second = pack(1, asked, live_counts, pool_blocks, part)
    incoming = exchange(first, CTX)
    held = hold(queries, d_attn, w_key, w_value)
    second, incoming, held = lax.optimization_barrier((second, incoming, held))
    late = exchange(second, CTX)
    keep, give = pick(owner_col, incoming)
    sides = near(keep, give)
    late, *shards = lax.optimization_barrier((late, keep, *sides, *far(*sides[:2])))
    first_rows = project(shards, *held[2:], "project_first")
    keep, give = pick(owner_col, late)
    keep_right, got_left, *sides = near(keep, give)
    ends = far(keep_right, got_left)
    near_rows = project((keep, keep_right, got_left, *sides), *held[2:], "project_near")
    tokens, other, rows, grads = attend(ends, *held, *first_rows, *near_rows)
    pair = (own_sum(first_rows[0], rows, grads) + swap(other).astype(F32)).astype(BF16)
    half = width // z_low
    by_y = added(exchange(pair.reshape(y_count * z_low, half, HEAD_DIM), ("y", "zl")))
    attn_out, d_queries = join(tokens, swap(tokens))
    terms = exchange(jnp.broadcast_to(by_y[None], (z_high,) + by_y.shape), "zh")
    terms, attn_out, d_queries = lax.optimization_barrier((terms, attn_out, d_queries))
    by_z = added(terms)
    hops = (0, 1, y_count - 1) + tuple(range(2, y_count - 1))
    near_z = [turn(by_z, "y", hop) if hop else by_z for hop in hops]
    pieces = near_z + [turn(x, "zl", 1) for x in near_z]
    d_w_key, d_w_value = lay(hops, pieces, [swap(x) for x in pieces])
    return (attn_out, d_queries, d_w_key, d_w_value)


def solution(mesh):
    z_high = mesh.shape["ctx"] // (Y_CHIPS * Z_PAIR)
    shape = (Y_CHIPS, z_high, Z_PAIR, mesh.shape["ret"], mesh.shape["tp"])
    fine = Mesh(mesh.devices.reshape(shape), CTX + ("ret", "tp"))
    ctx = CTX
    return jax.shard_map(
        body,
        mesh=fine,
        in_specs=(
            P(ctx, "tp"),
            P(ctx, "tp"),
            P("ret", ctx, None),
            P(None, "tp"),
            P(None, "tp"),
            P(),
            P(),
            P(),
        ),
        out_specs=(P(ctx, "tp"), P(ctx, "tp"), P(None, "tp"), P(None, "tp")),
        check_vma=False,
    )
```

```python
import functools
import math

import jax
import jax.numpy as jnp
from jax import lax
from jax.experimental import pallas as pl
from jax.experimental.pallas import tpu as pltpu
from jax.sharding import Mesh
from jax.sharding import PartitionSpec as P

HEAD_DIM = 128
SPAN = 64
NBR_LEN = 128
CH_DEV = 16
Y_CHIPS = 4
Z_PAIR = 2
CTX = ("y", "zh", "zl")


CHUNKS = 2
TOGETHER = 2

BF16 = jnp.bfloat16
F32 = jnp.float32
ANY = pl.BlockSpec(memory_space=pl.ANY)
SMEM = pl.BlockSpec(memory_space=pltpu.SMEM)
WHOLE = pl.BlockSpec(memory_space=pltpu.VMEM)


def ctx_index():
    z = lax.axis_index("zh") * lax.axis_size("zl") + lax.axis_index("zl")
    return lax.axis_index("y") * (lax.axis_size("zh") * lax.axis_size("zl")) + z


def pack_kernel(row, asked, live_counts, pool, out, held, in_sem, out_sem):
    part = held.shape[1]
    chunk = lax.axis_index("tp") * CHUNKS + row
    start = pl.multiple_of(chunk * part, part)
    load = pltpu.make_async_copy(pool.at[:, pl.ds(start, part), :], held, in_sem)
    load.start()
    live = live_counts[lax.axis_index("ret"), ctx_index()]
    slots = [lax.rem(asked[d], live) for d in range(out.shape[0])]
    copies = [
        pltpu.make_async_copy(held.at[slots[d]], out.at[d], out_sem.at[d])
        for d in range(out.shape[0])
    ]
    load.wait()
    for copy in copies:
        copy.start()
    for copy in copies:
        copy.wait()


def pack(row, asked, live_counts, pool_blocks, part):
    blocks, _, width = pool_blocks.shape
    count = asked.shape[0]
    return pl.pallas_call(
        functools.partial(pack_kernel, row),
        out_shape=jax.ShapeDtypeStruct((count, part, width), BF16),
        in_specs=[SMEM, SMEM, ANY],
        out_specs=ANY,
        scratch_shapes=[
            pltpu.VMEM((blocks, part, width), BF16),
            pltpu.SemaphoreType.DMA,
            pltpu.SemaphoreType.DMA((count,)),
        ],
        compiler_params=pltpu.CompilerParams(vmem_limit_bytes=60 << 20),
        name=f"pack{row}",
    )(asked, live_counts, pool_blocks)


def pick_kernel(owner_col, incoming, keep, give):
    half = keep.shape[0]
    me = lax.axis_index("ret")
    first = ctx_index() * (2 * half)
    for k in range(half):
        keep[k] = incoming[owner_col[first + me * half + k]]
        give[k] = incoming[owner_col[first + (1 - me) * half + k]]


def pick(owner_col, incoming):
    half = jax.ShapeDtypeStruct((CH_DEV // 2,) + incoming.shape[1:], BF16)
    return pl.pallas_call(
        pick_kernel,
        out_shape=(half, half),
        in_specs=[SMEM, WHOLE],
        out_specs=(WHOLE, WHOLE),
        compiler_params=pltpu.CompilerParams(vmem_limit_bytes=8 << 20),
        name="pick",
    )(owner_col, incoming)


def dot(a, b, dims=((1,), (0,))):
    return lax.dot_general(a, b, (dims, ((), ())), preferred_element_type=F32)


ROWS = ((1,), (1,))
DOWN = ((0,), (0,))


def two_heads(x):
    col = lax.broadcasted_iota(jnp.int32, x.shape, 1)
    zero = jnp.zeros_like(x)
    return jnp.concatenate(
        [jnp.where(col < HEAD_DIM, x, zero), jnp.where(col < HEAD_DIM, zero, x)], axis=0
    )


def own_heads(x):
    return jnp.concatenate([x[:SPAN, :HEAD_DIM], x[SPAN:, HEAD_DIM:]], axis=1)


def gather_rows(shards, rows, j):
    part = shards[0].shape[1]
    for p, shard in enumerate(shards):
        rows[j, p * part : (p + 1) * part, :] = shard[j]


def hold_kernel(queries, d_attn, w_key, w_value, q_out, g_out, k_out, v_out, sem):
    tokens = q_out.shape[0]
    place = pl.ds(pl.multiple_of(lax.axis_index("ret") * tokens, tokens), tokens)
    loads = [
        pltpu.make_async_copy(queries.at[place, :], q_out, sem.at[0]),
        pltpu.make_async_copy(d_attn.at[place, :], g_out, sem.at[1]),
        pltpu.make_async_copy(w_key, k_out, sem.at[2]),
        pltpu.make_async_copy(w_value, v_out, sem.at[3]),
    ]
    for load in loads:
        load.start()
    for load in loads:
        load.wait()


def hold(queries, d_attn, w_key, w_value):
    half = jax.ShapeDtypeStruct((queries.shape[0] // 2, queries.shape[1]), BF16)
    weight = jax.ShapeDtypeStruct(w_key.shape, BF16)
    return pl.pallas_call(
        hold_kernel,
        out_shape=(half, half, weight, weight),
        in_specs=[ANY] * 4,
        out_specs=(WHOLE,) * 4,
        scratch_shapes=[pltpu.SemaphoreType.DMA((4,))],
        compiler_params=pltpu.CompilerParams(vmem_limit_bytes=60 << 20),
        cost_estimate=pl.CostEstimate(flops=0, bytes_accessed=6 << 20, transcendentals=0),
        name="hold",
    )(queries, d_attn, w_key, w_value)


def project_kernel(count, *refs):
    shards = refs[:count]
    w_key, w_value, rows, pairs = refs[count:]
    spans, held, head_cols = pairs.shape
    head_cols //= 2
    for j in range(spans):
        gather_rows(shards, rows, j)
    flat = rows[...].reshape(spans * held, rows.shape[2])
    for side, weight in enumerate((w_key, w_value)):
        made = dot(flat, weight[...]).astype(BF16).reshape(spans, held, head_cols)
        pairs[:, :, side * head_cols : (side + 1) * head_cols] = made


def project(shards, w_key, w_value, name):
    spans, part, width = shards[0].shape
    head_cols = w_key.shape[1]
    count = len(shards) * part
    return pl.pallas_call(
        functools.partial(project_kernel, len(shards)),
        out_shape=(
            jax.ShapeDtypeStruct((spans, count, width), BF16),
            jax.ShapeDtypeStruct((spans, count, 2 * head_cols), BF16),
        ),
        in_specs=[WHOLE] * (len(shards) + 2),
        out_specs=(WHOLE,) * 2,
        compiler_params=pltpu.CompilerParams(vmem_limit_bytes=12 << 20),
        cost_estimate=pl.CostEstimate(
            flops=4 * spans * count * width * head_cols, bytes_accessed=4 << 20, transcendentals=0
        ),
        name=name,
    )(*shards, w_key, w_value)


def weight_sum(rows_a, rows_b, grads, side):
    head_cols = grads.shape[2] // 2
    cut = pl.ds(pl.multiple_of(side * head_cols, head_cols), head_cols)
    width = rows_a.shape[2]
    flat = jnp.concatenate([rows_a[...].reshape(-1, width), rows_b[...].reshape(-1, width)], axis=0)
    return dot(flat, grads[:, :, cut].reshape(-1, head_cols), DOWN)


def attend_kernel(count, *refs):
    shards = refs[:count]
    queries, d_attn, w_key, w_value, rows_a, pairs_a, rows_m, pairs_m = refs[count : count + 8]
    tokens_out, other, rows_b, grads, far_rows = refs[count + 8 :]
    spans, near_rows, width = rows_a.shape
    far_count = far_rows.shape[1]
    head_cols = w_key.shape[1]
    heads = head_cols // HEAD_DIM
    scale = 1.0 / math.sqrt(HEAD_DIM)
    raise_by = scale / math.log(2.0)
    for j in range(spans):
        gather_rows(shards, far_rows, j)
        rows_b[j, : near_rows - far_count, :] = rows_m[j]
        rows_b[j, near_rows - far_count :, :] = far_rows[j]
    far_flat = far_rows[...].reshape(spans * far_count, width)
    far_keys = dot(far_flat, w_key[...]).astype(BF16)
    far_values = dot(far_flat, w_value[...]).astype(BF16)
    for start in range(0, spans, TOGETHER):
        units = []
        for j in range(start, start + TOGETHER):
            units += [
                (
                    j,
                    slice(h * HEAD_DIM, (h + 2) * HEAD_DIM),
                    slice(head_cols + h * HEAD_DIM, head_cols + (h + 2) * HEAD_DIM),
                    slice(j * SPAN, (j + 1) * SPAN),
                    slice(j * near_rows, (j + 1) * near_rows),
                )
                for h in range(0, heads, 2)
            ]

        def made(far, j, cut, side_cut):
            late = far[j * far_count : (j + 1) * far_count, cut]
            return jnp.concatenate([pairs_a[j, :, side_cut], pairs_m[j, :, side_cut], late], axis=0)

        keys = [made(far_keys, j, cut, cut) for j, cut, _, _, _ in units]
        values = [made(far_values, j, cut, past) for j, cut, past, _, _ in units]
        qs = [two_heads(queries[at, cut]) for _, cut, _, at, _ in units]
        gs = [two_heads(d_attn[at, cut]) for _, cut, _, at, _ in units]
        scores = [dot(k, q, ROWS) for k, q in zip(keys, qs)]
        grad_probs = [dot(v, g, ROWS) for v, g in zip(values, gs)]
        tops = [jnp.max(x, axis=0, keepdims=True) for x in scores]
        raised = [jnp.exp2((x - top) * raise_by) for x, top in zip(scores, tops)]
        probs = [x * (1.0 / jnp.sum(x, axis=0, keepdims=True)) for x in raised]
        probs_b = [x.astype(BF16) for x in probs]
        out_dots = [jnp.sum(p * g, axis=0, keepdims=True) for p, g in zip(probs, grad_probs)]
        dscores = [
            (p * ((g - o) * scale)).astype(BF16) for p, g, o in zip(probs, grad_probs, out_dots)
        ]
        for i, (_, cut, past, at, to) in enumerate(units):
            k_grad = dot(dscores[i], qs[i]).astype(BF16)
            v_grad = dot(probs_b[i], gs[i]).astype(BF16)
            for side in range(2):
                part = slice(side * near_rows, (side + 1) * near_rows)
                grads[side, to, cut] = k_grad[part]
                grads[side, to, past] = v_grad[part]
            tokens_out[0, at, cut] = own_heads(dot(probs_b[i], values[i], DOWN)).astype(BF16)
            tokens_out[1, at, cut] = own_heads(dot(dscores[i], keys[i], DOWN)).astype(BF16)
    sums = weight_sum(rows_a, rows_b, grads, 1 - lax.axis_index("ret"))
    for h in range(heads):
        other[h] = sums[:, h * HEAD_DIM : (h + 1) * HEAD_DIM].astype(other.dtype)


def attend(shards, queries, d_attn, w_key, w_value, rows_a, pairs_a, rows_m, pairs_m):
    spans, near_rows, width = rows_a.shape
    nbr_rows = 2 * NBR_LEN
    head_cols = w_key.shape[1]
    heads = head_cols // HEAD_DIM
    tokens = spans * SPAN
    flops = 2 * spans * nbr_rows * head_cols * (2 * width + 12 * SPAN)
    return pl.pallas_call(
        functools.partial(attend_kernel, len(shards)),
        out_shape=(
            jax.ShapeDtypeStruct((2, tokens, head_cols), BF16),
            jax.ShapeDtypeStruct((heads, width, HEAD_DIM), BF16),
            jax.ShapeDtypeStruct((spans, near_rows, width), BF16),
            jax.ShapeDtypeStruct((2, spans * near_rows, 2 * head_cols), BF16),
        ),
        in_specs=[WHOLE] * (len(shards) + 8),
        out_specs=(WHOLE,) * 4,
        scratch_shapes=[pltpu.VMEM((spans, near_rows - rows_m.shape[1], width), BF16)],
        compiler_params=pltpu.CompilerParams(vmem_limit_bytes=16 << 20),
        cost_estimate=pl.CostEstimate(
            flops=flops, bytes_accessed=10 << 20, transcendentals=spans * SPAN * nbr_rows * heads
        ),
        name="attend",
    )(*shards, queries, d_attn, w_key, w_value, rows_a, pairs_a, rows_m, pairs_m)


def own_sum_kernel(rows_a, rows_b, grads, mine):
    sums = weight_sum(rows_a, rows_b, grads, lax.axis_index("ret"))
    for h in range(mine.shape[0]):
        mine[h] = sums[:, h * HEAD_DIM : (h + 1) * HEAD_DIM]


def own_sum(rows_a, rows_b, grads):
    width = rows_a.shape[2]
    heads = grads.shape[2] // 2 // HEAD_DIM
    return pl.pallas_call(
        own_sum_kernel,
        out_shape=jax.ShapeDtypeStruct((heads, width, HEAD_DIM), F32),
        in_specs=[WHOLE] * 3,
        out_specs=WHOLE,
        compiler_params=pltpu.CompilerParams(vmem_limit_bytes=16 << 20),
        cost_estimate=pl.CostEstimate(
            flops=4 * grads.shape[1] * width * heads * HEAD_DIM,
            bytes_accessed=4 << 20,
            transcendentals=0,
        ),
        name="own_sum",
    )(rows_a, rows_b, grads)


def join_kernel(mine, other, attn_out, d_queries, sem):
    me = lax.axis_index("ret")
    tokens = mine.shape[1]
    copies = []
    for side, held in ((me, mine), (1 - me, other)):
        place = pl.ds(pl.multiple_of(side * tokens, tokens), tokens)
        for which, out in enumerate((attn_out, d_queries)):
            copies.append(
                pltpu.make_async_copy(held.at[which], out.at[place, :], sem.at[len(copies)])
            )
    for copy in copies:
        copy.start()
    for copy in copies:
        copy.wait()


def join(mine, other):
    out = jax.ShapeDtypeStruct((2 * mine.shape[1], mine.shape[2]), BF16)
    return pl.pallas_call(
        join_kernel,
        out_shape=(out, out),
        in_specs=[ANY] * 2,
        out_specs=(ANY, ANY),
        scratch_shapes=[pltpu.SemaphoreType.DMA((4,))],
        compiler_params=pltpu.CompilerParams(vmem_limit_bytes=4 << 20),
        name="join",
    )(mine, other)


def lay_kernel(hops, *refs):
    d_w_key, d_w_value = refs[-2:]
    total = 2 * len(hops)
    half = refs[0].shape[0]
    low = lax.axis_index("ret") == 0
    count = lax.axis_size("y")
    for i in range(total):
        mine, other = refs[i], refs[total + i]
        h = lax.rem(lax.axis_index("y") + (count - hops[i % len(hops)]), count)
        side = lax.rem(lax.axis_index("zl") + i // len(hops), 2)
        place = (
            pl.ds(pl.multiple_of(side * half, half), half),
            pl.ds(pl.multiple_of(h * HEAD_DIM, HEAD_DIM), HEAD_DIM),
        )
        d_w_key[place] = jnp.where(low, mine[...], other[...])
        d_w_value[place] = jnp.where(low, other[...], mine[...])


def lay(hops, mine, other):
    half, cols = mine[0].shape
    out = jax.ShapeDtypeStruct((2 * half, len(hops) * cols), BF16)
    return pl.pallas_call(
        functools.partial(lay_kernel, hops),
        out_shape=(out, out),
        in_specs=[WHOLE] * (len(mine) + len(other)),
        out_specs=(WHOLE, WHOLE),
        compiler_params=pltpu.CompilerParams(vmem_limit_bytes=12 << 20),
        name="lay",
    )(*mine, *other)


def turn(x, axis, by):
    count = lax.axis_size(axis)
    return lax.ppermute(x, axis, [(i, (i + by) % count) for i in range(count)])


def swap(x):
    return turn(x, "ret", 1)


def cross(x, by):
    count = lax.axis_size("tp")
    return lax.ppermute(
        x,
        ("ret", "tp"),
        [(r * count + i, (1 - r) * count + (i + by) % count) for r in range(2) for i in range(count)],
    )


def near(keep, give):
    return turn(keep, "tp", 1), cross(give, -1), turn(keep, "tp", -1), cross(give, 1), cross(give, 0)


def far(keep_right, got_left):
    return turn(keep_right, "tp", 1), turn(got_left, "tp", -1)


def exchange(x, axis):
    return lax.all_to_all(x, axis, split_axis=0, concat_axis=0, tiled=True)


def added(x):
    return jnp.sum(x.astype(F32), axis=0).astype(BF16)


def body(queries, d_attn, pool, w_key, w_value, owners, picks, live_counts):
    y_count = lax.axis_size("y")
    z_high = lax.axis_size("zh")
    z_low = lax.axis_size("zl")
    ctx_count = y_count * z_high * z_low
    width = pool.shape[2]
    part = NBR_LEN // lax.axis_size("tp") // CHUNKS
    low = lax.axis_index("ret") == 0
    owner_col = jnp.where(low, owners[:, 0], owners[:, 1])
    pick_col = jnp.where(low, picks[:, 0], picks[:, 1])
    asked = jnp.sum(
        jnp.where(owner_col == ctx_index(), pick_col, 0).reshape(ctx_count, CH_DEV), axis=1
    )
    pool_blocks = pool[0].reshape(-1, NBR_LEN, width)

    first = pack(0, asked, live_counts, pool_blocks, part)
    second = pack(1, asked, live_counts, pool_blocks, part)
    incoming = exchange(first, CTX)
    held = hold(queries, d_attn, w_key, w_value)
    second, incoming, held = lax.optimization_barrier((second, incoming, held))
    late = exchange(second, CTX)
    keep, give = pick(owner_col, incoming)
    sides = near(keep, give)
    late, *shards = lax.optimization_barrier((late, keep, *sides, *far(*sides[:2])))
    first_rows = project(shards, *held[2:], "project_first")
    keep, give = pick(owner_col, late)
    keep_right, got_left, *sides = near(keep, give)
    ends = far(keep_right, got_left)
    near_rows = project((keep, keep_right, got_left, *sides), *held[2:], "project_near")
    tokens, other, rows, grads = attend(ends, *held, *first_rows, *near_rows)
    pair = (own_sum(first_rows[0], rows, grads) + swap(other).astype(F32)).astype(BF16)
    half = width // z_low
    by_y = added(exchange(pair.reshape(y_count * z_low, half, HEAD_DIM), ("y", "zl")))
    attn_out, d_queries = join(tokens, swap(tokens))
    terms = exchange(jnp.broadcast_to(by_y[None], (z_high,) + by_y.shape), "zh")
    terms, attn_out, d_queries = lax.optimization_barrier((terms, attn_out, d_queries))
    by_z = (jnp.sum(terms.astype(F32), axis=0) * (1.0 / (CH_DEV * ctx_count))).astype(BF16)
    hops = (0, 1, y_count - 1) + tuple(range(2, y_count - 1))
    near_z = [turn(by_z, "y", hop) if hop else by_z for hop in hops]
    pieces = near_z + [turn(x, "zl", 1) for x in near_z]
    d_w_key, d_w_value = lay(hops, pieces, [swap(x) for x in pieces])
    return (attn_out, d_queries, d_w_key, d_w_value)


def solution(mesh):
    z_high = mesh.shape["ctx"] // (Y_CHIPS * Z_PAIR)
    shape = (Y_CHIPS, z_high, Z_PAIR, mesh.shape["ret"], mesh.shape["tp"])
    fine = Mesh(mesh.devices.reshape(shape), CTX + ("ret", "tp"))
    ctx = CTX
    return jax.shard_map(
        body,
        mesh=fine,
        in_specs=(
            P(ctx, "tp"),
            P(ctx, "tp"),
            P("ret", ctx, None),
            P(None, "tp"),
            P(None, "tp"),
            P(),
            P(),
            P(),
        ),
        out_specs=(P(ctx, "tp"), P(ctx, "tp"), P(None, "tp"), P(None, "tp")),
        check_vma=False,
    )
```
